32 devices in a mesh: dp: 8 (over z, y), mp: 4 (over x, core).
Axes of the slice: x: 2, y: 2, z: 4, core: 2. Of those that a mesh axis runs over, the one named last changes fastest.
Arguments:
- hidden_in: bfloat16 [16384, 1024], P('dp', 'mp'), may hold values from -6 to 6
- cotangent: bfloat16 [16384, 1024], P('dp', 'mp'), may hold values from -6 to 6
- owners: int32 [128], replicated, may hold values from 0 to 7, as said below
- masters: float32 [4, 256, 32, 1024], P('mp', 'dp'), may hold values from -0.1875 to 0.1875
- firsts: float32 [4, 256, 32, 1024], P('mp', 'dp'), may hold values from -6 to 6
- seconds: float32 [4, 256, 32, 1024], P('mp', 'dp'), may hold values from 19.33312 to 77.66016
- width_gains: float32 [3, 1024], P(None, 'mp'), may hold values from 0.1 to 1.6, as said below
- width_first: float32 [3, 1024], P(None, 'mp'), may hold values from -32 to 32
- width_second: float32 [3, 1024], P(None, 'mp'), may hold values from 137.6256 to 552.1408
- hidden_gains: float32 [2, 4096], P(None, 'mp'), may hold values from 0.25 to 1.75
- hidden_first: float32 [2, 4096], P(None, 'mp'), may hold values from -6 to 6
- hidden_second: float32 [2, 4096], P(None, 'mp'), may hold values from 19.33312 to 77.66016
Outputs:
- hidden_out: float32 [16384, 1024], P('dp', 'mp')
- grad_in: float32 [16384, 1024], P('dp', 'mp')
- masters_new: float32 [4, 256, 32, 1024], P('mp', 'dp')
- firsts_new: float32 [4, 256, 32, 1024], P('mp', 'dp')
- seconds_new: float32 [4, 256, 32, 1024], P('mp', 'dp')
- weight_grads: float32 [4, 256, 32, 1024], P('mp', 'dp')
- width_gains_new: float32 [3, 1024], P(None, 'mp')
- width_grads: float32 [3, 1024], P(None, 'mp')
- width_first_new: float32 [3, 1024], P(None, 'mp')
- width_second_new: float32 [3, 1024], P(None, 'mp')
- hidden_gains_new: float32 [2, 4096], P(None, 'mp')
- hidden_grads: float32 [2, 4096], P(None, 'mp')
- hidden_first_new: float32 [2, 4096], P(None, 'mp')
- hidden_second_new: float32 [2, 4096], P(None, 'mp')
The draws below stay inside these ranges and needn't reach their ends.
Inputs may be any that keep to these rules, and one draw needn't show every extreme that they name: owners[b] is the index of dp that owns row block b; no index owns more than 32 blocks, and some index owns exactly 32. `width_gains`: row 0 lies in 0.8 to 1.6, rows 1 and 2 in 0.1 to 0.8.
All inputs are finite; a program needn't handle non-finite values.
Results may differ from the reference program's by a relative error of at most 0.015.
The reference program's roundings to bfloat16 on the way count: a program that leaves them out, or rounds other values in their place, can miss the bound.
Values may be sent and summed in bfloat16 or wider, within the bound.
A program may use at most 256 MiB of HBM per device.

```python
import math
import jax
import jax.numpy as jnp
from jax import lax

D = 1024
FF = 4096
HEADS = 16
HD = 64
TOK_DP = 2048
BR = 32
STEP = 7
TOKENS = 16384
NBLK = 128
SLOTS = 32
N_DP = 8
N_MP = 4


def draw_owners(key, part):
    order_key, share_key, mix_key = jax.random.split(key, 3)
    half_count = N_DP // 2
    owner_order = jax.random.permutation(order_key, N_DP)
    owner_share = jax.random.randint(share_key, (half_count,), 0, SLOTS + 1).astype(jnp.int32)
    owner_share = owner_share.at[0].set(SLOTS)
    owner_counts = jnp.zeros((N_DP,), jnp.int32).at[owner_order[:half_count]].set(owner_share)
    owner_counts = owner_counts.at[owner_order[half_count:]].set(SLOTS - owner_share)
    count_ends = jnp.cumsum(owner_counts)
    position = jnp.arange(NBLK).astype(jnp.int32)
    sorted_owner = jnp.sum((count_ends[None, :] <= position[:, None]).astype(jnp.int32), axis=1).astype(jnp.int32)
    mixing = jax.random.permutation(mix_key, NBLK)
    return sorted_owner[mixing]


def draw_width_gains(key, part):
    scale_key, rate_key = jax.random.split(key)
    scale_row = jax.random.uniform(scale_key, (1, D), jnp.float32, 0.8, 1.6)
    rate_rows = jnp.exp(jax.random.uniform(rate_key, (2, D), jnp.float32, math.log(0.1), math.log(0.8)))
    return jnp.concatenate([scale_row, rate_rows], axis=0)


def level_of(key, dims, cuts, smallest, high):
    loudness = 1.0
    for dim, shards_of in cuts:
        heights = jax.random.uniform(jax.random.fold_in(jax.random.fold_in(key, 6), dim), (shards_of,), jnp.float32, smallest / len(cuts), high / len(cuts))
        loudness = loudness * jnp.repeat(jnp.exp(heights), dims[dim] // shards_of).reshape((-1,) + (1,) * (len(dims) - 1 - dim))
    return loudness


def noise(stream_key, shape, deviation, most, cuts=(), held_as=jnp.bfloat16):
    values = jax.random.normal(stream_key, shape, jnp.float32) * deviation
    if len(cuts) > 0:
        values = level_of(stream_key, shape, cuts, -0.22, 0.18) * values
    return jnp.clip(values, min=-most, max=most).astype(held_as)


def setup_inputs(seed: int = 0) -> dict:
    key_of = jax.random.split(jax.random.key(seed), 13)
    hidden_in = noise(key_of[0], (TOKENS, D), 1.0, 6.0, ((0, 8), (1, 4)))
    cotangent = noise(key_of[1], (TOKENS, D), 1.0, 6.0, ((0, 8), (1, 4)))
    owners = draw_owners(jax.random.fold_in(key_of[12], 71), 0)
    masters = noise(key_of[3], (N_MP, N_DP * SLOTS, BR, D), D ** -0.5, 0.1875, ((0, 4), (1, 8)), jnp.float32)
    firsts = noise(key_of[4], (N_MP, N_DP * SLOTS, BR, D), (0.0167 * TOKENS ** 0.5), 6.0, ((0, 4), (1, 8)), jnp.float32)
    seconds = jnp.clip(19.33312 + 58.3270359 * jax.random.uniform(key_of[5], (N_MP, N_DP * SLOTS, BR, D), jnp.float32) ** level_of(key_of[5], (N_MP, N_DP * SLOTS, BR, D), ((0, 4), (1, 8)), -0.2, 0.2), 19.33312, 77.66016)
    width_gains = draw_width_gains(jax.random.fold_in(key_of[12], 71), 0)
    width_first = noise(key_of[7], (3, D), (0.044 * TOKENS ** 0.5), 32.0, ((1, 4),), jnp.float32)
    width_second = jnp.clip(137.6256 + 414.5152 * jax.random.uniform(key_of[8], (3, D), jnp.float32) ** level_of(key_of[8], (3, D), ((1, 4),), -0.2, 0.2), 137.6256, 552.1408)
    hidden_gains = jnp.clip(1.0 + 0.15 * jax.random.normal(key_of[9], (2, FF), jnp.float32), 0.25, 1.75)
    hidden_first = noise(key_of[10], (2, FF), (0.0167 * TOKENS ** 0.5), 6.0, ((1, 4),), jnp.float32)
    hidden_second = jnp.clip(19.33312 + 58.3270359 * jax.random.uniform(key_of[11], (2, FF), jnp.float32) ** level_of(key_of[11], (2, FF), ((1, 4),), -0.2, 0.2), 19.33312, 77.66016)
    return dict(hidden_in=hidden_in, cotangent=cotangent, owners=owners, masters=masters, firsts=firsts, seconds=seconds, width_gains=width_gains, width_first=width_first, width_second=width_second, hidden_gains=hidden_gains, hidden_first=hidden_first, hidden_second=hidden_second)


EPSILON = 1e-06
ADAM_EPSILON = 1e-08
BETA_FIRST = 0.9
BETA_SECOND = 0.95
LEARN_RATE = 0.05
GAIN_RATE = 0.6
WEIGHT_DECAY = 0.1
MASKED_SCORE = -1e+30
HIGHEST = lax.Precision.HIGHEST

@jax.custom_vjp
def low(v):
    return lax.optimization_barrier(v.astype(jnp.bfloat16)).astype(jnp.float32)

@jax.custom_vjp
def low_back(v):
    return v

def low_keep(v):
    return (low(v), None)

def low_pass(kept, grad):
    return (grad,)

def back_keep(v):
    return (v, None)

def back_low(kept, grad):
    return (low(grad),)
low.defvjp(low_keep, low_pass)
low_back.defvjp(back_keep, back_low)

def rows_times(left_rows, weight):
    return jnp.dot(left_rows, weight.T, precision=HIGHEST)

def matmul(left_rows, right_rows):
    return jnp.dot(left_rows, right_rows, precision=HIGHEST)

def rownorm(vector):
    return vector * lax.rsqrt(lax.optimization_barrier(jnp.mean(vector * vector, axis=-1, keepdims=True)) + EPSILON)

def head_unit(vector):
    return vector * lax.rsqrt(lax.optimization_barrier(jnp.sum(vector * vector, axis=-1, keepdims=True)) + EPSILON)

def rope_tables(length, head_size):
    half_size = head_size // 2
    position = jnp.arange(length).astype(jnp.float32)
    frequency = jnp.exp(jnp.arange(half_size).astype(jnp.float32) * (-2.0 * math.log(10000.0) / head_size))
    angles = position[:, None] * frequency[None, :]
    return (jnp.cos(angles)[:, None, :], jnp.sin(angles)[:, None, :])

def rotate(vector, cosine_table, sine_table):
    half_size = vector.shape[-1] // 2
    first_half = vector[..., :half_size]
    second_half = vector[..., half_size:]
    return jnp.concatenate([first_half * cosine_table - second_half * sine_table, first_half * sine_table + second_half * cosine_table], axis=-1)

def layer_forward(stream, weights, width_gains, hidden_gains):
    w_query, w_key, w_value, w_out, w_up, w_gate, w_down = [low(matrix) for matrix in weights]
    length = stream.shape[0]
    score_scale = float(HD) ** 0.5
    start_unit = rownorm(stream)
    operand = low(start_unit)
    query_raw = low_back(rows_times(operand, w_query)).reshape(length, HEADS, HD)
    key_raw = low_back(rows_times(operand, w_key)).reshape(length, HEADS, HD)
    value_heads = low(low_back(rows_times(operand, w_value))).reshape(length, HEADS, HD)
    cosine_table, sine_table = rope_tables(length, HD)
    qk_heads = width_gains[0].reshape(HEADS, HD)
    queries = low(qk_heads * head_unit(rotate(query_raw, cosine_table, sine_table)))
    key_rows = low(qk_heads * head_unit(rotate(key_raw, cosine_table, sine_table)))
    block_size = min(512, length)
    block_count = length // block_size
    columns = jnp.arange(length).astype(jnp.int32)

    def attend(inputs):
        query_part, first_row = inputs
        raw_scores = low_back(jnp.einsum('qhd,khd->hqk', query_part, key_rows, precision=HIGHEST) * score_scale)
        allowed = (first_row + jnp.arange(block_size).astype(jnp.int32))[:, None] >= columns[None, :]
        prob_rows = low(jax.nn.softmax(jnp.where(allowed[None], raw_scores, MASKED_SCORE), axis=-1))
        return jnp.einsum('hqk,khd->qhd', prob_rows, value_heads, precision=HIGHEST)
    starts = (jnp.arange(block_count) * block_size).astype(jnp.int32)
    mixed_all = lax.map(jax.checkpoint(attend), (queries.reshape(block_count, block_size, HEADS, HD), starts))
    attended = low_back(low(mixed_all.reshape(length, D)))
    attn_branch = low_back(matmul(attended, w_out))
    middle = rownorm(start_unit + width_gains[1] * (rownorm(attn_branch) - start_unit))
    middle_rows = low(middle)
    up_raw = low_back(rows_times(middle_rows, w_up))
    gate_raw = low_back(rows_times(middle_rows, w_gate))
    up_val = hidden_gains[0] * up_raw
    gate_val = hidden_gains[1] * gate_raw
    product = low(up_val * jax.nn.silu(gate_val))
    mlp_branch = low_back(matmul(product, w_down))
    return rownorm(middle + width_gains[2] * (rownorm(mlp_branch) - middle))

def slot_ranks(owners):
    block_order = jnp.arange(owners.shape[0]).astype(jnp.int32)
    same_owner = owners[:, None] == owners[None, :]
    return lax.optimization_barrier(jnp.sum(jnp.logical_and(same_owner, block_order[None, :] < block_order[:, None]).astype(jnp.int32), axis=1)).astype(jnp.int32)

def to_matrices(stacked):
    narrow = D // N_MP
    hidden_local = FF // N_MP
    matrices = []
    offset = 0
    for rows_here in [narrow, narrow, narrow, narrow, hidden_local, hidden_local, hidden_local]:
        matrices.append(stacked[:, offset:offset + rows_here].reshape(N_MP * rows_here, D))
        offset = offset + rows_here
    return matrices

def to_stack(matrices):
    return jnp.concatenate([matrix.reshape(N_MP, matrix.shape[0] // N_MP, D) for matrix in matrices], axis=1)

def add_up(left_sum, right_sum):
    return left_sum + right_sum

def adam_update(params, gradient, first_moment, second_moment, decay_rate, step_rate):
    first_new = BETA_FIRST * first_moment + (1.0 - BETA_FIRST) * gradient
    second_new = BETA_SECOND * second_moment + (1.0 - BETA_SECOND) * gradient * gradient
    corrected = first_new / (1.0 - BETA_FIRST ** STEP) / (jnp.sqrt(second_new / (1.0 - BETA_SECOND ** STEP)) + ADAM_EPSILON)
    return (params - step_rate * (corrected + decay_rate * params), first_new, second_new)

def reference(hidden_in, cotangent, owners, masters, firsts, seconds, width_gains, width_first, width_second, hidden_gains, hidden_first, hidden_second):
    slot_rank = slot_ranks(owners)
    places = (owners * SLOTS + slot_rank).astype(jnp.int32)
    stacked = masters[:, places].reshape(N_MP, NBLK * BR, D)
    weights = tuple(to_matrices(stacked))
    streams = hidden_in.astype(jnp.float32).reshape(N_DP, TOK_DP, D)
    cotangents = cotangent.astype(jnp.float32).reshape(N_DP, TOK_DP, D)

    def sequence_step(totals, inputs):
        stream, seq_cot = inputs
        output, pull_back = jax.vjp(layer_forward, stream, weights, width_gains, hidden_gains)
        gradients = pull_back(seq_cot)
        totals = jax.tree.map(add_up, totals, (gradients[1], gradients[2], gradients[3]))
        return (totals, (output, gradients[0]))
    initial = jax.tree.map(jnp.zeros_like, (weights, width_gains, hidden_gains))
    totals, (outputs, input_grads) = lax.scan(sequence_step, initial, (streams, cotangents))
    weight_totals, width_totals, hidden_totals = totals
    grad_stack = to_stack(list(weight_totals)).reshape(N_MP, NBLK, BR, D)
    weight_grads = jnp.zeros_like(masters).at[:, places].set(grad_stack)
    slot_index = jnp.arange(N_DP * SLOTS).astype(jnp.int32)
    owner_counts = lax.optimization_barrier(jnp.sum((owners[None, :] == jnp.arange(N_DP).astype(jnp.int32)[:, None]).astype(jnp.int32), axis=1))
    in_use = (slot_index % SLOTS < owner_counts[slot_index // SLOTS])[None, :, None, None]
    stepped, firsts_new, seconds_new = adam_update(masters, weight_grads, firsts, seconds, WEIGHT_DECAY, LEARN_RATE)
    masters_new = stepped * lax.rsqrt(lax.optimization_barrier(jnp.sum(stepped * stepped, axis=-1, keepdims=True)) + EPSILON)
    masters_new = jnp.where(in_use, masters_new, 0.0)
    firsts_new = jnp.where(in_use, firsts_new, 0.0)
    seconds_new = jnp.where(in_use, seconds_new, 0.0)
    weight_grads = jnp.where(in_use, weight_grads, 0.0)
    width_new, width_first_new, width_second_new = adam_update(width_gains, width_totals, width_first, width_second, 0.0, GAIN_RATE)
    hidden_new, hidden_first_new, hidden_second_new = adam_update(hidden_gains, hidden_totals, hidden_first, hidden_second, 0.0, GAIN_RATE)
    return (outputs.reshape(TOKENS, D), input_grads.reshape(TOKENS, D), masters_new, firsts_new, seconds_new, weight_grads, width_new, width_totals, width_first_new, width_second_new, hidden_new, hidden_totals, hidden_first_new, hidden_second_new)
```

```python
import functools
import math

import jax
import jax.numpy as jnp
from jax import lax
from jax.experimental import pallas as pl
from jax.experimental.pallas import tpu as pltpu
from jax.sharding import PartitionSpec as P

D = 1024
HD = 64
STEP = 7
LANES = 128
STEPS = 4

EPSILON = 1e-06
ADAM_EPSILON = 1e-08
BETA_FIRST = 0.9
BETA_SECOND = 0.95
LEARN_RATE = 0.05
GAIN_RATE = 0.6
WEIGHT_DECAY = 0.1
SCORE_SCALE = float(HD) ** 0.5

f32 = jnp.float32
bf16 = jnp.bfloat16


def nn(left, right):
    return jnp.dot(left, right, preferred_element_type=f32)


def nt(left, right):
    return lax.dot_general(left, right, (((1,), (1,)), ((), ())), preferred_element_type=f32)


def tn(left, right):
    return lax.dot_general(left, right, (((0,), (0,)), ((), ())), preferred_element_type=f32)


def normalize(vector):
    inverse = lax.rsqrt(jnp.sum(vector * vector, axis=-1, keepdims=True) / D + EPSILON)
    return (vector * inverse, inverse)


def normalize_back(unit_rows, inverse, upstream):
    return inverse * (upstream - unit_rows * (jnp.sum(unit_rows * upstream, axis=-1, keepdims=True) / D))


def blend_branch(base_rows, branch, branch_rate):
    branch_unit, branch_inv = normalize(branch)
    mixed_unit, mixed_inv = normalize(base_rows + branch_rate * (branch_unit - base_rows))
    return (branch_unit, branch_inv, mixed_unit, mixed_inv)


def blend_back(base_rows, branch_unit, branch_inv, mixed_unit, mixed_inv, branch_rate, upstream):
    d_mixed = normalize_back(mixed_unit, mixed_inv, upstream)
    d_branch = normalize_back(branch_unit, branch_inv, branch_rate * d_mixed)
    return (
        (1.0 - branch_rate) * d_mixed,
        d_branch,
        jnp.sum(d_mixed * (branch_unit - base_rows), axis=0),
    )


def adam_update(params, gradient, first_moment, second_moment, decay_rate, step_rate):
    first_new = BETA_FIRST * first_moment + (1.0 - BETA_FIRST) * gradient
    second_new = BETA_SECOND * second_moment + (1.0 - BETA_SECOND) * gradient * gradient
    corrected = (
        first_new
        / (1.0 - BETA_FIRST**STEP)
        / (jnp.sqrt(second_new / (1.0 - BETA_SECOND**STEP)) + ADAM_EPSILON)
    )
    return (params - step_rate * (corrected + decay_rate * params), first_new, second_new)


def swap_halves(pair, lane):
    return jnp.where(
        lane % HD < HD // 2, pltpu.roll(pair, LANES - HD // 2, 1), pltpu.roll(pair, HD // 2, 1)
    )


def head_sums(values):
    width = values.shape[1]
    row = lax.broadcasted_iota(jnp.int32, (width, width), 0) // HD
    column = lax.broadcasted_iota(jnp.int32, (width, width), 1) // HD
    same = jnp.where(row == column, 1.0, 0.0).astype(bf16)
    high = values.astype(bf16)
    rest = values - high.astype(f32)
    middle = rest.astype(bf16)
    low = (rest - middle.astype(f32)).astype(bf16)
    return nn(high, same) + nn(middle, same) + nn(low, same)


def project_kernel(
    narrow, x_ref, w_ref, gain_ref, cos_ref, sin_ref, op_ref, q_ref, k_ref, v_ref, qr_ref, kr_ref
):
    rows = x_ref.shape[1]
    x = jnp.concatenate([x_ref[d] for d in range(x_ref.shape[0])], axis=1).astype(f32)
    operand = (x * lax.rsqrt(jnp.sum(x * x, axis=1, keepdims=True) / D + EPSILON)).astype(bf16)
    op_ref[...] = operand
    lane = lax.broadcasted_iota(jnp.int32, (rows, LANES), 1)
    cosine, sine = cos_ref[...], sin_ref[...]
    raw = nt(operand, w_ref[...])
    pairs = range(narrow // LANES)
    for which in range(2):
        out_ref, rot_ref = ((q_ref, qr_ref), (k_ref, kr_ref))[which]
        fill = (0.0, 1.0)[which]
        turned = []
        for pair in pairs:
            here = raw[:, which * narrow + pair * LANES : which * narrow + (pair + 1) * LANES]
            turned.append(here * cosine + swap_halves(here, lane) * sine)
        turned = jnp.concatenate(turned, axis=1)
        rot_ref[...] = turned
        gained = gain_ref[...] * (turned * lax.rsqrt(head_sums(turned * turned) + EPSILON))
        gained = gained.astype(bf16).astype(f32)
        if which == 0:
            gained = gained * SCORE_SCALE
        for pair in pairs:
            here = gained[:, pair * LANES : (pair + 1) * LANES]
            out_ref[2 * pair] = jnp.where(lane < HD, here, fill).astype(bf16)
            out_ref[2 * pair + 1] = jnp.where(lane < HD, pltpu.roll(here, HD, 1), fill).astype(bf16)
    for pair in range(narrow // LANES):
        here = raw[:, 2 * narrow + pair * LANES : 2 * narrow + (pair + 1) * LANES]
        v_ref[2 * pair] = jnp.where(lane < HD, here, 1.0).astype(bf16)
        v_ref[2 * pair + 1] = jnp.where(lane < HD, pltpu.roll(here, HD, 1), 1.0).astype(bf16)


def project(x_all, weights, gain, cosine, sine):
    size, tokens, narrow = x_all.shape
    heads = narrow // HD
    rows = min(512, tokens)
    head_spec = pl.BlockSpec((heads, rows, LANES), lambda i: (0, i, 0))
    row_spec = lambda width: pl.BlockSpec((rows, width), lambda i: (i, 0))
    whole = lambda a: pl.BlockSpec(a.shape, lambda i: (0, 0))
    return pl.pallas_call(
        functools.partial(project_kernel, narrow),
        grid=(tokens // rows,),
        in_specs=[pl.BlockSpec((size, rows, narrow), lambda i: (0, i, 0)), pl.BlockSpec((3 * narrow, D), lambda i: (0, 0)), whole(gain), row_spec(LANES), row_spec(LANES)],
        out_specs=[row_spec(D), head_spec, head_spec, head_spec, row_spec(narrow), row_spec(narrow)],
        out_shape=[jax.ShapeDtypeStruct((tokens, D), bf16)]
        + [jax.ShapeDtypeStruct((heads, tokens, LANES), bf16)] * 3
        + [jax.ShapeDtypeStruct((tokens, narrow), f32)] * 2,
        cost_estimate=pl.CostEstimate(
            flops=2 * tokens * D * 3 * narrow, bytes_accessed=tokens * D * 8, transcendentals=0
        ),
        name="project",
    )(x_all, weights, gain, cosine, sine)


def attend_kernel(block, q_ref, k_ref, v_ref, att_ref, o_ref):
    i = pl.program_id(1)
    lane = lax.broadcasted_iota(jnp.int32, (block, LANES), 1)
    queries = [q_ref[h] for h in range(2)]

    def step(j, sums, diagonal):
        rows = pl.ds(pl.multiple_of(j * block, block), block)
        new = []
        for h in range(2):
            weight = jnp.exp(nt(queries[h], k_ref[h, rows, :]))
            if diagonal:
                row = lax.broadcasted_iota(jnp.int32, weight.shape, 0)
                column = lax.broadcasted_iota(jnp.int32, weight.shape, 1)
                weight = jnp.where(row >= column, weight, 0.0)
            new.append(sums[h] + nn(weight.astype(bf16), v_ref[h, rows, :]))
        return tuple(new)

    zero = jnp.zeros((block, LANES), f32)
    sums = lax.fori_loop(0, i, lambda j, s: step(j, s, False), (zero, zero))
    sums = step(i, sums, True)
    mixed = []
    for h in range(2):
        total = pltpu.roll(sums[h], HD, 1)
        o_ref[h] = jnp.where(lane < HD, sums[h] / total, jnp.log(sums[h]))
        mixed.append(o_ref[h])
    att_ref[...] = jnp.where(lane < HD, mixed[0], pltpu.roll(mixed[1], HD, 1)).astype(bf16)


def attend(queries, keys, values):
    heads, tokens, _ = queries.shape
    block = min(512, tokens)
    part = pl.BlockSpec((2, block, LANES), lambda p, i: (p, i, 0))
    whole = pl.BlockSpec((2, tokens, LANES), lambda p, i: (p, 0, 0))
    return pl.pallas_call(
        functools.partial(attend_kernel, block),
        grid=(heads // 2, tokens // block),
        in_specs=[part, whole, whole],
        out_specs=[pl.BlockSpec((block, LANES), lambda p, i: (i, p)), part],
        out_shape=[
            jax.ShapeDtypeStruct((tokens, heads * HD), bf16),
            jax.ShapeDtypeStruct((heads, tokens, LANES), f32),
        ],
        cost_estimate=pl.CostEstimate(
            flops=heads * tokens * tokens * LANES * 4,
            bytes_accessed=heads * tokens * LANES * 10,
            transcendentals=heads * tokens * tokens // 2,
        ),
        name="attend",
    )(queries, keys, values)


def with_parts(lane, base, value):
    high = value.astype(bf16).astype(f32)
    rest = value - high
    middle = rest.astype(bf16).astype(f32)
    low = rest - middle
    tail = jnp.where(lane == HD, high, jnp.where(lane == HD + 1, middle, jnp.where(lane == HD + 2, low, 0.0)))
    return jnp.where(lane < HD, base, tail).astype(bf16)


def attend_back_kernel(
    block, q_ref, k_ref, v_ref, o_ref, do_ref, dq_ref, dk_ref, dv_ref, dk_sum, dv_sum
):
    i = pl.program_id(1)
    count = pl.num_programs(1)
    lane = lax.broadcasted_iota(jnp.int32, (block, LANES), 1)

    @pl.when(i == 0)
    def _():
        dk_sum[...] = jnp.zeros_like(dk_sum)
        dv_sum[...] = jnp.zeros_like(dv_sum)

    d_pair = do_ref[...].astype(f32)
    d_heads = [d_pair, pltpu.roll(d_pair, HD, 1)]
    queries, upstream = [], []
    for h in range(2):
        mixed = o_ref[h]
        delta = jnp.sum(jnp.where(lane < HD, mixed * d_heads[h], 0.0), axis=1, keepdims=True)
        queries.append(with_parts(lane, q_ref[h].astype(f32), -mixed))
        upstream.append(with_parts(lane, d_heads[h], -jnp.broadcast_to(delta, (block, LANES))))

    def step(j, sums, diagonal):
        rows = pl.ds(pl.multiple_of(j * block, block), block)
        new = []
        for h in range(2):
            keys = k_ref[h, rows, :]
            probs = jnp.exp(nt(keys, queries[h]))
            if diagonal:
                row = lax.broadcasted_iota(jnp.int32, probs.shape, 0)
                column = lax.broadcasted_iota(jnp.int32, probs.shape, 1)
                probs = jnp.where(column >= row, probs, 0.0)
            d_scores = (probs * nt(v_ref[h, rows, :], upstream[h])).astype(bf16)
            dv_sum[h, rows, :] += nn(probs.astype(bf16), upstream[h])
            dk_sum[h, rows, :] += nn(d_scores, queries[h])
            new.append(sums[h] + tn(d_scores, keys))
        return tuple(new)

    zero = jnp.zeros((block, LANES), f32)
    sums = lax.fori_loop(0, i, lambda j, s: step(j, s, False), (zero, zero))
    sums = step(i, sums, True)
    dq_ref[...] = jnp.where(lane < HD, sums[0], pltpu.roll(sums[1], HD, 1)) * SCORE_SCALE

    @pl.when(i == count - 1)
    def _():
        def put(j, carry):
            rows = pl.ds(pl.multiple_of(j * block, block), block)
            dk_ref[rows, :] = jnp.where(lane < HD, dk_sum[0, rows, :], pltpu.roll(dk_sum[1, rows, :], HD, 1))
            dv_ref[rows, :] = jnp.where(lane < HD, dv_sum[0, rows, :], pltpu.roll(dv_sum[1, rows, :], HD, 1))
            return carry

        lax.fori_loop(0, count, put, 0)


def attend_back(queries, keys, values, mixed, d_attended):
    heads, tokens, _ = queries.shape
    block = min(512, tokens)
    part = pl.BlockSpec((2, block, LANES), lambda p, i: (p, i, 0))
    whole = pl.BlockSpec((2, tokens, LANES), lambda p, i: (p, 0, 0))
    pair_part = pl.BlockSpec((block, LANES), lambda p, i: (i, p))
    pair_whole = pl.BlockSpec((tokens, LANES), lambda p, i: (0, p))
    return pl.pallas_call(
        functools.partial(attend_back_kernel, block),
        grid=(heads // 2, tokens // block),
        in_specs=[part, whole, whole, part, pair_part],
        out_specs=[pair_part, pair_whole, pair_whole],
        out_shape=[jax.ShapeDtypeStruct((tokens, heads * HD), f32)] * 3,
        scratch_shapes=[pltpu.VMEM((2, tokens, LANES), f32)] * 2,
        cost_estimate=pl.CostEstimate(
            flops=heads * tokens * tokens * LANES * 10,
            bytes_accessed=heads * tokens * LANES * 20,
            transcendentals=heads * tokens * tokens // 2,
        ),
        name="attend_back",
    )(queries, keys, values, mixed, d_attended)


def project_back_kernel(
    narrow, dq_ref, dk_ref, dv_ref, qr_ref, kr_ref, gain_ref, cos_ref, sin_ref, out_ref, gg_ref
):
    rows = dq_ref.shape[0]
    lane = lax.broadcasted_iota(jnp.int32, (rows, LANES), 1)
    cosine, sine = cos_ref[...], sin_ref[...]

    @pl.when(pl.program_id(0) == 0)
    def _():
        gg_ref[...] = jnp.zeros_like(gg_ref)

    for which in range(2):
        d_ref, rot_ref = ((dq_ref, qr_ref), (dk_ref, kr_ref))[which]
        turned = rot_ref[...]
        inverse = lax.rsqrt(head_sums(turned * turned) + EPSILON)
        unit_rows = turned * inverse
        upstream = d_ref[...]
        gg_ref[...] += jnp.sum(upstream * unit_rows, axis=0, keepdims=True)
        upstream = upstream * gain_ref[...]
        back = inverse * (upstream - unit_rows * head_sums(unit_rows * upstream))
        for pair in range(narrow // LANES):
            here = back[:, pair * LANES : (pair + 1) * LANES]
            here = here * cosine - swap_halves(here, lane) * sine
            out_ref[:, which * narrow + pair * LANES : which * narrow + (pair + 1) * LANES] = here.astype(bf16)
    out_ref[:, 2 * narrow : 3 * narrow] = dv_ref[...].astype(bf16)


def project_back(d_queries, d_keys, d_values, q_turned, k_turned, gain, cosine, sine):
    tokens, narrow = d_queries.shape
    rows = min(512, tokens)
    row_spec = lambda width: pl.BlockSpec((rows, width), lambda i: (i, 0))
    one = pl.BlockSpec((1, narrow), lambda i: (0, 0))
    return pl.pallas_call(
        functools.partial(project_back_kernel, narrow),
        grid=(tokens // rows,),
        in_specs=[row_spec(narrow)] * 5 + [one, row_spec(LANES), row_spec(LANES)],
        out_specs=[row_spec(3 * narrow), one],
        out_shape=[
            jax.ShapeDtypeStruct((tokens, 3 * narrow), bf16),
            jax.ShapeDtypeStruct((1, narrow), f32),
        ],
        cost_estimate=pl.CostEstimate(
            flops=tokens * narrow * 60, bytes_accessed=tokens * narrow * 26, transcendentals=0
        ),
        name="project_back",
    )(d_queries, d_keys, d_values, q_turned, k_turned, gain, cosine, sine)


MESH = pl.DeviceIdType.MESH


class Group:
    def __init__(self, size, steps, tokens):
        self.size, self.steps = size, steps
        self.chips = size // 2
        self.own = tokens // size
        self.rows = self.own // steps
        self.dp, self.me = lax.axis_index("dp"), lax.axis_index("mp")
        self.chip, self.core = self.me // 2, lax.rem(self.me, 2)
        self.partner = self.me + 1 - 2 * self.core

    def other(self, k, core):
        return 2 * lax.rem(self.chip + k, self.chips) + core

    def slot(self, device):
        k = lax.rem(device // 2 - self.chip + self.chips, self.chips)
        return jnp.where(k == 0, 0, 2 * k - 1 + (lax.rem(device, 2) != self.core).astype(jnp.int32))

    def piece(self, ref, index, step):
        return ref.at[index, pl.ds(pl.multiple_of(step * self.rows, self.rows), self.rows), :]

    def copy(self, source, target, send, receive, device):
        return pltpu.make_async_remote_copy(
            src_ref=source,
            dst_ref=target,
            send_sem=send,
            recv_sem=receive,
            device_id=(self.dp, device),
            device_id_type=MESH,
        )

    def meet(self, everyone=False):
        barrier = pltpu.get_barrier_semaphore()
        devices = [self.partner] + [self.other(k, self.core) for k in range(1, self.chips)]
        if everyone:
            devices = [lax.rem(self.me + j, self.size) for j in range(1, self.size)]
        for device in devices:
            pl.semaphore_signal(barrier, inc=1, device_id=(self.dp, device), device_id_type=MESH)
        pl.semaphore_wait(barrier, len(devices))

    def place(self, i, remote_first=False):
        size, steps = self.size, self.steps
        others = steps * (size - 1)
        if remote_first:
            is_own = i >= others
            j = jnp.where(is_own, 0, i)
            s = jnp.where(is_own, i - others, j // (size - 1))
            r = lax.rem(lax.rem(j, size - 1) + 1, size - 1)
        else:
            is_own = i < steps
            j = jnp.where(is_own, 0, i - steps)
            s = jnp.where(is_own, i, j // (size - 1))
            r = lax.rem(j, size - 1)
        other = jnp.logical_not(is_own)
        is_partner = jnp.logical_and(other, r == 0)
        remote = jnp.logical_and(other, r > 0)
        is_first = jnp.logical_and(remote, lax.rem(r, 2) == 1)
        is_second = jnp.logical_and(remote, lax.rem(r, 2) == 0)
        k = jnp.where(remote, (r + 1) // 2, 0)
        core = jnp.where(jnp.logical_or(is_own, is_first), self.core, 1 - self.core)
        return self.other(k, core), s, k, is_own, is_partner, is_first, is_second

    def run(self, compute, gather=None, settle=None, remote_first=False, after=None, ready=(), between=None):
        steps, chips, size = self.steps, self.chips, self.size

        if gather:
            own_ref, all_ref, g_send, g_recv = gather

            def own_piece(s):
                return own_ref.at[pl.ds(pl.multiple_of(s * self.rows, self.rows), self.rows), :]

            def start_own(s, carry):
                for k in range(1, chips):
                    self.copy(own_piece(s), self.piece(all_ref, self.me, s), g_send.at[k, s], g_recv.at[self.me, s], self.other(k, self.core)).start()
                self.copy(own_piece(s), self.piece(all_ref, self.me, s), g_send.at[0, s], g_recv.at[self.me, s], self.partner).start()
                return carry

            lax.fori_loop(0, steps, start_own, 0)
            all_ref[self.me] = own_ref[...]

            def got(device, s):
                here = self.piece(all_ref, device, s)
                self.copy(here, here, g_send.at[0, s], g_recv.at[device, s], self.partner).wait_recv()

            def forward(k, s):
                device = self.other(k, self.core)
                here = self.piece(all_ref, device, s)
                return self.copy(here, here, g_send.at[chips + k - 1, s], g_recv.at[device, s], self.partner)

        if settle:
            out_ref, mine, kept, to_partner, from_partner, to_chip, from_chip, p_send, p_recv, x_send, x_recv = settle

            def to_partner_copy(k, s):
                return self.copy(self.piece(to_partner, k, s), self.piece(from_partner, k, s), p_send.at[k, s], p_recv.at[k, s], self.partner)

            def to_chip_copy(k, s):
                return self.copy(self.piece(to_chip, k - 1, s), self.piece(from_chip, k - 1, s), x_send.at[k - 1, s], x_recv.at[k - 1, s], self.other(k, self.core))

        for copy in ready:
            copy.wait()

        def item(i, carry):
            device, s, k, is_own, is_partner, is_first, is_second = self.place(i, remote_first)
            if gather:

                @pl.when(jnp.logical_not(is_own))
                def _():
                    got(device, s)

                @pl.when(is_first)
                def _():
                    forward(k, s).start()

            term = compute(device, s, i)
            if between:
                between(device, jnp.logical_or(i == steps - 1, jnp.logical_and(is_partner, s == steps - 1)))
            if settle:
                here = pl.ds(pl.multiple_of(s * self.rows, self.rows), self.rows)

                @pl.when(is_own)
                def _():
                    mine[here, :] = term

                @pl.when(is_first)
                def _():
                    kept[...] = term

                @pl.when(jnp.logical_or(is_partner, is_second))
                def _():
                    to_partner[k, here, :] = term.astype(bf16)
                    to_partner_copy(k, s).start()

                @pl.when(is_second)
                def _():
                    to_partner_copy(k, s).wait_recv()
                    to_chip[k - 1, here, :] = (kept[...] + from_partner[k, here, :].astype(f32)).astype(bf16)
                    to_chip_copy(k, s).start()

            return carry

        lax.fori_loop(0, size * steps, item, 0)

        def end(s, carry):
            if settle:
                here = pl.ds(pl.multiple_of(s * self.rows, self.rows), self.rows)
                to_partner_copy(0, s).wait_recv()
                total = mine[here, :] + from_partner[0, here, :].astype(f32)
                for k in range(1, chips):
                    to_chip_copy(k, s).wait_recv()
                    total = total + from_chip[k - 1, here, :].astype(f32)
                out_ref[here, :] = total
                if after:
                    after(s)
                for k in range(chips):
                    to_partner_copy(k, s).wait_send()
                for k in range(1, chips):
                    to_chip_copy(k, s).wait_send()
            if gather:
                for k in range(2 * chips - 1):
                    self.copy(own_piece(s), own_piece(s), g_send.at[k, s], g_recv.at[0, s], self.partner).wait_send()
            return carry

        self.end = lambda first=0, last=steps: lax.fori_loop(first, last, end, 0)


def settle_scratch(size, steps, tokens):
    own, chips = tokens // size, size // 2
    return [
        pltpu.VMEM((own, D), f32),
        pltpu.VMEM((own // steps, D), f32),
        pltpu.VMEM((chips, own, D), bf16),
        pltpu.VMEM((chips, own, D), bf16),
        pltpu.VMEM((chips - 1, own, D), bf16),
        pltpu.VMEM((chips - 1, own, D), bf16),
        pltpu.SemaphoreType.DMA((chips, steps)),
        pltpu.SemaphoreType.DMA((chips, steps)),
        pltpu.SemaphoreType.DMA((chips - 1, steps)),
        pltpu.SemaphoreType.DMA((chips - 1, steps)),
    ]


def gather_sems(size, steps):
    return [pltpu.SemaphoreType.DMA((size - 1, steps)), pltpu.SemaphoreType.DMA((size, steps))]


VMEM_WHOLE = pl.BlockSpec(memory_space=pltpu.VMEM)
ANYWHERE = pl.BlockSpec(memory_space=pl.ANY)
GRANT = 63 << 20


def weight_scratch(rows, count=1):
    return [pltpu.VMEM((rows, D), bf16)] * count + [pltpu.SemaphoreType.DMA((count,))]


def weight_copies(weights, buffers, sem, first):
    copies = []
    for i, buffer in enumerate(buffers):
        copies.append(pltpu.make_async_copy(weights.at[pl.ds(first, buffer.shape[0]), :], buffer, sem.at[i]))
        first += buffer.shape[0]
    return copies


def remote_params(collective_id):
    return pltpu.CompilerParams(
        collective_id=collective_id, has_side_effects=True, vmem_limit_bytes=GRANT
    )


def attention_sum_kernel(
    size, steps, first_row, rows_ref, w_hbm, start_ref, rates_ref,
    out_ref, middle_ref, low_ref, w_ref, w_sem, *scratch
):
    tokens = rows_ref.shape[0]
    group = Group(size, steps, tokens)
    (copy,) = weight_copies(w_hbm, [w_ref], w_sem, first_row)
    copy.start()
    group.meet()
    copy.wait()

    def compute(device, s, i):
        first = pl.multiple_of(device * group.own + s * group.rows, group.rows)
        return nn(rows_ref[pl.ds(first, group.rows), :], w_ref[...])

    def after(s):
        here = pl.ds(pl.multiple_of(s * group.rows, group.rows), group.rows)
        middle = blend_branch(start_ref[here, :], out_ref[here, :], rates_ref[1:2, :])[2]
        middle_ref[here, :] = middle
        low_ref[here, :] = middle.astype(bf16)

    group.run(compute, settle=(out_ref, *scratch), remote_first=True, after=after)
    group.end()


def attention_sum(rows, weights, start_unit, rates, first_row, size, steps, collective_id):
    tokens, depth = rows.shape
    own = jax.ShapeDtypeStruct((tokens // size, D), f32)
    return pl.pallas_call(
        functools.partial(attention_sum_kernel, size, steps, first_row),
        out_shape=[own, own, jax.ShapeDtypeStruct(own.shape, bf16)],
        in_specs=[VMEM_WHOLE, ANYWHERE, VMEM_WHOLE, VMEM_WHOLE],
        out_specs=[VMEM_WHOLE] * 3,
        scratch_shapes=weight_scratch(depth) + settle_scratch(size, steps, tokens),
        compiler_params=remote_params(collective_id),
        cost_estimate=pl.CostEstimate(flops=2 * tokens * depth * D, bytes_accessed=tokens * D * 8, transcendentals=0),
        name="attention_sum",
    )(rows, weights, start_unit, rates)


def mlp_kernel(
    size, steps, own_ref, w_hbm, scale_ref, middle_ref, cot_ref, rates_ref,
    out_ref, rows_ref, ur_hbm, gr_hbm, d_mlp_ref, d_middle_ref, g_rate_ref, branch_ref,
    up_ref, gate_ref, down_ref, w_sem, u_buf, g_buf, b_sem, *scratch
):
    tokens = own_ref.shape[0] * size
    group = Group(size, steps, tokens)
    copies = weight_copies(w_hbm, [up_ref, gate_ref, down_ref], w_sem, scale_ref.shape[1])
    for c in copies:
        c.start()
    group.meet()

    def save(i, device, s):
        slot = lax.rem(i, 2)
        rows = pl.ds(pl.multiple_of(device * group.own + s * group.rows, group.rows), group.rows)
        return (
            pltpu.make_async_copy(u_buf.at[slot], ur_hbm.at[rows, :], b_sem.at[0, slot]),
            pltpu.make_async_copy(g_buf.at[slot], gr_hbm.at[rows, :], b_sem.at[1, slot]),
        )

    def compute(device, s, i):
        slot = lax.rem(i, 2)

        @pl.when(i >= 2)
        def _():
            for c in save(i, device, s):
                c.wait()

        rows = group.piece(rows_ref, device, s)[...]
        up_raw = nt(rows, up_ref[...])
        gate_raw = nt(rows, gate_ref[...])
        u_buf[slot] = up_raw
        g_buf[slot] = gate_raw
        for c in save(i, device, s):
            c.start()
        gate_val = scale_ref[1:2, :] * gate_raw
        product = (scale_ref[0:1, :] * up_raw * (gate_val * jax.nn.sigmoid(gate_val))).astype(bf16)
        return nn(product, down_ref[...])

    g_rate_ref[...] = jnp.zeros_like(g_rate_ref)

    def after(s):
        here = pl.ds(pl.multiple_of(s * group.rows, group.rows), group.rows)
        middle, rate = middle_ref[here, :], rates_ref[2:3, :]
        branch_unit, branch_inv, mixed, mixed_inv = blend_branch(middle, branch_ref[here, :], rate)
        out_ref[here, :] = mixed
        upstream = jnp.concatenate([cot_ref[d, here, :] for d in range(size)], axis=1).astype(f32)
        d_middle, d_branch, g_rate = blend_back(
            middle, branch_unit, branch_inv, mixed, mixed_inv, rate, upstream
        )
        d_middle_ref[here, :] = d_middle
        d_mlp_ref[here, :] = d_branch.astype(bf16)
        g_rate_ref[...] += g_rate[None]

    group.run(
        compute, gather=(own_ref, rows_ref, scratch[0], scratch[1]), settle=(branch_ref, *scratch[2:]), ready=copies, after=after
    )
    for i in range(2):
        for c in save(i, 0, 0):
            c.wait()
    group.end()


def mlp(own, weights, scales, middle, cot_all, rates, size, steps, collective_id):
    hidden = scales.shape[1]
    tokens = own.shape[0] * size
    rows = own.shape[0] // steps
    return pl.pallas_call(
        functools.partial(mlp_kernel, size, steps),
        out_shape=[
            jax.ShapeDtypeStruct((own.shape[0], D), f32),
            jax.ShapeDtypeStruct((size, own.shape[0], D), bf16),
            jax.ShapeDtypeStruct((tokens, hidden), f32),
            jax.ShapeDtypeStruct((tokens, hidden), f32),
            jax.ShapeDtypeStruct((own.shape[0], D), bf16),
            jax.ShapeDtypeStruct((own.shape[0], D), f32),
            jax.ShapeDtypeStruct((1, D), f32),
        ],
        in_specs=[VMEM_WHOLE, ANYWHERE] + [VMEM_WHOLE] * 4,
        out_specs=[VMEM_WHOLE, VMEM_WHOLE, ANYWHERE, ANYWHERE] + [VMEM_WHOLE] * 3,
        scratch_shapes=[pltpu.VMEM((own.shape[0], D), f32)]
        + weight_scratch(hidden, 3)
        + [
            pltpu.VMEM((2, rows, hidden), f32),
            pltpu.VMEM((2, rows, hidden), f32),
            pltpu.SemaphoreType.DMA((2, 2)),
        ]
        + gather_sems(size, steps)
        + settle_scratch(size, steps, tokens),
        compiler_params=remote_params(collective_id),
        cost_estimate=pl.CostEstimate(flops=6 * tokens * hidden * D, bytes_accessed=tokens * D * 12, transcendentals=tokens * hidden),
        name="mlp",
    )(own, weights, scales, middle, cot_all, rates)


def mlp_back_kernel(
    size, steps, own_ref, w_hbm, scale_ref, ur_hbm, gr_hbm, middle_rows_ref, d_middle_hbm, start_hbm, branch_hbm, rates_ref,
    d_attn_ref, d_start_ref, g_rate_ref, gs_ref, wide_hbm, down_hbm,
    stage, stage_sem, late, late_sem,
    sum_ref, rows_ref, product_ref, d_ref, grads_sum,
    up_ref, gate_ref, down_ref, w_sem, u_buf, g_buf, b_sem, *scratch
):
    tokens = own_ref.shape[0] * size
    group = Group(size, steps, tokens)

    def load(i):
        device, s = group.place(i)[:2]
        slot = lax.rem(i, 2)
        rows = pl.ds(pl.multiple_of(device * group.own + s * group.rows, group.rows), group.rows)
        return (
            pltpu.make_async_copy(ur_hbm.at[rows, :], u_buf.at[slot], b_sem.at[0, slot]),
            pltpu.make_async_copy(gr_hbm.at[rows, :], g_buf.at[slot], b_sem.at[1, slot]),
        )

    copies = weight_copies(w_hbm, [up_ref, gate_ref, down_ref], w_sem, scale_ref.shape[1])
    for c in (*load(0), *copies):
        c.start()
    gs_ref[...] = jnp.zeros_like(gs_ref)
    g_rate_ref[...] = jnp.zeros_like(g_rate_ref)
    group.meet()
    hidden = scale_ref.shape[1]
    part = min(256, hidden)

    def weight_grads(device):
        rows = pl.ds(pl.multiple_of(group.slot(device) * group.own, group.own), group.own)

        def one(source, offset, other):
            def column(c, carry):
                first = pl.multiple_of(c * part, part)
                to = pl.ds(pl.multiple_of(offset + first, part), part)
                term = tn(source[rows, pl.ds(first, part)], other[device])
                grads_sum[to, :] += term
                return carry

            lax.fori_loop(0, source.shape[1] // part, column, 0)

        one(d_ref, 0, middle_rows_ref)
        one(product_ref, 2 * hidden, rows_ref)

    def clear(c, carry):
        grads_sum[pl.ds(pl.multiple_of(c * part, part), part), :] = jnp.zeros((part, D), f32)
        return carry

    lax.fori_loop(0, 3 * hidden // part, clear, 0)

    def between(device, done):
        @pl.when(done)
        def _():
            weight_grads(device)

    def late_copies(s):
        here = pl.ds(pl.multiple_of(s * group.rows, group.rows), group.rows)
        return [
            pltpu.make_async_copy(ref.at[here, :], late.at[lax.rem(s, 2), i], late_sem.at[lax.rem(s, 2), i])
            for i, ref in enumerate((start_hbm, branch_hbm, d_middle_hbm))
        ]

    for c in late_copies(0):
        c.start()

    def after(s):
        here = pl.ds(pl.multiple_of(s * group.rows, group.rows), group.rows)
        for c in late_copies(s):
            c.wait()

        @pl.when(s + 1 < steps)
        def _():
            for c in late_copies(s + 1):
                c.start()

        start, branch, d_middle = [late[lax.rem(s, 2), i] for i in range(3)]
        rate = rates_ref[1:2, :]
        branch_unit, branch_inv, middle, middle_inv = blend_branch(start, branch, rate)
        d_start, d_branch, g_rate = blend_back(
            start, branch_unit, branch_inv, middle, middle_inv, rate, d_middle + sum_ref[here, :]
        )
        d_start_ref[here, :] = d_start
        d_attn_ref[here, :] = d_branch.astype(bf16)
        g_rate_ref[...] += g_rate[None]

    def compute(device, s, i):
        slot = lax.rem(i, 2)

        @pl.when(i + 1 < size * steps)
        def _():
            for c in load(i + 1):
                c.start()

        rows = group.piece(rows_ref, device, s)[...]
        d_product = nt(rows, down_ref[...])
        for c in load(i):
            c.wait()
        first = pl.multiple_of(group.slot(device) * group.own + s * group.rows, group.rows)
        here = pl.ds(first, group.rows)
        up_raw, gate_raw = u_buf[slot], g_buf[slot]
        up_val = scale_ref[0:1, :] * up_raw
        gate_val = scale_ref[1:2, :] * gate_raw
        sigmoid = jax.nn.sigmoid(gate_val)
        activated = gate_val * sigmoid
        product_ref[here, :] = (up_val * activated).astype(bf16)
        d_up = d_product * activated
        d_gate = d_product * up_val * (sigmoid * (1.0 + gate_val * (1.0 - sigmoid)))
        gs_ref[0:1, :] += jnp.sum(d_up * up_raw, axis=0, keepdims=True)
        gs_ref[1:2, :] += jnp.sum(d_gate * gate_raw, axis=0, keepdims=True)
        d_up_raw = (d_up * scale_ref[0:1, :]).astype(bf16)
        d_gate_raw = (d_gate * scale_ref[1:2, :]).astype(bf16)
        d_ref[here, :hidden] = d_up_raw
        d_ref[here, hidden:] = d_gate_raw
        return nn(d_up_raw, up_ref[...]) + nn(d_gate_raw, gate_ref[...])

    group.run(
        compute, gather=(own_ref, rows_ref, scratch[0], scratch[1]), settle=(sum_ref, *scratch[2:]), ready=copies,
        after=after, between=between,
    )

    def rest(j, carry):
        weight_grads(group.other(1 + j // 2, lax.rem(j, 2)))
        return carry

    lax.fori_loop(0, size - 2, rest, 0)

    wide_parts = 2 * hidden // part

    def stage_copy(c, ref, first):
        here = pl.ds(pl.multiple_of((c - first) * part, part), part)
        return pltpu.make_async_copy(stage.at[lax.rem(c, 2)], ref.at[here, :], stage_sem.at[lax.rem(c, 2)])

    def put(c, carry):
        @pl.when(c >= 2)
        def _():
            stage_copy(lax.rem(c, 2), wide_hbm, 0).wait()

        stage[lax.rem(c, 2)] = grads_sum[pl.ds(pl.multiple_of(c * part, part), part), :].astype(bf16)

        @pl.when(c < wide_parts)
        def _():
            stage_copy(c, wide_hbm, 0).start()

        @pl.when(c >= wide_parts)
        def _():
            stage_copy(c, down_hbm, wide_parts).start()

        return carry

    parts = 3 * hidden // part
    lax.fori_loop(0, parts, put, 0)
    group.end()
    for c in range(2):
        stage_copy(c, wide_hbm, 0).wait()


def mlp_back(own, weights, scales, up_raw, gate_raw, middle_rows, d_middle, start_unit, branch, rates, size, steps, collective_id):
    tokens, hidden = up_raw.shape
    rows = own.shape[0] // steps
    return pl.pallas_call(
        functools.partial(mlp_back_kernel, size, steps),
        out_shape=[
            jax.ShapeDtypeStruct((own.shape[0], D), bf16),
            jax.ShapeDtypeStruct((own.shape[0], D), f32),
            jax.ShapeDtypeStruct((1, D), f32),
            jax.ShapeDtypeStruct((2, hidden), f32),
            jax.ShapeDtypeStruct((2 * hidden, D), bf16),
            jax.ShapeDtypeStruct((hidden, D), bf16),
        ],
        in_specs=[VMEM_WHOLE, ANYWHERE, VMEM_WHOLE, ANYWHERE, ANYWHERE, VMEM_WHOLE] + [ANYWHERE] * 3 + [VMEM_WHOLE],
        out_specs=[VMEM_WHOLE] * 4 + [ANYWHERE] * 2,
        scratch_shapes=[
            pltpu.VMEM((2, min(256, hidden), D), bf16),
            pltpu.SemaphoreType.DMA((2,)),
            pltpu.VMEM((2, 3, rows, D), f32),
            pltpu.SemaphoreType.DMA((2, 3)),
            pltpu.VMEM((own.shape[0], D), f32),
            pltpu.VMEM((size, own.shape[0], D), bf16),
            pltpu.VMEM((tokens - own.shape[0], hidden), bf16),
            pltpu.VMEM((tokens - own.shape[0], 2 * hidden), bf16),
            pltpu.VMEM((3 * hidden, D), f32),
        ]
        + weight_scratch(hidden, 3)
        + [
            pltpu.VMEM((2, rows, hidden), f32),
            pltpu.VMEM((2, rows, hidden), f32),
            pltpu.SemaphoreType.DMA((2, 2)),
        ]
        + gather_sems(size, steps)
        + settle_scratch(size, steps, tokens),
        compiler_params=remote_params(collective_id),
        cost_estimate=pl.CostEstimate(flops=6 * tokens * hidden * D, bytes_accessed=tokens * D * 24, transcendentals=tokens * hidden),
        name="mlp_back",
    )(own, weights, scales, up_raw, gate_raw, middle_rows, d_middle, start_unit, branch, rates)


def gather_project_kernel(size, steps, first_row, own_ref, w_hbm, out_ref, rows_ref, w_ref, w_sem, *scratch):
    tokens = own_ref.shape[0] * size
    group = Group(size, steps, tokens)
    copies = weight_copies(w_hbm, [w_ref], w_sem, first_row)
    copies[0].start()
    group.meet()

    def compute(device, s, i):
        first = pl.multiple_of(device * group.own + s * group.rows, group.rows)
        out_ref[pl.ds(first, group.rows), :] = nt(group.piece(rows_ref, device, s)[...], w_ref[...]).astype(bf16)

    group.run(compute, gather=(own_ref, rows_ref, scratch[0], scratch[1]), ready=copies)
    group.end()


def gather_project(own, weights, width, first_row, size, steps, collective_id, name):
    tokens = own.shape[0] * size
    return pl.pallas_call(
        functools.partial(gather_project_kernel, size, steps, first_row),
        out_shape=[
            jax.ShapeDtypeStruct((tokens, width), bf16),
            jax.ShapeDtypeStruct((size, own.shape[0], D), bf16),
        ],
        in_specs=[VMEM_WHOLE, ANYWHERE],
        out_specs=[VMEM_WHOLE, VMEM_WHOLE],
        scratch_shapes=weight_scratch(width) + gather_sems(size, steps),
        compiler_params=remote_params(collective_id),
        cost_estimate=pl.CostEstimate(flops=2 * tokens * width * D, bytes_accessed=tokens * D * 4, transcendentals=0),
        name=name,
    )(own, weights)


def start_sum_kernel(
    size, steps, rows_ref, w_hbm, base_ref, unit_ref, inv_ref, operand_hbm, attended_hbm, d_attn_hbm,
    out_ref, grads_ref, operand_ref, attended_ref, d_attn_ref, late_sem, w_ref, w_sem, total_ref, pieces, d_send, d_recv, *scratch
):
    tokens = rows_ref.shape[0]
    narrow = out_ref.shape[2]
    group = Group(size, steps, tokens)
    copies = weight_copies(w_hbm, [w_ref], w_sem, 0)
    copies[0].start()
    late = [
        pltpu.make_async_copy(source, target, late_sem.at[i])
        for i, (source, target) in enumerate(
            ((operand_hbm, operand_ref), (attended_hbm, attended_ref), (d_attn_hbm, d_attn_ref))
        )
    ]
    for copy in late:
        copy.start()
    group.meet(everyone=True)
    copies[0].wait()

    def compute(device, s, i):
        first = pl.multiple_of(device * group.own + s * group.rows, group.rows)
        return nn(rows_ref[pl.ds(first, group.rows), :], w_ref[...])

    def deal(j, s):
        device = lax.rem(group.me + j, size)
        return group.copy(
            group.piece(pieces, device, s), group.piece(out_ref, group.me, s), d_send.at[j - 1, s], d_recv.at[group.me, s], device
        )

    def after(s):
        here = pl.ds(pl.multiple_of(s * group.rows, group.rows), group.rows)
        back = normalize_back(unit_ref[here, :], inv_ref[here, :], base_ref[here, :] + total_ref[here, :])
        for device in range(size):
            pieces[device, here, :] = back[:, device * narrow : (device + 1) * narrow].astype(bf16)
        out_ref[group.me, here, :] = pieces[group.me, here, :]
        for j in range(1, size):
            deal(j, s).start()

    group.run(compute, settle=(total_ref, *scratch), remote_first=True, after=after)

    for copy in late:
        copy.wait()
    for c in range(3):
        here = slice(c * narrow, (c + 1) * narrow)
        grads_ref[here, :] = tn(rows_ref[:, here], operand_ref[...]).astype(bf16)
        group.end(c * steps // 4, (c + 1) * steps // 4)
    out_sum = jnp.zeros((narrow, D), f32)
    for d in range(size):
        out_sum += tn(attended_ref[d * group.own : (d + 1) * group.own, :], d_attn_ref[d])
    grads_ref[3 * narrow :, :] = out_sum.astype(bf16)
    group.end(3 * steps // 4, steps)

    def finish(s, carry):
        for j in range(1, size):
            device = lax.rem(group.me + j, size)
            here = group.piece(out_ref, device, s)
            group.copy(here, here, d_send.at[j - 1, s], d_recv.at[device, s], group.partner).wait_recv()
            deal(j, s).wait_send()
        return carry

    lax.fori_loop(0, steps, finish, 0)


def start_sum(rows, weights, base, unit_rows, inverse, operand, attended, d_attn_rows, size, steps, collective_id):
    tokens, depth = rows.shape
    own, narrow = tokens // size, D // size
    return pl.pallas_call(
        functools.partial(start_sum_kernel, size, steps),
        out_shape=[jax.ShapeDtypeStruct((size, own, narrow), bf16), jax.ShapeDtypeStruct((4 * narrow, D), bf16)],
        in_specs=[VMEM_WHOLE, ANYWHERE] + [VMEM_WHOLE] * 3 + [ANYWHERE] * 3,
        out_specs=[VMEM_WHOLE] * 2,
        scratch_shapes=[
            pltpu.VMEM(operand.shape, bf16),
            pltpu.VMEM(attended.shape, bf16),
            pltpu.VMEM(d_attn_rows.shape, bf16),
            pltpu.SemaphoreType.DMA((3,)),
        ]
        + weight_scratch(depth)
        + [
            pltpu.VMEM((own, D), f32),
            pltpu.VMEM((size, own, narrow), bf16),
            pltpu.SemaphoreType.DMA((size - 1, steps)),
            pltpu.SemaphoreType.DMA((size, steps)),
        ]
        + settle_scratch(size, steps, tokens),
        compiler_params=remote_params(collective_id),
        cost_estimate=pl.CostEstimate(flops=2 * tokens * depth * D, bytes_accessed=tokens * D * 8, transcendentals=0),
        name="start_sum",
    )(rows, weights, base, unit_rows, inverse, operand, attended, d_attn_rows)


def tail_plan(devices, rows):
    lines = min(4, devices)
    columns = devices // lines
    cuts = 2 if rows % (devices * 32) == 0 else 1
    return lines, columns, cuts, rows // (devices * cuts)


def tail_sum_kernel(
    devices, size, late_ref, early_ref, rates_ref, small_ref, late_out, early_out, small_out,
    y_land, y_sum, z_land, rate_parts, rate_land, pack, small_land,
    a_send, a_recv, b_send, b_recv, c_send, c_recv, d_send, d_recv, m_send, m_recv, s_send, s_recv
):
    dp, me = lax.axis_index("dp"), lax.axis_index("mp")
    lines, columns, cuts, rows = tail_plan(devices, late_ref.shape[0])
    a, b = dp // columns, lax.rem(dp, columns)
    span = lines * rows
    narrow = rate_parts.shape[2]
    chunks = [(early_ref, early_out, q) for q in range(cuts)] + [(late_ref, late_out, q) for q in range(cuts)]

    def remote(source, target, send, receive, device):
        return pltpu.make_async_remote_copy(
            src_ref=source, dst_ref=target, send_sem=send, recv_sem=receive, device_id=device, device_id_type=MESH
        )

    def peer(j):
        return lax.rem(dp + j, devices)

    def column(j):
        return lax.rem(b + j, columns)

    def line(j):
        return lax.rem(a + j, lines)

    barrier = pltpu.get_barrier_semaphore()

    def greet(j, carry):
        pl.semaphore_signal(barrier, inc=1, device_id=(peer(j), me), device_id_type=MESH)
        return carry

    lax.fori_loop(1, devices, greet, 0)
    for j in range(1, size):
        pl.semaphore_signal(barrier, inc=1, device_id=(dp, lax.rem(me + j, size)), device_id_type=MESH)
    pl.semaphore_wait(barrier, devices - 1 + size - 1)

    def part(ref, q, col):
        return ref.at[pl.ds(pl.multiple_of((q * columns + col) * span, span), span), :]

    def to_column(c, j):
        ref, _, q = chunks[c]
        return remote(part(ref, q, column(j)), y_land.at[c, b], a_send.at[c, j], a_recv.at[c, b], (a * columns + column(j), me))

    def from_column(c, j):
        here = y_land.at[c, column(j)]
        return remote(here, here, a_send.at[c, j], a_recv.at[c, column(j)], (a * columns + column(j), me))

    def to_line(c, j):
        there = pl.ds(pl.multiple_of(line(j) * rows, rows), rows)
        return remote(y_sum.at[c, there, :], z_land.at[c, a], b_send.at[c, j], b_recv.at[c, a], (line(j) * columns + b, me))

    def from_line(c, j):
        here = z_land.at[c, line(j)]
        return remote(here, here, b_send.at[c, j], b_recv.at[c, line(j)], (line(j) * columns + b, me))

    def sum_of(c, col, row):
        _, out, q = chunks[c]
        return out.at[(q * columns + col) * lines + row]

    def back_line(c, j):
        here = sum_of(c, b, a)
        return remote(here, here, c_send.at[c, j], c_recv.at[c, a], (line(j) * columns + b, me))

    def back_line_got(c, j):
        here = sum_of(c, b, line(j))
        return remote(here, here, c_send.at[c, j], c_recv.at[c, line(j)], (line(j) * columns + b, me))

    def back_column(c, i, j):
        here = sum_of(c, b, line(i))
        return remote(here, here, d_send.at[c, i, j], d_recv.at[c, line(i), b], (a * columns + column(j), me))

    def back_column_got(c, i, j):
        here = sum_of(c, column(j), line(i))
        return remote(here, here, d_send.at[c, i, j], d_recv.at[c, line(i), column(j)], (a * columns + column(j), me))

    def rate_copy(j):
        device = lax.rem(me + j, size)
        return remote(rate_parts.at[device], rate_land.at[me], m_send.at[j - 1], m_recv.at[me], (dp, device))

    for c in range(len(chunks)):
        for j in range(1, columns):
            to_column(c, j).start()
    for d in range(size):
        rate_parts[d, 0:2, :] = rates_ref[:, d * narrow : (d + 1) * narrow]
    for j in range(1, size):
        rate_copy(j).start()

    rates = rate_parts[me]
    for j in range(1, size):
        source = lax.rem(me + j, size)
        remote(rate_land.at[source], rate_land.at[source], m_send.at[j - 1], m_recv.at[source], (dp, source)).wait_recv()
        rates = rates + rate_land[source]
    pack[...] = small_ref[...]
    pack[3:5, :narrow] = rates[0:2, :]

    def small_copy(j):
        return remote(pack, small_land.at[dp], s_send.at[j - 1], s_recv.at[dp], (peer(j), me))

    def small_give(j, carry):
        small_copy(j).start()
        return carry

    lax.fori_loop(1, devices, small_give, 0)

    def settle_column(c):
        ref, _, q = chunks[c]
        for j in range(1, columns):
            from_column(c, j).wait_recv()

        def add(i, carry):
            here = pl.ds(pl.multiple_of(i * rows, rows), rows)
            own = pl.ds(pl.multiple_of((q * columns + b) * span + i * rows, rows), rows)
            total = ref[own, :].astype(f32)
            for j in range(1, columns):
                total = total + y_land[c, column(j), here, :].astype(f32)
            y_sum[c, here, :] = total.astype(bf16)
            return carry

        lax.fori_loop(0, lines, add, 0)
        for j in range(1, lines):
            to_line(c, j).start()

    def settle_line(c):
        for j in range(1, lines):
            from_line(c, j).wait_recv()
        total = y_sum[c, pl.ds(pl.multiple_of(a * rows, rows), rows), :].astype(f32)
        for j in range(1, lines):
            total = total + z_land[c, line(j)].astype(f32)
        sum_of(c, b, a)[...] = total.astype(bf16)
        for j in range(1, lines):
            back_line(c, j).start()
        for j in range(1, columns):
            back_column(c, 0, j).start()

    def pass_on(c):
        for i in range(1, lines):
            back_line_got(c, i).wait_recv()
            for j in range(1, columns):
                back_column(c, i, j).start()

    count = len(chunks)
    for step in range(count + 2):
        if step < count:
            settle_column(step)
        if 1 <= step <= count:
            settle_line(step - 1)
        if step >= 2:
            pass_on(step - 2)

    def small_take(j, total):
        source = peer(j)
        remote(small_land.at[source], small_land.at[source], s_send.at[j - 1], s_recv.at[source], (source, me)).wait_recv()
        return total + small_land[source]

    small_out[...] = lax.fori_loop(1, devices, small_take, pack[...])
    for c in range(count):
        for i in range(lines):
            for j in range(1, columns):
                back_column_got(c, i, j).wait_recv()
                back_column(c, i, j).wait_send()
        for j in range(1, lines):
            back_line(c, j).wait_send()
            to_line(c, j).wait_send()
        for j in range(1, columns):
            to_column(c, j).wait_send()

    def finish(j, carry):
        small_copy(j).wait_send()
        return carry

    lax.fori_loop(1, devices, finish, 0)
    for j in range(1, size):
        rate_copy(j).wait_send()


def tail_sum(late, early, rates, small, devices, size, collective_id):
    lines, columns, cuts, rows = tail_plan(devices, late.shape[0])
    narrow = D // size
    chunks = 2 * cuts
    dma = pltpu.SemaphoreType.DMA
    total = jax.ShapeDtypeStruct((late.shape[0] // rows, rows, D), bf16)
    return pl.pallas_call(
        functools.partial(tail_sum_kernel, devices, size),
        out_shape=[total, total, jax.ShapeDtypeStruct(small.shape, f32)],
        in_specs=[VMEM_WHOLE] * 4,
        out_specs=[VMEM_WHOLE] * 3,
        scratch_shapes=[
            pltpu.VMEM((chunks, columns, lines * rows, D), bf16),
            pltpu.VMEM((chunks, lines * rows, D), bf16),
            pltpu.VMEM((chunks, lines, rows, D), bf16),
            pltpu.VMEM((size, 8, narrow), f32),
            pltpu.VMEM((size, 8, narrow), f32),
            pltpu.VMEM(small.shape, f32),
            pltpu.VMEM((devices, *small.shape), f32),
            dma((chunks, columns)), dma((chunks, columns)),
            dma((chunks, lines)), dma((chunks, lines)),
            dma((chunks, lines)), dma((chunks, lines)),
            dma((chunks, lines, columns)), dma((chunks, lines, columns)),
            dma((size - 1,)), dma((size,)),
            dma((devices - 1,)), dma((devices,)),
        ],
        compiler_params=remote_params(collective_id),
        cost_estimate=pl.CostEstimate(flops=0, bytes_accessed=late.shape[0] * D * 16, transcendentals=0),
        name="tail_sum",
    )(late, early, rates, small)


def optimizer_kernel(
    counts, index_ref, attn_ref, wide_ref, down_ref, m_ref, f_ref, s_ref, mo_ref, fo_ref, so_ref, go_ref
):
    group = m_ref.shape[0]
    for j in range(group):
        slot = pl.program_id(0) * group + j
        block, live = index_ref[slot, 0], index_ref[slot, 1]

        @pl.when(live == 0)
        def _():
            for ref in (mo_ref, fo_ref, so_ref, go_ref):
                ref[j] = jnp.zeros_like(m_ref[j])

        for ref, first, last in (
            (attn_ref, 0, counts[0]),
            (wide_ref, counts[0], counts[0] + counts[1]),
            (down_ref, counts[0] + counts[1], sum(counts)),
        ):

            @pl.when(jnp.logical_and(live == 1, jnp.logical_and(block >= first, block < last)))
            def _():
                gradient = ref[block - first].astype(f32)
                stepped, first_new, second_new = adam_update(
                    m_ref[j], gradient, f_ref[j], s_ref[j], WEIGHT_DECAY, LEARN_RATE
                )
                go_ref[j] = gradient
                fo_ref[j] = first_new
                so_ref[j] = second_new
                mo_ref[j] = stepped * lax.rsqrt(jnp.sum(stepped * stepped, axis=-1, keepdims=True) + EPSILON)


def optimizer(index, attn_grads, wide_grads, down_grads, masters, firsts, seconds):
    slots, height, _ = masters.shape
    group = math.gcd(slots, 4)
    grads = [g.reshape(-1, height, D) for g in (attn_grads, wide_grads, down_grads)]
    block = pl.BlockSpec((group, height, D), lambda i, ref: (i, 0, 0))
    return pl.pallas_call(
        functools.partial(optimizer_kernel, tuple(g.shape[0] for g in grads)),
        grid_spec=pltpu.PrefetchScalarGridSpec(
            num_scalar_prefetch=1,
            grid=(slots // group,),
            in_specs=[pl.BlockSpec(memory_space=pltpu.VMEM)] * 3 + [block] * 3,
            out_specs=[block] * 4,
        ),
        out_shape=[jax.ShapeDtypeStruct(masters.shape, f32)] * 4,
        compiler_params=pltpu.CompilerParams(vmem_limit_bytes=GRANT),
        cost_estimate=pl.CostEstimate(flops=20 * masters.size, bytes_accessed=30 * masters.size, transcendentals=0),
        name="optimizer",
    )(index, *grads, masters, firsts, seconds)


def collect_kernel(count, places_ref, slots_hbm, out_ref, sems):
    def copy(b):
        return pltpu.make_async_copy(slots_hbm.at[places_ref[b]], out_ref.at[b], sems.at[b])

    def start(b, carry):
        copy(b).start()
        return carry

    def wait(b, carry):
        copy(b).wait()
        return carry

    lax.fori_loop(0, count, start, 0)
    lax.fori_loop(0, count, wait, 0)


def collect(places, slots):
    count, shape = places.shape[0], slots.shape[1:]
    return pl.pallas_call(
        functools.partial(collect_kernel, count),
        grid_spec=pltpu.PrefetchScalarGridSpec(
            num_scalar_prefetch=1,
            grid=(1,),
            in_specs=[pl.BlockSpec(memory_space=pl.ANY)],
            out_specs=pl.BlockSpec(memory_space=pltpu.VMEM),
            scratch_shapes=[pltpu.SemaphoreType.DMA((count,))],
        ),
        out_shape=jax.ShapeDtypeStruct((count, *shape), bf16),
        compiler_params=pltpu.CompilerParams(vmem_limit_bytes=GRANT),
        cost_estimate=pl.CostEstimate(flops=0, bytes_accessed=4 * count * math.prod(shape), transcendentals=0),
        name="collect",
    )(places, slots)


def spread_plan(devices, slots):
    lines = min(4, devices)
    columns = devices // lines
    across = slots * 5 // 32 if columns == 2 else 0
    cuts = next(q for q in (9, 3, 2, 1) if (slots - across) % q == 0)
    return lines, columns, across, cuts


def spread_kernel(
    devices, size, slots, height, slots_ref, x_ref, cot_ref, gains_ref,
    all_ref, x_all, cot_all, gains_all, cos_ref, sin_ref, gains_land,
    z_send, z_recv, y_send, y_recv, e_send, e_recv, x_send, x_recv, c_send, c_recv, w_send, w_recv, local_sem
):
    lines, columns, across, cuts = spread_plan(devices, slots)
    dp, me = lax.axis_index("dp"), lax.axis_index("mp")
    a, b = dp // columns, lax.rem(dp, columns)
    chips = size // 2
    chip, core = me // 2, lax.rem(me, 2)
    partner = me + 1 - 2 * core
    tokens, narrow = x_ref.shape
    own = tokens // size
    x_steps = x_recv.shape[1]
    x_rows = tokens // x_steps
    cut_rows = (slots - across) * height // cuts
    has_left, has_right = a > 0, a < lines - 1

    def remote(source, target, send, receive, device):
        return pltpu.make_async_remote_copy(
            src_ref=source, dst_ref=target, send_sem=send, recv_sem=receive, device_id=device, device_id_type=MESH
        )

    def column(j):
        return lax.rem(b + j, columns)

    def other(k, which):
        return 2 * lax.rem(chip + k, chips) + which

    def mp_peer(j):
        return lax.rem(me + j, size)

    barrier = pltpu.get_barrier_semaphore()

    def greet(device):
        pl.semaphore_signal(barrier, inc=1, device_id=device, device_id_type=MESH)

    for j in range(1, columns):
        greet((a * columns + column(j), me))
    for j in range(1, size):
        greet((dp, mp_peer(j)))

    @pl.when(has_left)
    def _():
        greet((dp - columns, me))

    @pl.when(has_right)
    def _():
        greet((dp + columns, me))

    pl.semaphore_wait(
        barrier, columns - 1 + size - 1 + has_left.astype(jnp.int32) + has_right.astype(jnp.int32)
    )

    items = cuts + (columns if across else 0)

    def region(ref, line, c, row=None):
        if c < cuts:
            source, first, count = line * columns + b, across * height + c * cut_rows, cut_rows
        else:
            source, first, count = line * columns + (c - cuts), 0, across * height
        return ref.at[source, pl.ds(first, count), :]

    def own_part(c):
        first, count = (across * height + c * cut_rows, cut_rows) if c < cuts else (0, across * height)
        return slots_ref.at[pl.ds(first, count), :]

    def along(line, c, to_right, source=None):
        here = region(all_ref, line, c)
        side = 1 if to_right else 0
        device = (dp + columns if to_right else dp - columns, me)
        return remote(here if source is None else source, here, z_send.at[line, side, c], z_recv.at[line, c], device)

    def over(line, c, j, source=None):
        here = region(all_ref, line, c)
        return remote(
            here if source is None else source, here, y_send.at[line, j, c], y_recv.at[line, b, c],
            (a * columns + column(j), me),
        )

    def over_got(line, column_from, c):
        first = across * height + c * cut_rows
        here = all_ref.at[line * columns + column_from, pl.ds(first, cut_rows), :]
        return remote(here, here, y_send.at[line, 1, c], y_recv.at[line, column_from, c], (dp, partner))

    def early(j):
        here = all_ref.at[dp, pl.ds(0, across * height), :]
        return remote(own_part(cuts), here, e_send.at[j], e_recv.at[b], (a * columns + column(j), me))

    def early_got(column_from):
        here = all_ref.at[a * columns + column_from, pl.ds(0, across * height), :]
        return remote(here, here, e_send.at[1], e_recv.at[column_from], (dp, partner))

    def x_piece(ref, s):
        return ref.at[pl.ds(s * x_rows, x_rows), :]

    def x_own(s, k):
        device = (dp, partner) if k == 0 else (dp, other(k, core))
        return remote(x_piece(x_ref, s), x_piece(x_all.at[me], s), x_send.at[k, s], x_recv.at[me, s], device)

    def x_forward(s, k):
        source = other(k, core)
        here = x_piece(x_all.at[source], s)
        return remote(here, here, x_send.at[chips + k - 1, s], x_recv.at[source, s], (dp, partner))

    def x_got(s, source):
        here = x_piece(x_all.at[source], s)
        return remote(here, here, x_send.at[0, s], x_recv.at[source, s], (dp, partner))

    def cot_own(j):
        device = mp_peer(j)
        rows = pl.ds(pl.multiple_of(device * own, own), own)
        return remote(cot_ref.at[rows, :], cot_all.at[me], c_send.at[j - 1], c_recv.at[me], (dp, device))

    def cot_got(j):
        here = cot_all.at[mp_peer(j)]
        return remote(here, here, c_send.at[j - 1], c_recv.at[mp_peer(j)], (dp, partner))

    def gains_own(j):
        return remote(gains_ref, gains_land.at[me], w_send.at[j - 1], w_recv.at[me], (dp, mp_peer(j)))

    if across:
        for j in range(1, columns):
            early(j).start()
    for j in range(1, size):
        gains_own(j).start()
    gains_land[me] = gains_ref[...]
    for c in range(cuts):
        for side, there in ((False, has_left), (True, has_right)):

            @pl.when(there)
            def _():
                along(a, c, side, own_part(c)).start()

        for j in range(1, columns):
            over(a, c, j, own_part(c)).start()
    for s in range(x_steps):
        for k in range(chips):
            x_own(s, (k + 1) % chips).start()
    for j in range(1, size):
        cot_own(j).start()
    local = [
        pltpu.make_async_copy(slots_ref, all_ref.at[dp], local_sem.at[0]),
        pltpu.make_async_copy(x_ref, x_all.at[me], local_sem.at[1]),
        pltpu.make_async_copy(
            cot_ref.at[pl.ds(pl.multiple_of(me * own, own), own), :], cot_all.at[me], local_sem.at[2]
        ),
    ]
    for copy in local:
        copy.start()
    if across:
        for j in range(1, columns):
            early_got(column(j)).wait_recv()
        for c in range(cuts, items):
            for side, there in ((False, has_left), (True, has_right)):
                mine = b == c - cuts

                @pl.when(jnp.logical_and(there, mine))
                def _():
                    along(a, c, side, own_part(c)).start()

                @pl.when(jnp.logical_and(there, jnp.logical_not(mine)))
                def _():
                    along(a, c, side).start()

    for s in range(x_steps):
        for k in range(1, chips):
            x_got(s, other(k, core)).wait_recv()
            x_forward(s, k).start()

    rope_rows = min(256, tokens)

    def rope_table(i, carry):
        here = pl.ds(pl.multiple_of(i * rope_rows, rope_rows), rope_rows)
        lane = lax.broadcasted_iota(jnp.int32, (rope_rows, LANES), 1)
        position = (lax.broadcasted_iota(jnp.int32, (rope_rows, LANES), 0) + i * rope_rows).astype(f32)
        j = lane % (HD // 2)
        angle = position * jnp.exp(j.astype(f32) * (-2.0 * math.log(10000.0) / HD))
        cos_ref[here, :] = jnp.cos(angle)
        sin_ref[here, :] = jnp.where(lane % HD < HD // 2, -1.0, 1.0) * jnp.sin(angle)
        return carry

    lax.fori_loop(0, tokens // rope_rows, rope_table, 0)

    for hop in range(1, lines):
        for c in range(items):
            for to_right in (True, False):
                line = a - hop if to_right else a + hop
                there = line >= 0 if to_right else line < lines
                onward = has_right if to_right else has_left

                @pl.when(there)
                def _():
                    along(line, c, to_right).wait_recv()

                    @pl.when(onward)
                    def _():
                        along(line, c, to_right).start()

                    if c < cuts:
                        for j in range(1, columns):
                            over(line, c, j).start()

    for line in range(lines):
        for c in range(cuts):
            for j in range(1, columns):
                over_got(line, column(j), c).wait_recv()
    for s in range(x_steps):
        x_got(s, partner).wait_recv()
        for k in range(1, chips):
            x_got(s, other(k, 1 - core)).wait_recv()
    for j in range(1, size):
        cot_got(j).wait_recv()
        here = gains_land.at[mp_peer(j)]
        remote(here, here, w_send.at[j - 1], w_recv.at[mp_peer(j)], (dp, partner)).wait_recv()
        gains_own(j).wait_send()
    for d in range(size):
        gains_all[:, d * narrow : (d + 1) * narrow] = gains_land[d]
    for copy in local:
        copy.wait()
    if across:
        for j in range(1, columns):
            early(j).wait_send()
    for s in range(x_steps):
        for k in range(chips):
            x_own(s, k).wait_send()
        for k in range(1, chips):
            x_forward(s, k).wait_send()
    for j in range(1, size):
        cot_own(j).wait_send()
    for line in range(lines):
        for c in range(items):
            @pl.when(jnp.logical_and(has_right, line <= a))
            def _():
                along(line, c, True).wait_send()

            @pl.when(jnp.logical_and(has_left, line >= a))
            def _():
                along(line, c, False).wait_send()

            if c < cuts:
                for j in range(1, columns):
                    over(line, c, j).wait_send()


def spread(slots_low, hidden_in, cotangent, gains, devices, size, collective_id):
    slots, height, _ = slots_low.shape
    tokens, narrow = hidden_in.shape
    lines, columns, across, cuts = spread_plan(devices, slots)
    items = cuts + (columns if across else 0)
    chips = size // 2
    x_steps = 4
    dma = pltpu.SemaphoreType.DMA
    return pl.pallas_call(
        functools.partial(spread_kernel, devices, size, slots, height),
        out_shape=[
            jax.ShapeDtypeStruct((devices, slots * height, D), bf16),
            jax.ShapeDtypeStruct((size, tokens, narrow), bf16),
            jax.ShapeDtypeStruct((size, tokens // size, narrow), bf16),
            jax.ShapeDtypeStruct((gains.shape[0], D), f32),
            jax.ShapeDtypeStruct((tokens, LANES), f32),
            jax.ShapeDtypeStruct((tokens, LANES), f32),
        ],
        in_specs=[VMEM_WHOLE] * 4,
        out_specs=[ANYWHERE] * 3 + [VMEM_WHOLE] * 3,
        scratch_shapes=[
            pltpu.VMEM((size, *gains.shape), f32),
            dma((lines, 2, items)),
            dma((lines, items)),
            dma((lines, columns, cuts)),
            dma((lines, columns, cuts)),
            dma((columns,)),
            dma((columns,)),
            dma((2 * chips - 1, x_steps)),
            dma((size, x_steps)),
            dma((size - 1,)),
            dma((size,)),
            dma((size - 1,)),
            dma((size,)),
            dma((3,)),
        ],
        compiler_params=remote_params(collective_id),
        cost_estimate=pl.CostEstimate(flops=0, bytes_accessed=devices * slots * height * D * 4, transcendentals=0),
        name="spread",
    )(slots_low.reshape(slots * height, D), hidden_in, cotangent, gains)


def shards(
    n_dp,
    hidden_in,
    cotangent,
    owners,
    masters,
    firsts,
    seconds,
    width_gains,
    width_first,
    width_second,
    hidden_gains,
    hidden_first,
    hidden_second,
):
    tokens = hidden_in.shape[0]
    narrow = hidden_in.shape[1]
    slot_count = masters.shape[1]
    block_rows = masters.shape[2]
    blocks = owners.shape[0]
    hidden_local = hidden_gains.shape[1]
    dp_index = lax.axis_index("dp")
    mp_index = lax.axis_index("mp")
    own_tokens = tokens // (D // narrow)

    block_order = jnp.arange(blocks)
    same_owner = owners[:, None] == owners[None, :]
    slot_rank = jnp.sum(
        jnp.logical_and(same_owner, block_order[None, :] < block_order[:, None]).astype(jnp.int32),
        axis=1,
    )
    owned_mask = owners == dp_index
    in_use = jnp.arange(slot_count) < jnp.sum(owned_mask.astype(jnp.int32))
    slot_block = jnp.sum(
        jnp.where(
            jnp.logical_and(owned_mask[None, :], slot_rank[None, :] == jnp.arange(slot_count)[:, None]),
            block_order[None, :],
            0,
        ),
        axis=1,
    )

    size = D // narrow
    all_slots, x_all, cot_all, gains, cosine, sine = spread(
        masters[0].astype(bf16), hidden_in, cotangent, width_gains, n_dp, size, 6
    )
    weights = collect(
        owners * slot_count + slot_rank, all_slots.reshape(n_dp * slot_count, block_rows, D)
    ).reshape(blocks * block_rows, D)
    x_own = lax.dynamic_slice_in_dim(x_all, mp_index * own_tokens, own_tokens, 1)
    x_own = x_own.transpose(1, 0, 2).reshape(own_tokens, D).astype(f32)

    gain_qk = width_gains[0:1]

    operand, queries, keys, values, q_turned, k_turned = project(x_all, weights, gain_qk, cosine, sine)
    start_unit, start_inv = normalize(x_own)
    attended, mixed = attend(queries, keys, values)

    attn_branch, middle, middle_low = attention_sum(
        attended, weights, start_unit, gains, 3 * narrow, size, STEPS, 1
    )
    out_rows, middle_rows, up_raw, gate_raw, d_mlp, d_middle, g_rate_mlp = mlp(
        middle_low, weights, hidden_gains, middle, cot_all, gains, size, STEPS, 2
    )
    d_attn, d_start, g_rate_attn, g_scales, g_wide, g_down = mlp_back(
        d_mlp, weights, hidden_gains, up_raw, gate_raw, middle_rows, d_middle, start_unit, attn_branch, gains,
        size, STEPS, 3,
    )
    d_attn, g_wide = lax.optimization_barrier((d_attn, g_wide))
    wide_grads = lax.psum(g_wide.reshape(-1, block_rows, D), "dp")
    d_attended, attn_grad_rows = gather_project(d_attn, weights, narrow, 3 * narrow, size, STEPS, 4, "attention_gather")
    d_attended, out_rows = lax.optimization_barrier((d_attended, out_rows))
    hidden_out = lax.all_to_all(out_rows, "mp", split_axis=1, concat_axis=0, tiled=True)
    d_queries, d_keys, d_values = attend_back(queries, keys, values, mixed, d_attended)
    d_queries, hidden_out = lax.optimization_barrier((d_queries, hidden_out))
    grads_qkv, g_qk = project_back(
        d_queries, d_keys, d_values, q_turned, k_turned, gain_qk, cosine, sine
    )
    grad_in, g_attn = start_sum(
        grads_qkv, weights, d_start, start_unit, start_inv, operand, attended, attn_grad_rows, size, STEPS, 5
    )
    grad_in = grad_in.reshape(tokens, narrow).astype(f32)
    small = jnp.zeros((8, hidden_local), f32)
    small = small.at[0:1, :narrow].set(g_qk).at[1:3, :].set(g_scales)
    attn_grads, down_grads, small = tail_sum(g_attn, g_down, jnp.concatenate([g_rate_attn, g_rate_mlp], axis=0), small, n_dp, size, 7)
    width_total = jnp.concatenate([small[0:1, :narrow], small[3:5, :narrow]], axis=0)
    hidden_total = small[1:3, :]
    index = jnp.stack([slot_block, in_use.astype(jnp.int32)], axis=1)
    masters_new, firsts_new, seconds_new, weight_grads = [
        part[None]
        for part in optimizer(index, attn_grads, wide_grads, down_grads, masters[0], firsts[0], seconds[0])
    ]
    width_new, width_first_new, width_second_new = adam_update(
        width_gains, width_total, width_first, width_second, 0.0, GAIN_RATE
    )
    hidden_new, hidden_first_new, hidden_second_new = adam_update(
        hidden_gains, hidden_total, hidden_first, hidden_second, 0.0, GAIN_RATE
    )
    return (
        hidden_out,
        grad_in,
        masters_new,
        firsts_new,
        seconds_new,
        weight_grads,
        width_new,
        width_total,
        width_first_new,
        width_second_new,
        hidden_new,
        hidden_total,
        hidden_first_new,
        hidden_second_new,
    )


def solution(mesh):
    in_specs = (
        P("dp", "mp"),
        P("dp", "mp"),
        P(),
        P("mp", "dp", None, None),
        P("mp", "dp", None, None),
        P("mp", "dp", None, None),
        P(None, "mp"),
        P(None, "mp"),
        P(None, "mp"),
        P(None, "mp"),
        P(None, "mp"),
        P(None, "mp"),
    )
    out_specs = (
        P("dp", "mp"),
        P("dp", "mp"),
        P("mp", "dp", None, None),
        P("mp", "dp", None, None),
        P("mp", "dp", None, None),
        P("mp", "dp", None, None),
        P(None, "mp"),
        P(None, "mp"),
        P(None, "mp"),
        P(None, "mp"),
        P(None, "mp"),
        P(None, "mp"),
        P(None, "mp"),
        P(None, "mp"),
    )
    return jax.shard_map(functools.partial(shards, mesh.shape["dp"]), mesh=mesh, in_specs=in_specs, out_specs=out_specs, check_vma=False)
```

```python
import functools
import math

import jax
import jax.numpy as jnp
from jax import lax
from jax.experimental import pallas as pl
from jax.experimental.pallas import tpu as pltpu
from jax.sharding import PartitionSpec as P

D = 1024
HD = 64
STEP = 7
LANES = 128
STEPS = 4
MLP_STEPS = 2
LATE_PARTS = 2

EPSILON = 1e-06
ADAM_EPSILON = 1e-08
BETA_FIRST = 0.9
BETA_SECOND = 0.95
LEARN_RATE = 0.05
GAIN_RATE = 0.6
WEIGHT_DECAY = 0.1
SCORE_SCALE = float(HD) ** 0.5

f32 = jnp.float32
bf16 = jnp.bfloat16


def nn(left, right):
    return jnp.dot(left, right, preferred_element_type=f32)


def nt(left, right):
    return lax.dot_general(left, right, (((1,), (1,)), ((), ())), preferred_element_type=f32)


def tn(left, right):
    return lax.dot_general(left, right, (((0,), (0,)), ((), ())), preferred_element_type=f32)


def normalize(vector):
    inverse = lax.rsqrt(jnp.sum(vector * vector, axis=-1, keepdims=True) / D + EPSILON)
    return (vector * inverse, inverse)


def normalize_back(unit_rows, inverse, upstream):
    return inverse * (upstream - unit_rows * (jnp.sum(unit_rows * upstream, axis=-1, keepdims=True) / D))


def blend_branch(base_rows, branch, branch_rate):
    branch_unit, branch_inv = normalize(branch)
    mixed_unit, mixed_inv = normalize(base_rows + branch_rate * (branch_unit - base_rows))
    return (branch_unit, branch_inv, mixed_unit, mixed_inv)


def blend_back(base_rows, branch_unit, branch_inv, mixed_unit, mixed_inv, branch_rate, upstream):
    d_mixed = normalize_back(mixed_unit, mixed_inv, upstream)
    d_branch = normalize_back(branch_unit, branch_inv, branch_rate * d_mixed)
    return (
        (1.0 - branch_rate) * d_mixed,
        d_branch,
        jnp.sum(d_mixed * (branch_unit - base_rows), axis=0),
    )


def adam_update(params, gradient, first_moment, second_moment, decay_rate, step_rate):
    first_new = BETA_FIRST * first_moment + (1.0 - BETA_FIRST) * gradient
    second_new = BETA_SECOND * second_moment + (1.0 - BETA_SECOND) * gradient * gradient
    corrected = (
        first_new
        / (1.0 - BETA_FIRST**STEP)
        / (jnp.sqrt(second_new / (1.0 - BETA_SECOND**STEP)) + ADAM_EPSILON)
    )
    return (params - step_rate * (corrected + decay_rate * params), first_new, second_new)


def swap_halves(pair, lane):
    return jnp.where(
        lane % HD < HD // 2, pltpu.roll(pair, LANES - HD // 2, 1), pltpu.roll(pair, HD // 2, 1)
    )


def head_sums(values):
    width = values.shape[1]
    row = lax.broadcasted_iota(jnp.int32, (width, width), 0) // HD
    column = lax.broadcasted_iota(jnp.int32, (width, width), 1) // HD
    same = jnp.where(row == column, 1.0, 0.0).astype(bf16)
    high = values.astype(bf16)
    rest = values - high.astype(f32)
    middle = rest.astype(bf16)
    low = (rest - middle.astype(f32)).astype(bf16)
    return nn(high, same) + nn(middle, same) + nn(low, same)


def project_kernel(
    narrow, x_ref, w_ref, gain_ref, cos_ref, sin_ref, op_ref, q_ref, k_ref, v_ref, qr_ref, kr_ref
):
    rows = x_ref.shape[1]
    x = jnp.concatenate([x_ref[d] for d in range(x_ref.shape[0])], axis=1).astype(f32)
    operand = (x * lax.rsqrt(jnp.sum(x * x, axis=1, keepdims=True) / D + EPSILON)).astype(bf16)
    op_ref[...] = operand
    lane = lax.broadcasted_iota(jnp.int32, (rows, LANES), 1)
    cosine, sine = cos_ref[...], sin_ref[...]
    raw = nt(operand, w_ref[...])
    pairs = range(narrow // LANES)
    for which in range(2):
        out_ref, rot_ref = ((q_ref, qr_ref), (k_ref, kr_ref))[which]
        fill = (0.0, 1.0)[which]
        turned = []
        for pair in pairs:
            here = raw[:, which * narrow + pair * LANES : which * narrow + (pair + 1) * LANES]
            turned.append(here * cosine + swap_halves(here, lane) * sine)
        turned = jnp.concatenate(turned, axis=1)
        rot_ref[...] = turned
        gained = gain_ref[0:1, :] * (turned * lax.rsqrt(head_sums(turned * turned) + EPSILON))
        gained = gained.astype(bf16).astype(f32)
        if which == 0:
            gained = gained * SCORE_SCALE
        for pair in pairs:
            here = gained[:, pair * LANES : (pair + 1) * LANES]
            out_ref[2 * pair] = jnp.where(lane < HD, here, fill).astype(bf16)
            out_ref[2 * pair + 1] = jnp.where(lane < HD, pltpu.roll(here, HD, 1), fill).astype(bf16)
    for pair in range(narrow // LANES):
        here = raw[:, 2 * narrow + pair * LANES : 2 * narrow + (pair + 1) * LANES]
        v_ref[2 * pair] = jnp.where(lane < HD, here, 1.0).astype(bf16)
        v_ref[2 * pair + 1] = jnp.where(lane < HD, pltpu.roll(here, HD, 1), 1.0).astype(bf16)


def project(x_all, weights, gain, cosine, sine):
    size, tokens, narrow = x_all.shape
    heads = narrow // HD
    rows = min(512, tokens)
    head_spec = pl.BlockSpec((heads, rows, LANES), lambda i: (0, i, 0))
    row_spec = lambda width: pl.BlockSpec((rows, width), lambda i: (i, 0))
    whole = lambda a: pl.BlockSpec(a.shape, lambda i: (0, 0))
    return pl.pallas_call(
        functools.partial(project_kernel, narrow),
        grid=(tokens // rows,),
        in_specs=[pl.BlockSpec((size, rows, narrow), lambda i: (0, i, 0)), pl.BlockSpec((3 * narrow, D), lambda i: (0, 0)), whole(gain), row_spec(LANES), row_spec(LANES)],
        out_specs=[row_spec(D), head_spec, head_spec, head_spec, row_spec(narrow), row_spec(narrow)],
        out_shape=[jax.ShapeDtypeStruct((tokens, D), bf16)]
        + [jax.ShapeDtypeStruct((heads, tokens, LANES), bf16)] * 3
        + [jax.ShapeDtypeStruct((tokens, narrow), f32)] * 2,
        cost_estimate=pl.CostEstimate(
            flops=2 * tokens * D * 3 * narrow, bytes_accessed=tokens * D * 8, transcendentals=0
        ),
        name="project",
    )(x_all, weights, gain, cosine, sine)


def attend_kernel(block, q_ref, k_ref, v_ref, att_ref, o_ref):
    i = pl.program_id(1)
    lane = lax.broadcasted_iota(jnp.int32, (block, LANES), 1)
    queries = [q_ref[h] for h in range(2)]

    def step(j, sums, diagonal):
        rows = pl.ds(pl.multiple_of(j * block, block), block)
        new = []
        for h in range(2):
            weight = jnp.exp(nt(queries[h], k_ref[h, rows, :]))
            if diagonal:
                row = lax.broadcasted_iota(jnp.int32, weight.shape, 0)
                column = lax.broadcasted_iota(jnp.int32, weight.shape, 1)
                weight = jnp.where(row >= column, weight, 0.0)
            new.append(sums[h] + nn(weight.astype(bf16), v_ref[h, rows, :]))
        return tuple(new)

    zero = jnp.zeros((block, LANES), f32)
    sums = lax.fori_loop(0, i, lambda j, s: step(j, s, False), (zero, zero))
    sums = step(i, sums, True)
    mixed = []
    for h in range(2):
        total = pltpu.roll(sums[h], HD, 1)
        o_ref[h] = jnp.where(lane < HD, sums[h] / total, jnp.log(sums[h]))
        mixed.append(o_ref[h])
    att_ref[...] = jnp.where(lane < HD, mixed[0], pltpu.roll(mixed[1], HD, 1)).astype(bf16)


def attend(queries, keys, values):
    heads, tokens, _ = queries.shape
    block = min(512, tokens)
    part = pl.BlockSpec((2, block, LANES), lambda p, i: (p, i, 0))
    whole = pl.BlockSpec((2, tokens, LANES), lambda p, i: (p, 0, 0))
    return pl.pallas_call(
        functools.partial(attend_kernel, block),
        grid=(heads // 2, tokens // block),
        in_specs=[part, whole, whole],
        out_specs=[pl.BlockSpec((block, LANES), lambda p, i: (i, p)), part],
        out_shape=[
            jax.ShapeDtypeStruct((tokens, heads * HD), bf16),
            jax.ShapeDtypeStruct((heads, tokens, LANES), f32),
        ],
        cost_estimate=pl.CostEstimate(
            flops=heads * tokens * tokens * LANES * 4,
            bytes_accessed=heads * tokens * LANES * 10,
            transcendentals=heads * tokens * tokens // 2,
        ),
        name="attend",
    )(queries, keys, values)


def with_parts(lane, base, value):
    high = value.astype(bf16).astype(f32)
    rest = value - high
    middle = rest.astype(bf16).astype(f32)
    low = rest - middle
    tail = jnp.where(lane == HD, high, jnp.where(lane == HD + 1, middle, jnp.where(lane == HD + 2, low, 0.0)))
    return jnp.where(lane < HD, base, tail).astype(bf16)


def attend_back_kernel(
    block, q_ref, k_ref, v_ref, o_ref, do_ref, dq_ref, dk_ref, dv_ref, dk_sum, dv_sum
):
    i = pl.program_id(1)
    count = pl.num_programs(1)
    lane = lax.broadcasted_iota(jnp.int32, (block, LANES), 1)

    @pl.when(i == 0)
    def _():
        dk_sum[...] = jnp.zeros_like(dk_sum)
        dv_sum[...] = jnp.zeros_like(dv_sum)

    d_pair = do_ref[...].astype(f32)
    d_heads = [d_pair, pltpu.roll(d_pair, HD, 1)]
    queries, upstream = [], []
    for h in range(2):
        mixed = o_ref[h]
        delta = jnp.sum(jnp.where(lane < HD, mixed * d_heads[h], 0.0), axis=1, keepdims=True)
        queries.append(with_parts(lane, q_ref[h].astype(f32), -mixed))
        upstream.append(with_parts(lane, d_heads[h], -jnp.broadcast_to(delta, (block, LANES))))

    def step(j, sums, diagonal):
        rows = pl.ds(pl.multiple_of(j * block, block), block)
        new = []
        for h in range(2):
            keys = k_ref[h, rows, :]
            probs = jnp.exp(nt(keys, queries[h]))
            if diagonal:
                row = lax.broadcasted_iota(jnp.int32, probs.shape, 0)
                column = lax.broadcasted_iota(jnp.int32, probs.shape, 1)
                probs = jnp.where(column >= row, probs, 0.0)
            d_scores = (probs * nt(v_ref[h, rows, :], upstream[h])).astype(bf16)
            dv_sum[h, rows, :] += nn(probs.astype(bf16), upstream[h])
            dk_sum[h, rows, :] += nn(d_scores, queries[h])
            new.append(sums[h] + tn(d_scores, keys))
        return tuple(new)

    zero = jnp.zeros((block, LANES), f32)
    sums = lax.fori_loop(0, i, lambda j, s: step(j, s, False), (zero, zero))
    sums = step(i, sums, True)
    dq_ref[...] = jnp.where(lane < HD, sums[0], pltpu.roll(sums[1], HD, 1)) * SCORE_SCALE

    @pl.when(i == count - 1)
    def _():
        def put(j, carry):
            rows = pl.ds(pl.multiple_of(j * block, block), block)
            dk_ref[rows, :] = jnp.where(lane < HD, dk_sum[0, rows, :], pltpu.roll(dk_sum[1, rows, :], HD, 1))
            dv_ref[rows, :] = jnp.where(lane < HD, dv_sum[0, rows, :], pltpu.roll(dv_sum[1, rows, :], HD, 1))
            return carry

        lax.fori_loop(0, count, put, 0)


def attend_back(queries, keys, values, mixed, d_attended):
    heads, tokens, _ = queries.shape
    block = min(512, tokens)
    part = pl.BlockSpec((2, block, LANES), lambda p, i: (p, i, 0))
    whole = pl.BlockSpec((2, tokens, LANES), lambda p, i: (p, 0, 0))
    pair_part = pl.BlockSpec((block, LANES), lambda p, i: (i, p))
    pair_whole = pl.BlockSpec((tokens, LANES), lambda p, i: (0, p))
    return pl.pallas_call(
        functools.partial(attend_back_kernel, block),
        grid=(heads // 2, tokens // block),
        in_specs=[part, whole, whole, part, pair_part],
        out_specs=[pair_part, pair_whole, pair_whole],
        out_shape=[jax.ShapeDtypeStruct((tokens, heads * HD), f32)] * 3,
        scratch_shapes=[pltpu.VMEM((2, tokens, LANES), f32)] * 2,
        cost_estimate=pl.CostEstimate(
            flops=heads * tokens * tokens * LANES * 10,
            bytes_accessed=heads * tokens * LANES * 20,
            transcendentals=heads * tokens * tokens // 2,
        ),
        name="attend_back",
    )(queries, keys, values, mixed, d_attended)


def project_back_kernel(
    narrow, dq_ref, dk_ref, dv_ref, qr_ref, kr_ref, gain_ref, cos_ref, sin_ref, out_ref, gg_ref
):
    rows = dq_ref.shape[0]
    lane = lax.broadcasted_iota(jnp.int32, (rows, LANES), 1)
    cosine, sine = cos_ref[...], sin_ref[...]

    @pl.when(pl.program_id(0) == 0)
    def _():
        gg_ref[...] = jnp.zeros_like(gg_ref)

    for which in range(2):
        d_ref, rot_ref = ((dq_ref, qr_ref), (dk_ref, kr_ref))[which]
        turned = rot_ref[...]
        inverse = lax.rsqrt(head_sums(turned * turned) + EPSILON)
        unit_rows = turned * inverse
        upstream = d_ref[...]
        gg_ref[...] += jnp.sum(upstream * unit_rows, axis=0, keepdims=True)
        upstream = upstream * gain_ref[0:1, :]
        back = inverse * (upstream - unit_rows * head_sums(unit_rows * upstream))
        for pair in range(narrow // LANES):
            here = back[:, pair * LANES : (pair + 1) * LANES]
            here = here * cosine - swap_halves(here, lane) * sine
            out_ref[:, which * narrow + pair * LANES : which * narrow + (pair + 1) * LANES] = here.astype(bf16)
    out_ref[:, 2 * narrow : 3 * narrow] = dv_ref[...].astype(bf16)


def project_back(d_queries, d_keys, d_values, q_turned, k_turned, gain, cosine, sine):
    tokens, narrow = d_queries.shape
    rows = min(512, tokens)
    row_spec = lambda width: pl.BlockSpec((rows, width), lambda i: (i, 0))
    one = pl.BlockSpec((1, narrow), lambda i: (0, 0))
    whole = pl.BlockSpec(gain.shape, lambda i: (0, 0))
    return pl.pallas_call(
        functools.partial(project_back_kernel, narrow),
        grid=(tokens // rows,),
        in_specs=[row_spec(narrow)] * 5 + [whole, row_spec(LANES), row_spec(LANES)],
        out_specs=[row_spec(3 * narrow), one],
        out_shape=[
            jax.ShapeDtypeStruct((tokens, 3 * narrow), bf16),
            jax.ShapeDtypeStruct((1, narrow), f32),
        ],
        cost_estimate=pl.CostEstimate(
            flops=tokens * narrow * 60, bytes_accessed=tokens * narrow * 26, transcendentals=0
        ),
        name="project_back",
    )(d_queries, d_keys, d_values, q_turned, k_turned, gain, cosine, sine)


MESH = pl.DeviceIdType.MESH


class Group:
    def __init__(self, size, steps, tokens):
        self.size, self.steps = size, steps
        self.chips = size // 2
        self.own = tokens // size
        self.rows = self.own // steps
        self.dp, self.me = lax.axis_index("dp"), lax.axis_index("mp")
        self.chip, self.core = self.me // 2, lax.rem(self.me, 2)
        self.partner = self.me + 1 - 2 * self.core

    def other(self, k, core):
        return 2 * lax.rem(self.chip + k, self.chips) + core

    def slot(self, device):
        k = lax.rem(device // 2 - self.chip + self.chips, self.chips)
        return jnp.where(k == 0, 0, 2 * k - 1 + (lax.rem(device, 2) != self.core).astype(jnp.int32))

    def piece(self, ref, index, step):
        return ref.at[index, pl.ds(pl.multiple_of(step * self.rows, self.rows), self.rows), :]

    def copy(self, source, target, send, receive, device):
        return pltpu.make_async_remote_copy(
            src_ref=source,
            dst_ref=target,
            send_sem=send,
            recv_sem=receive,
            device_id=(self.dp, device),
            device_id_type=MESH,
        )

    def meet(self, everyone=False):
        barrier = pltpu.get_barrier_semaphore()
        devices = [self.partner] + [self.other(k, self.core) for k in range(1, self.chips)]
        if everyone:
            devices = [lax.rem(self.me + j, self.size) for j in range(1, self.size)]
        for device in devices:
            pl.semaphore_signal(barrier, inc=1, device_id=(self.dp, device), device_id_type=MESH)
        pl.semaphore_wait(barrier, len(devices))

    def place(self, i, remote_first=False):
        size, steps = self.size, self.steps
        others = steps * (size - 1)
        if remote_first:
            is_own = i >= others
            j = jnp.where(is_own, 0, i)
            s = jnp.where(is_own, i - others, j // (size - 1))
            r = lax.rem(lax.rem(j, size - 1) + 1, size - 1)
        else:
            is_own = i < steps
            j = jnp.where(is_own, 0, i - steps)
            s = jnp.where(is_own, i, j // (size - 1))
            r = lax.rem(j, size - 1)
        other = jnp.logical_not(is_own)
        is_partner = jnp.logical_and(other, r == 0)
        remote = jnp.logical_and(other, r > 0)
        is_first = jnp.logical_and(remote, lax.rem(r, 2) == 1)
        is_second = jnp.logical_and(remote, lax.rem(r, 2) == 0)
        k = jnp.where(remote, (r + 1) // 2, 0)
        core = jnp.where(jnp.logical_or(is_own, is_first), self.core, 1 - self.core)
        return self.other(k, core), s, k, is_own, is_partner, is_first, is_second

    def run(self, compute, gather=None, settle=None, remote_first=False, after=None, ready=(), between=None):
        steps, chips, size = self.steps, self.chips, self.size

        if gather:
            own_ref, all_ref, g_send, g_recv = gather

            def own_piece(s):
                return own_ref.at[pl.ds(pl.multiple_of(s * self.rows, self.rows), self.rows), :]

            def start_own(s, carry):
                for k in range(1, chips):
                    self.copy(own_piece(s), self.piece(all_ref, self.me, s), g_send.at[k, s], g_recv.at[self.me, s], self.other(k, self.core)).start()
                self.copy(own_piece(s), self.piece(all_ref, self.me, s), g_send.at[0, s], g_recv.at[self.me, s], self.partner).start()
                return carry

            lax.fori_loop(0, steps, start_own, 0)
            all_ref[self.me] = own_ref[...]

            def got(device, s):
                here = self.piece(all_ref, device, s)
                self.copy(here, here, g_send.at[0, s], g_recv.at[device, s], self.partner).wait_recv()

            def forward(k, s):
                device = self.other(k, self.core)
                here = self.piece(all_ref, device, s)
                return self.copy(here, here, g_send.at[chips + k - 1, s], g_recv.at[device, s], self.partner)

        if settle:
            out_ref, kept, to_partner, from_partner, to_chip, from_chip, p_send, p_recv, x_send, x_recv = settle

            def to_partner_copy(k, s):
                return self.copy(self.piece(to_partner, k, s), self.piece(from_partner, k, s), p_send.at[k, s], p_recv.at[k, s], self.partner)

            def to_chip_copy(k, s):
                return self.copy(self.piece(to_chip, k - 1, s), self.piece(from_chip, k - 1, s), x_send.at[k - 1, s], x_recv.at[k - 1, s], self.other(k, self.core))

        for copy in ready:
            copy.wait()

        def item(i, carry):
            device, s, k, is_own, is_partner, is_first, is_second = self.place(i, remote_first)
            if gather:

                @pl.when(jnp.logical_not(is_own))
                def _():
                    got(device, s)

                @pl.when(is_first)
                def _():
                    forward(k, s).start()

            term = compute(device, s, i)
            if between:
                between(device, jnp.logical_or(i == steps - 1, jnp.logical_and(is_partner, s == steps - 1)))
            if settle:
                here = pl.ds(pl.multiple_of(s * self.rows, self.rows), self.rows)

                @pl.when(is_own)
                def _():
                    out_ref[here, :] = term

                @pl.when(is_first)
                def _():
                    kept[...] = term

                @pl.when(jnp.logical_or(is_partner, is_second))
                def _():
                    to_partner[k, here, :] = term.astype(bf16)
                    to_partner_copy(k, s).start()

                @pl.when(is_second)
                def _():
                    to_partner_copy(k, s).wait_recv()
                    to_chip[k - 1, here, :] = (kept[...] + from_partner[k, here, :].astype(f32)).astype(bf16)
                    to_chip_copy(k, s).start()

            return carry

        lax.fori_loop(0, size * steps, item, 0)

        def end(s, carry):
            if settle:
                here = pl.ds(pl.multiple_of(s * self.rows, self.rows), self.rows)
                to_partner_copy(0, s).wait_recv()
                total = out_ref[here, :] + from_partner[0, here, :].astype(f32)
                for k in range(1, chips):
                    to_chip_copy(k, s).wait_recv()
                    total = total + from_chip[k - 1, here, :].astype(f32)
                out_ref[here, :] = total
                if after:
                    after(s)
                for k in range(chips):
                    to_partner_copy(k, s).wait_send()
                for k in range(1, chips):
                    to_chip_copy(k, s).wait_send()
            if gather:
                for k in range(2 * chips - 1):
                    self.copy(own_piece(s), own_piece(s), g_send.at[k, s], g_recv.at[0, s], self.partner).wait_send()
            return carry

        self.end = lambda first=0, last=steps: lax.fori_loop(first, last, end, 0)


def settle_scratch(size, steps, tokens):
    own, chips = tokens // size, size // 2
    return [
        pltpu.VMEM((own // steps, D), f32),
        pltpu.VMEM((chips, own, D), bf16),
        pltpu.VMEM((chips, own, D), bf16),
        pltpu.VMEM((chips - 1, own, D), bf16),
        pltpu.VMEM((chips - 1, own, D), bf16),
        pltpu.SemaphoreType.DMA((chips, steps)),
        pltpu.SemaphoreType.DMA((chips, steps)),
        pltpu.SemaphoreType.DMA((chips - 1, steps)),
        pltpu.SemaphoreType.DMA((chips - 1, steps)),
    ]


def gather_sems(size, steps):
    return [pltpu.SemaphoreType.DMA((size - 1, steps)), pltpu.SemaphoreType.DMA((size, steps))]


VMEM_WHOLE = pl.BlockSpec(memory_space=pltpu.VMEM)
ANYWHERE = pl.BlockSpec(memory_space=pl.ANY)
GRANT = 67043328


def weight_scratch(rows, count=1):
    return [pltpu.VMEM((rows, D), bf16)] * count + [pltpu.SemaphoreType.DMA((count,))]


def weight_copies(weights, buffers, sem, first):
    copies = []
    for i, buffer in enumerate(buffers):
        copies.append(pltpu.make_async_copy(weights.at[pl.ds(first, buffer.shape[0]), :], buffer, sem.at[i]))
        first += buffer.shape[0]
    return copies


def remote_params(collective_id):
    return pltpu.CompilerParams(
        collective_id=collective_id, has_side_effects=True, vmem_limit_bytes=GRANT
    )


def attention_sum_kernel(
    size, steps, first_row, rows_ref, w_hbm, start_ref, rates_ref,
    out_ref, middle_ref, low_ref, w_ref, w_sem, *scratch
):
    tokens = rows_ref.shape[0]
    group = Group(size, steps, tokens)
    (copy,) = weight_copies(w_hbm, [w_ref], w_sem, first_row)
    copy.start()
    group.meet()
    copy.wait()

    def compute(device, s, i):
        first = pl.multiple_of(device * group.own + s * group.rows, group.rows)
        return nn(rows_ref[pl.ds(first, group.rows), :], w_ref[...])

    def after(s):
        here = pl.ds(pl.multiple_of(s * group.rows, group.rows), group.rows)
        middle = blend_branch(start_ref[here, :], out_ref[here, :], rates_ref[1:2, :])[2]
        middle_ref[here, :] = middle
        low_ref[here, :] = middle.astype(bf16)

    group.run(compute, settle=(out_ref, *scratch), remote_first=True, after=after)
    group.end()


def attention_sum(rows, weights, start_unit, rates, first_row, size, steps, collective_id):
    tokens, depth = rows.shape
    own = jax.ShapeDtypeStruct((tokens // size, D), f32)
    return pl.pallas_call(
        functools.partial(attention_sum_kernel, size, steps, first_row),
        out_shape=[own, own, jax.ShapeDtypeStruct(own.shape, bf16)],
        in_specs=[VMEM_WHOLE, ANYWHERE, VMEM_WHOLE, VMEM_WHOLE],
        out_specs=[VMEM_WHOLE] * 3,
        scratch_shapes=weight_scratch(depth) + settle_scratch(size, steps, tokens),
        compiler_params=remote_params(collective_id),
        cost_estimate=pl.CostEstimate(flops=2 * tokens * depth * D, bytes_accessed=tokens * D * 8, transcendentals=0),
        name="attention_sum",
    )(rows, weights, start_unit, rates)


def mlp_kernel(
    size, steps, own_ref, w_hbm, scale_ref, middle_ref, cot_ref, rates_ref,
    out_ref, rows_ref, ur_hbm, gr_hbm, d_mlp_ref, d_middle_ref, g_rate_ref, branch_ref,
    up_ref, gate_ref, down_ref, w_sem, u_buf, g_buf, b_sem, *scratch
):
    tokens = own_ref.shape[0] * size
    group = Group(size, steps, tokens)
    copies = weight_copies(w_hbm, [up_ref, gate_ref, down_ref], w_sem, scale_ref.shape[1])
    for c in copies:
        c.start()
    group.meet()

    def save(i, device, s):
        slot = lax.rem(i, 2)
        rows = pl.ds(pl.multiple_of(device * group.own + s * group.rows, group.rows), group.rows)
        return (
            pltpu.make_async_copy(u_buf.at[slot], ur_hbm.at[rows, :], b_sem.at[0, slot]),
            pltpu.make_async_copy(g_buf.at[slot], gr_hbm.at[rows, :], b_sem.at[1, slot]),
        )

    def compute(device, s, i):
        slot = lax.rem(i, 2)

        @pl.when(i >= 2)
        def _():
            for c in save(i, device, s):
                c.wait()

        rows = group.piece(rows_ref, device, s)[...]
        up_raw = nt(rows, up_ref[...])
        gate_raw = nt(rows, gate_ref[...])
        u_buf[slot] = up_raw
        g_buf[slot] = gate_raw
        for c in save(i, device, s):
            c.start()
        gate_val = scale_ref[1:2, :] * gate_raw
        product = (scale_ref[0:1, :] * up_raw * (gate_val * jax.nn.sigmoid(gate_val))).astype(bf16)
        return nn(product, down_ref[...])

    g_rate_ref[...] = jnp.zeros_like(g_rate_ref)

    def after(s):
        here = pl.ds(pl.multiple_of(s * group.rows, group.rows), group.rows)
        middle, rate = middle_ref[here, :], rates_ref[2:3, :]
        branch_unit, branch_inv, mixed, mixed_inv = blend_branch(middle, branch_ref[here, :], rate)
        for d in range(size):
            out_ref[d, here, :] = mixed[:, d * (D // size) : (d + 1) * (D // size)]
        upstream = jnp.concatenate([cot_ref[d, here, :] for d in range(size)], axis=1).astype(f32)
        d_middle, d_branch, g_rate = blend_back(
            middle, branch_unit, branch_inv, mixed, mixed_inv, rate, upstream
        )
        d_middle_ref[here, :] = d_middle
        d_mlp_ref[here, :] = d_branch.astype(bf16)
        g_rate_ref[...] += g_rate[None]

    group.run(
        compute, gather=(own_ref, rows_ref, scratch[0], scratch[1]), settle=(branch_ref, *scratch[2:]), ready=copies, after=after
    )
    for i in range(2):
        for c in save(i, 0, 0):
            c.wait()
    group.end()


def mlp(own, weights, scales, middle, cot_all, rates, size, steps, collective_id):
    hidden = scales.shape[1]
    tokens = own.shape[0] * size
    rows = own.shape[0] // steps
    return pl.pallas_call(
        functools.partial(mlp_kernel, size, steps),
        out_shape=[
            jax.ShapeDtypeStruct((size, own.shape[0], D // size), f32),
            jax.ShapeDtypeStruct((size, own.shape[0], D), bf16),
            jax.ShapeDtypeStruct((tokens, hidden), f32),
            jax.ShapeDtypeStruct((tokens, hidden), f32),
            jax.ShapeDtypeStruct((own.shape[0], D), bf16),
            jax.ShapeDtypeStruct((own.shape[0], D), f32),
            jax.ShapeDtypeStruct((1, D), f32),
        ],
        in_specs=[VMEM_WHOLE, ANYWHERE] + [VMEM_WHOLE] * 4,
        out_specs=[VMEM_WHOLE, VMEM_WHOLE, ANYWHERE, ANYWHERE] + [VMEM_WHOLE] * 3,
        scratch_shapes=[pltpu.VMEM((own.shape[0], D), f32)]
        + weight_scratch(hidden, 3)
        + [
            pltpu.VMEM((2, rows, hidden), f32),
            pltpu.VMEM((2, rows, hidden), f32),
            pltpu.SemaphoreType.DMA((2, 2)),
        ]
        + gather_sems(size, steps)
        + settle_scratch(size, steps, tokens),
        compiler_params=remote_params(collective_id),
        cost_estimate=pl.CostEstimate(flops=6 * tokens * hidden * D, bytes_accessed=tokens * D * 12, transcendentals=tokens * hidden),
        name="mlp",
    )(own, weights, scales, middle, cot_all, rates)


def mlp_back_kernel(
    size, steps, own_ref, w_hbm, scale_ref, ur_hbm, gr_hbm, middle_rows_ref, d_middle_hbm, start_hbm, branch_hbm, rates_ref,
    d_attn_ref, d_start_ref, g_rate_ref, gs_ref, wide_hbm, down_hbm,
    stage, stage_sem, late, late_sem,
    sum_ref, rows_ref, product_ref, d_ref, grads_sum,
    up_ref, gate_ref, down_ref, w_sem, u_buf, g_buf, b_sem, *scratch
):
    tokens = own_ref.shape[0] * size
    group = Group(size, steps, tokens)

    def load(i):
        device, s = group.place(i)[:2]
        slot = lax.rem(i, 2)
        rows = pl.ds(pl.multiple_of(device * group.own + s * group.rows, group.rows), group.rows)
        return (
            pltpu.make_async_copy(ur_hbm.at[rows, :], u_buf.at[slot], b_sem.at[0, slot]),
            pltpu.make_async_copy(gr_hbm.at[rows, :], g_buf.at[slot], b_sem.at[1, slot]),
        )

    copies = weight_copies(w_hbm, [up_ref, gate_ref, down_ref], w_sem, scale_ref.shape[1])
    for c in (*load(0), *copies):
        c.start()
    gs_ref[...] = jnp.zeros_like(gs_ref)
    g_rate_ref[...] = jnp.zeros_like(g_rate_ref)
    group.meet()
    hidden = scale_ref.shape[1]
    part = min(256, hidden)

    def weight_grads(device):
        rows = pl.ds(pl.multiple_of(group.slot(device) * group.own, group.own), group.own)

        def one(source, offset, other):
            def column(c, carry):
                first = pl.multiple_of(c * part, part)
                to = pl.ds(pl.multiple_of(offset + first, part), part)
                term = tn(source[rows, pl.ds(first, part)], other[device])
                grads_sum[to, :] += term
                return carry

            lax.fori_loop(0, source.shape[1] // part, column, 0)

        one(d_ref, 0, middle_rows_ref)
        one(product_ref, 2 * hidden, rows_ref)

    def clear(c, carry):
        grads_sum[pl.ds(pl.multiple_of(c * part, part), part), :] = jnp.zeros((part, D), f32)
        return carry

    lax.fori_loop(0, 3 * hidden // part, clear, 0)

    def between(device, done):
        @pl.when(done)
        def _():
            weight_grads(device)

    late_rows = late.shape[2]

    def late_copies(s):
        here = pl.ds(pl.multiple_of(s * late_rows, late_rows), late_rows)
        return [
            pltpu.make_async_copy(ref.at[here, :], late.at[lax.rem(s, 2), i], late_sem.at[lax.rem(s, 2), i])
            for i, ref in enumerate((start_hbm, branch_hbm, d_middle_hbm))
        ]

    for c in late_copies(0):
        c.start()

    def after_part(s, carry):
        here = pl.ds(pl.multiple_of(s * late_rows, late_rows), late_rows)
        for c in late_copies(s):
            c.wait()

        @pl.when(s + 1 < steps * LATE_PARTS)
        def _():
            for c in late_copies(s + 1):
                c.start()

        start, branch, d_middle = [late[lax.rem(s, 2), i] for i in range(3)]
        rate = rates_ref[1:2, :]
        branch_unit, branch_inv, middle, middle_inv = blend_branch(start, branch, rate)
        d_start, d_branch, g_rate = blend_back(
            start, branch_unit, branch_inv, middle, middle_inv, rate, d_middle + sum_ref[here, :]
        )
        d_start_ref[here, :] = d_start
        d_attn_ref[here, :] = d_branch.astype(bf16)
        g_rate_ref[...] += g_rate[None]
        return carry

    def after(s):
        lax.fori_loop(s * LATE_PARTS, (s + 1) * LATE_PARTS, after_part, 0)

    def compute(device, s, i):
        slot = lax.rem(i, 2)

        @pl.when(i + 1 < size * steps)
        def _():
            for c in load(i + 1):
                c.start()

        rows = group.piece(rows_ref, device, s)[...]
        d_product = nt(rows, down_ref[...])
        for c in load(i):
            c.wait()
        first = pl.multiple_of(group.slot(device) * group.own + s * group.rows, group.rows)
        here = pl.ds(first, group.rows)
        up_raw, gate_raw = u_buf[slot], g_buf[slot]
        up_val = scale_ref[0:1, :] * up_raw
        gate_val = scale_ref[1:2, :] * gate_raw
        sigmoid = jax.nn.sigmoid(gate_val)
        activated = gate_val * sigmoid
        product_ref[here, :] = (up_val * activated).astype(bf16)
        d_up = d_product * activated
        d_gate = d_product * up_val * (sigmoid * (1.0 + gate_val * (1.0 - sigmoid)))
        gs_ref[0:1, :] += jnp.sum(d_up * up_raw, axis=0, keepdims=True)
        gs_ref[1:2, :] += jnp.sum(d_gate * gate_raw, axis=0, keepdims=True)
        d_up_raw = (d_up * scale_ref[0:1, :]).astype(bf16)
        d_gate_raw = (d_gate * scale_ref[1:2, :]).astype(bf16)
        d_ref[here, :hidden] = d_up_raw
        d_ref[here, hidden:] = d_gate_raw
        return nn(d_up_raw, up_ref[...]) + nn(d_gate_raw, gate_ref[...])

    group.run(
        compute, gather=(own_ref, rows_ref, scratch[0], scratch[1]), settle=(sum_ref, *scratch[2:]), ready=copies,
        after=after, between=between,
    )

    def rest(j, carry):
        weight_grads(group.other(1 + j // 2, lax.rem(j, 2)))
        return carry

    lax.fori_loop(0, size - 2, rest, 0)

    wide_parts = 2 * hidden // part

    def stage_copy(c, ref, first):
        here = pl.ds(pl.multiple_of((c - first) * part, part), part)
        return pltpu.make_async_copy(stage.at[lax.rem(c, 2)], ref.at[here, :], stage_sem.at[lax.rem(c, 2)])

    def put(c, carry):
        @pl.when(c >= 2)
        def _():
            stage_copy(lax.rem(c, 2), wide_hbm, 0).wait()

        stage[lax.rem(c, 2)] = grads_sum[pl.ds(pl.multiple_of(c * part, part), part), :].astype(bf16)

        @pl.when(c < wide_parts)
        def _():
            stage_copy(c, wide_hbm, 0).start()

        @pl.when(c >= wide_parts)
        def _():
            stage_copy(c, down_hbm, wide_parts).start()

        return carry

    parts = 3 * hidden // part
    lax.fori_loop(0, parts, put, 0)
    group.end()
    for c in range(2):
        stage_copy(c, wide_hbm, 0).wait()


def mlp_back(own, weights, scales, up_raw, gate_raw, middle_rows, d_middle, start_unit, branch, rates, size, steps, collective_id):
    tokens, hidden = up_raw.shape
    rows = own.shape[0] // steps
    return pl.pallas_call(
        functools.partial(mlp_back_kernel, size, steps),
        out_shape=[
            jax.ShapeDtypeStruct((own.shape[0], D), bf16),
            jax.ShapeDtypeStruct((own.shape[0], D), f32),
            jax.ShapeDtypeStruct((1, D), f32),
            jax.ShapeDtypeStruct((2, hidden), f32),
            jax.ShapeDtypeStruct((2 * hidden, D), bf16),
            jax.ShapeDtypeStruct((hidden, D), bf16),
        ],
        in_specs=[VMEM_WHOLE, ANYWHERE, VMEM_WHOLE, ANYWHERE, ANYWHERE, VMEM_WHOLE] + [ANYWHERE] * 3 + [VMEM_WHOLE],
        out_specs=[VMEM_WHOLE] * 4 + [ANYWHERE] * 2,
        scratch_shapes=[
            pltpu.VMEM((2, min(256, hidden), D), bf16),
            pltpu.SemaphoreType.DMA((2,)),
            pltpu.VMEM((2, 3, rows // LATE_PARTS, D), f32),
            pltpu.SemaphoreType.DMA((2, 3)),
            pltpu.VMEM((own.shape[0], D), f32),
            pltpu.VMEM((size, own.shape[0], D), bf16),
            pltpu.VMEM((tokens - own.shape[0], hidden), bf16),
            pltpu.VMEM((tokens - own.shape[0], 2 * hidden), bf16),
            pltpu.VMEM((3 * hidden, D), f32),
        ]
        + weight_scratch(hidden, 3)
        + [
            pltpu.VMEM((2, rows, hidden), f32),
            pltpu.VMEM((2, rows, hidden), f32),
            pltpu.SemaphoreType.DMA((2, 2)),
        ]
        + gather_sems(size, steps)
        + settle_scratch(size, steps, tokens),
        compiler_params=remote_params(collective_id),
        cost_estimate=pl.CostEstimate(flops=6 * tokens * hidden * D, bytes_accessed=tokens * D * 24, transcendentals=tokens * hidden),
        name="mlp_back",
    )(own, weights, scales, up_raw, gate_raw, middle_rows, d_middle, start_unit, branch, rates)


def gather_project_kernel(size, steps, first_row, own_ref, w_hbm, out_ref, rows_ref, w_ref, w_sem, *scratch):
    tokens = own_ref.shape[0] * size
    group = Group(size, steps, tokens)
    copies = weight_copies(w_hbm, [w_ref], w_sem, first_row)
    copies[0].start()
    group.meet()

    def compute(device, s, i):
        first = pl.multiple_of(device * group.own + s * group.rows, group.rows)
        out_ref[pl.ds(first, group.rows), :] = nt(group.piece(rows_ref, device, s)[...], w_ref[...]).astype(bf16)

    group.run(compute, gather=(own_ref, rows_ref, scratch[0], scratch[1]), ready=copies)
    group.end()


def gather_project(own, weights, width, first_row, size, steps, collective_id, name):
    tokens = own.shape[0] * size
    return pl.pallas_call(
        functools.partial(gather_project_kernel, size, steps, first_row),
        out_shape=[
            jax.ShapeDtypeStruct((tokens, width), bf16),
            jax.ShapeDtypeStruct((size, own.shape[0], D), bf16),
        ],
        in_specs=[VMEM_WHOLE, ANYWHERE],
        out_specs=[VMEM_WHOLE, VMEM_WHOLE],
        scratch_shapes=weight_scratch(width) + gather_sems(size, steps),
        compiler_params=remote_params(collective_id),
        cost_estimate=pl.CostEstimate(flops=2 * tokens * width * D, bytes_accessed=tokens * D * 4, transcendentals=0),
        name=name,
    )(own, weights)


def start_sum_kernel(
    size, steps, rows_ref, w_hbm, base_ref, unit_ref, inv_ref, operand_hbm, attended_hbm, d_attn_hbm,
    pieces, grads_ref, operand_ref, attended_ref, d_attn_ref, late_sem, w_ref, w_sem, total_ref, *scratch
):
    tokens = rows_ref.shape[0]
    narrow = pieces.shape[2]
    group = Group(size, steps, tokens)
    copies = weight_copies(w_hbm, [w_ref], w_sem, 0)
    copies[0].start()
    late = [
        pltpu.make_async_copy(source, target, late_sem.at[i])
        for i, (source, target) in enumerate(
            ((operand_hbm, operand_ref), (attended_hbm, attended_ref), (d_attn_hbm, d_attn_ref))
        )
    ]
    for copy in late:
        copy.start()
    group.meet()
    copies[0].wait()

    def compute(device, s, i):
        first = pl.multiple_of(device * group.own + s * group.rows, group.rows)
        return nn(rows_ref[pl.ds(first, group.rows), :], w_ref[...])

    def after(s):
        here = pl.ds(pl.multiple_of(s * group.rows, group.rows), group.rows)
        back = normalize_back(unit_ref[here, :], inv_ref[here, 0:1], base_ref[here, :] + total_ref[here, :])
        for device in range(size):
            pieces[device, here, :] = back[:, device * narrow : (device + 1) * narrow].astype(bf16)

    group.run(compute, settle=(total_ref, *scratch), remote_first=True, after=after)

    for copy in late:
        copy.wait()
    for c in range(3):
        here = slice(c * narrow, (c + 1) * narrow)
        grads_ref[here, :] = tn(rows_ref[:, here], operand_ref[...]).astype(bf16)
        group.end(c * steps // 4, (c + 1) * steps // 4)
    out_sum = jnp.zeros((narrow, D), f32)
    for d in range(size):
        out_sum += tn(attended_ref[d * group.own : (d + 1) * group.own, :], d_attn_ref[d])
    grads_ref[3 * narrow :, :] = out_sum.astype(bf16)
    group.end(3 * steps // 4, steps)


def start_sum(rows, weights, base, unit_rows, inverse, operand, attended, d_attn_rows, size, steps, collective_id):
    tokens, depth = rows.shape
    own, narrow = tokens // size, D // size
    return pl.pallas_call(
        functools.partial(start_sum_kernel, size, steps),
        out_shape=[jax.ShapeDtypeStruct((size, own, narrow), bf16), jax.ShapeDtypeStruct((4 * narrow, D), bf16)],
        in_specs=[VMEM_WHOLE, ANYWHERE] + [VMEM_WHOLE] * 3 + [ANYWHERE] * 3,
        out_specs=[VMEM_WHOLE] * 2,
        scratch_shapes=[
            pltpu.VMEM(operand.shape, bf16),
            pltpu.VMEM(attended.shape, bf16),
            pltpu.VMEM(d_attn_rows.shape, bf16),
            pltpu.SemaphoreType.DMA((3,)),
        ]
        + weight_scratch(depth)
        + [
            pltpu.VMEM((own, D), f32),
        ]
        + settle_scratch(size, steps, tokens),
        compiler_params=remote_params(collective_id),
        cost_estimate=pl.CostEstimate(flops=2 * tokens * depth * D, bytes_accessed=tokens * D * 8, transcendentals=0),
        name="start_sum",
    )(rows, weights, base, unit_rows, inverse, operand, attended, d_attn_rows)


def tail_plan(devices, rows):
    lines = min(4, devices)
    columns = devices // lines
    cuts = 2 if rows % (devices * 32) == 0 else 1
    return lines, columns, cuts, rows // (devices * cuts)


def tail_sum_kernel(
    devices, size, late_ref, early_ref, rates_ref, small_ref, hidden_ref, back_ref,
    late_out, early_out, small_out, hidden_out, back_out,
    y_land, y_sum, z_land, rate_parts, rate_land, pack, small_land,
    a_send, a_recv, b_send, b_recv, c_send, c_recv, d_send, d_recv, m_send, m_recv, s_send, s_recv, h_send, h_recv, g_send, g_recv
):
    dp, me = lax.axis_index("dp"), lax.axis_index("mp")
    lines, columns, cuts, rows = tail_plan(devices, late_ref.shape[0])
    a, b = dp // columns, lax.rem(dp, columns)
    span = lines * rows
    narrow = rate_parts.shape[2]
    chunks = [(early_ref, early_out, q) for q in range(cuts)] + [(late_ref, late_out, q) for q in range(cuts)]

    def remote(source, target, send, receive, device):
        return pltpu.make_async_remote_copy(
            src_ref=source, dst_ref=target, send_sem=send, recv_sem=receive, device_id=device, device_id_type=MESH
        )

    def peer(j):
        return lax.rem(dp + j, devices)

    def column(j):
        return lax.rem(b + j, columns)

    def line(j):
        return lax.rem(a + j, lines)

    barrier = pltpu.get_barrier_semaphore()

    def greet(j, carry):
        pl.semaphore_signal(barrier, inc=1, device_id=(peer(j), me), device_id_type=MESH)
        return carry

    lax.fori_loop(1, devices, greet, 0)
    for j in range(1, size):
        pl.semaphore_signal(barrier, inc=1, device_id=(dp, lax.rem(me + j, size)), device_id_type=MESH)
    pl.semaphore_wait(barrier, devices - 1 + size - 1)

    def part(ref, q, col):
        return ref.at[pl.ds(pl.multiple_of((q * columns + col) * span, span), span), :]

    def to_column(c, j):
        ref, _, q = chunks[c]
        return remote(part(ref, q, column(j)), y_land.at[c, b], a_send.at[c, j], a_recv.at[c, b], (a * columns + column(j), me))

    def from_column(c, j):
        here = y_land.at[c, column(j)]
        return remote(here, here, a_send.at[c, j], a_recv.at[c, column(j)], (a * columns + column(j), me))

    def to_line(c, j):
        there = pl.ds(pl.multiple_of(line(j) * rows, rows), rows)
        return remote(y_sum.at[c, there, :], z_land.at[c, a], b_send.at[c, j], b_recv.at[c, a], (line(j) * columns + b, me))

    def from_line(c, j):
        here = z_land.at[c, line(j)]
        return remote(here, here, b_send.at[c, j], b_recv.at[c, line(j)], (line(j) * columns + b, me))

    def sum_of(c, col, row):
        _, out, q = chunks[c]
        return out.at[(q * columns + col) * lines + row]

    def back_line(c, j):
        here = sum_of(c, b, a)
        return remote(here, here, c_send.at[c, j], c_recv.at[c, a], (line(j) * columns + b, me))

    def back_line_got(c, j):
        here = sum_of(c, b, line(j))
        return remote(here, here, c_send.at[c, j], c_recv.at[c, line(j)], (line(j) * columns + b, me))

    def back_column(c, i, j):
        here = sum_of(c, b, line(i))
        return remote(here, here, d_send.at[c, i, j], d_recv.at[c, line(i), b], (a * columns + column(j), me))

    def back_column_got(c, i, j):
        here = sum_of(c, column(j), line(i))
        return remote(here, here, d_send.at[c, i, j], d_recv.at[c, line(i), column(j)], (a * columns + column(j), me))

    def rate_copy(j):
        device = lax.rem(me + j, size)
        return remote(rate_parts.at[device], rate_land.at[me], m_send.at[j - 1], m_recv.at[me], (dp, device))

    for c in range(len(chunks)):
        for j in range(1, columns):
            to_column(c, j).start()
    for d in range(size):
        rate_parts[d, 0:2, :] = rates_ref[:, d * narrow : (d + 1) * narrow]
    for j in range(1, size):
        rate_copy(j).start()

    def deal(j):
        device = lax.rem(me + j, size)
        return [
            remote(source.at[device], target.at[me], send.at[j - 1], receive.at[me], (dp, device))
            for source, target, send, receive in ((hidden_ref, hidden_out, h_send, h_recv), (back_ref, back_out, g_send, g_recv))
        ]

    def dealt(j):
        device = lax.rem(me + j, size)
        return [
            remote(target.at[device], target.at[device], send.at[j - 1], receive.at[device], (dp, device))
            for target, send, receive in ((hidden_out, h_send, h_recv), (back_out, g_send, g_recv))
        ]

    for j in range(1, size):
        for copy in deal(j):
            copy.start()
    hidden_out[me] = hidden_ref[me]
    back_out[me] = back_ref[me]

    rates = rate_parts[me]
    for j in range(1, size):
        source = lax.rem(me + j, size)
        remote(rate_land.at[source], rate_land.at[source], m_send.at[j - 1], m_recv.at[source], (dp, source)).wait_recv()
        rates = rates + rate_land[source]
    pack[...] = small_ref[...]
    pack[3:5, :narrow] = rates[0:2, :]

    def small_copy(j):
        return remote(pack, small_land.at[dp], s_send.at[j - 1], s_recv.at[dp], (peer(j), me))

    def small_give(j, carry):
        small_copy(j).start()
        return carry

    lax.fori_loop(1, devices, small_give, 0)

    def settle_column(c):
        ref, _, q = chunks[c]
        for j in range(1, columns):
            from_column(c, j).wait_recv()

        def add(i, carry):
            here = pl.ds(pl.multiple_of(i * rows, rows), rows)
            own = pl.ds(pl.multiple_of((q * columns + b) * span + i * rows, rows), rows)
            total = ref[own, :].astype(f32)
            for j in range(1, columns):
                total = total + y_land[c, column(j), here, :].astype(f32)
            y_sum[c, here, :] = total.astype(bf16)
            return carry

        lax.fori_loop(0, lines, add, 0)
        for j in range(1, lines):
            to_line(c, j).start()

    def settle_line(c):
        for j in range(1, lines):
            from_line(c, j).wait_recv()
        total = y_sum[c, pl.ds(pl.multiple_of(a * rows, rows), rows), :].astype(f32)
        for j in range(1, lines):
            total = total + z_land[c, line(j)].astype(f32)
        sum_of(c, b, a)[...] = total.astype(bf16)
        for j in range(1, lines):
            back_line(c, j).start()
        for j in range(1, columns):
            back_column(c, 0, j).start()

    def pass_on(c):
        for i in range(1, lines):
            back_line_got(c, i).wait_recv()
            for j in range(1, columns):
                back_column(c, i, j).start()

    count = len(chunks)
    for step in range(count + 2):
        if step < count:
            settle_column(step)
        if 1 <= step <= count:
            settle_line(step - 1)
        if step >= 2:
            pass_on(step - 2)

    def small_take(j, total):
        source = peer(j)
        remote(small_land.at[source], small_land.at[source], s_send.at[j - 1], s_recv.at[source], (source, me)).wait_recv()
        return total + small_land[source]

    small_out[...] = lax.fori_loop(1, devices, small_take, pack[...])
    for c in range(count):
        for i in range(lines):
            for j in range(1, columns):
                back_column_got(c, i, j).wait_recv()
                back_column(c, i, j).wait_send()
        for j in range(1, lines):
            back_line(c, j).wait_send()
            to_line(c, j).wait_send()
        for j in range(1, columns):
            to_column(c, j).wait_send()

    def finish(j, carry):
        small_copy(j).wait_send()
        return carry

    lax.fori_loop(1, devices, finish, 0)
    for j in range(1, size):
        rate_copy(j).wait_send()
        for copy in dealt(j):
            copy.wait_recv()
        for copy in deal(j):
            copy.wait_send()


def tail_sum(late, early, rates, small, hidden, back, devices, size, collective_id):
    lines, columns, cuts, rows = tail_plan(devices, late.shape[0])
    narrow = D // size
    chunks = 2 * cuts
    dma = pltpu.SemaphoreType.DMA
    total = jax.ShapeDtypeStruct((late.shape[0] // rows, rows, D), bf16)
    return pl.pallas_call(
        functools.partial(tail_sum_kernel, devices, size),
        out_shape=[total, total] + [jax.ShapeDtypeStruct(x.shape, x.dtype) for x in (small, hidden, back)],
        in_specs=[VMEM_WHOLE] * 6,
        out_specs=[VMEM_WHOLE] * 5,
        scratch_shapes=[
            pltpu.VMEM((chunks, columns, lines * rows, D), bf16),
            pltpu.VMEM((chunks, lines * rows, D), bf16),
            pltpu.VMEM((chunks, lines, rows, D), bf16),
            pltpu.VMEM((size, 8, narrow), f32),
            pltpu.VMEM((size, 8, narrow), f32),
            pltpu.VMEM(small.shape, f32),
            pltpu.VMEM((devices, *small.shape), f32),
            dma((chunks, columns)), dma((chunks, columns)),
            dma((chunks, lines)), dma((chunks, lines)),
            dma((chunks, lines)), dma((chunks, lines)),
            dma((chunks, lines, columns)), dma((chunks, lines, columns)),
            dma((size - 1,)), dma((size,)),
            dma((devices - 1,)), dma((devices,)),
            dma((size - 1,)), dma((size,)),
            dma((size - 1,)), dma((size,)),
        ],
        compiler_params=remote_params(collective_id),
        cost_estimate=pl.CostEstimate(flops=0, bytes_accessed=late.shape[0] * D * 16, transcendentals=0),
        name="tail_sum",
    )(late, early, rates, small, hidden, back)


def optimizer_kernel(
    counts, index_ref, attn_ref, wide_ref, down_ref, m_ref, f_ref, s_ref, mo_ref, fo_ref, so_ref, go_ref
):
    group = m_ref.shape[0]
    for j in range(group):
        slot = pl.program_id(0) * group + j
        block, live = index_ref[slot, 0], index_ref[slot, 1]

        @pl.when(live == 0)
        def _():
            for ref in (mo_ref, fo_ref, so_ref, go_ref):
                ref[j] = jnp.zeros_like(m_ref[j])

        for ref, first, last in (
            (attn_ref, 0, counts[0]),
            (wide_ref, counts[0], counts[0] + counts[1]),
            (down_ref, counts[0] + counts[1], sum(counts)),
        ):

            @pl.when(jnp.logical_and(live == 1, jnp.logical_and(block >= first, block < last)))
            def _():
                gradient = ref[block - first].astype(f32)
                stepped, first_new, second_new = adam_update(
                    m_ref[j], gradient, f_ref[j], s_ref[j], WEIGHT_DECAY, LEARN_RATE
                )
                go_ref[j] = gradient
                fo_ref[j] = first_new
                so_ref[j] = second_new
                mo_ref[j] = stepped * lax.rsqrt(jnp.sum(stepped * stepped, axis=-1, keepdims=True) + EPSILON)


def optimizer(index, attn_grads, wide_grads, down_grads, masters, firsts, seconds):
    slots, height, _ = masters.shape
    group = math.gcd(slots, 4)
    grads = [g.reshape(-1, height, D) for g in (attn_grads, wide_grads, down_grads)]
    block = pl.BlockSpec((group, height, D), lambda i, ref: (i, 0, 0))
    return pl.pallas_call(
        functools.partial(optimizer_kernel, tuple(g.shape[0] for g in grads)),
        grid_spec=pltpu.PrefetchScalarGridSpec(
            num_scalar_prefetch=1,
            grid=(slots // group,),
            in_specs=[pl.BlockSpec(memory_space=pltpu.VMEM)] * 3 + [block] * 3,
            out_specs=[block] * 4,
        ),
        out_shape=[jax.ShapeDtypeStruct(masters.shape, f32)] * 4,
        compiler_params=pltpu.CompilerParams(vmem_limit_bytes=GRANT),
        cost_estimate=pl.CostEstimate(flops=20 * masters.size, bytes_accessed=30 * masters.size, transcendentals=0),
        name="optimizer",
    )(index, *grads, masters, firsts, seconds)


def collect_kernel(count, places_ref, slots_hbm, out_ref, sems):
    def copy(b):
        return pltpu.make_async_copy(slots_hbm.at[places_ref[b]], out_ref.at[b], sems.at[b])

    def start(b, carry):
        copy(b).start()
        return carry

    def wait(b, carry):
        copy(b).wait()
        return carry

    lax.fori_loop(0, count, start, 0)
    lax.fori_loop(0, count, wait, 0)


def collect(places, slots):
    count, shape = places.shape[0], slots.shape[1:]
    return pl.pallas_call(
        functools.partial(collect_kernel, count),
        grid_spec=pltpu.PrefetchScalarGridSpec(
            num_scalar_prefetch=1,
            grid=(1,),
            in_specs=[pl.BlockSpec(memory_space=pl.ANY)],
            out_specs=pl.BlockSpec(memory_space=pltpu.VMEM),
            scratch_shapes=[pltpu.SemaphoreType.DMA((count,))],
        ),
        out_shape=jax.ShapeDtypeStruct((count, *shape), bf16),
        compiler_params=pltpu.CompilerParams(vmem_limit_bytes=GRANT),
        cost_estimate=pl.CostEstimate(flops=0, bytes_accessed=4 * count * math.prod(shape), transcendentals=0),
        name="collect",
    )(places, slots)


def spread_plan(devices, slots):
    lines = min(4, devices)
    columns = devices // lines
    across = slots * 5 // 32 if columns == 2 else 0
    cuts = next(q for q in (9, 3, 2, 1) if (slots - across) % q == 0)
    return lines, columns, across, cuts


def spread_kernel(
    devices, size, slots, height, slots_ref, x_ref, cot_ref, gains_ref,
    all_ref, x_all, cot_all, gains_all, cos_ref, sin_ref, start_ref, inv_ref, gains_land, x_own_ref,
    z_send, z_recv, y_send, y_recv, e_send, e_recv, x_send, x_recv, c_send, c_recv, w_send, w_recv, local_sem
):
    lines, columns, across, cuts = spread_plan(devices, slots)
    dp, me = lax.axis_index("dp"), lax.axis_index("mp")
    a, b = dp // columns, lax.rem(dp, columns)
    chips = size // 2
    chip, core = me // 2, lax.rem(me, 2)
    partner = me + 1 - 2 * core
    tokens, narrow = x_ref.shape
    own = tokens // size
    x_steps = x_recv.shape[1]
    x_rows = tokens // x_steps
    cut_rows = (slots - across) * height // cuts
    has_left, has_right = a > 0, a < lines - 1

    def remote(source, target, send, receive, device):
        return pltpu.make_async_remote_copy(
            src_ref=source, dst_ref=target, send_sem=send, recv_sem=receive, device_id=device, device_id_type=MESH
        )

    def column(j):
        return lax.rem(b + j, columns)

    def other(k, which):
        return 2 * lax.rem(chip + k, chips) + which

    def mp_peer(j):
        return lax.rem(me + j, size)

    barrier = pltpu.get_barrier_semaphore()

    def greet(device):
        pl.semaphore_signal(barrier, inc=1, device_id=device, device_id_type=MESH)

    for j in range(1, columns):
        greet((a * columns + column(j), me))
    for j in range(1, size):
        greet((dp, mp_peer(j)))

    @pl.when(has_left)
    def _():
        greet((dp - columns, me))

    @pl.when(has_right)
    def _():
        greet((dp + columns, me))

    pl.semaphore_wait(
        barrier, columns - 1 + size - 1 + has_left.astype(jnp.int32) + has_right.astype(jnp.int32)
    )

    items = cuts + (columns if across else 0)

    def region(ref, line, c, row=None):
        if c < cuts:
            source, first, count = line * columns + b, across * height + c * cut_rows, cut_rows
        else:
            source, first, count = line * columns + (c - cuts), 0, across * height
        return ref.at[source, pl.ds(first, count), :]

    def own_part(c):
        first, count = (across * height + c * cut_rows, cut_rows) if c < cuts else (0, across * height)
        return slots_ref.at[pl.ds(first, count), :]

    def along(line, c, to_right, source=None):
        here = region(all_ref, line, c)
        side = 1 if to_right else 0
        device = (dp + columns if to_right else dp - columns, me)
        return remote(here if source is None else source, here, z_send.at[line, side, c], z_recv.at[line, c], device)

    def over(line, c, j, source=None):
        here = region(all_ref, line, c)
        return remote(
            here if source is None else source, here, y_send.at[line, j, c], y_recv.at[line, b, c],
            (a * columns + column(j), me),
        )

    def over_got(line, column_from, c):
        first = across * height + c * cut_rows
        here = all_ref.at[line * columns + column_from, pl.ds(first, cut_rows), :]
        return remote(here, here, y_send.at[line, 1, c], y_recv.at[line, column_from, c], (dp, partner))

    def early(j):
        here = all_ref.at[dp, pl.ds(0, across * height), :]
        return remote(own_part(cuts), here, e_send.at[j], e_recv.at[b], (a * columns + column(j), me))

    def early_got(column_from):
        here = all_ref.at[a * columns + column_from, pl.ds(0, across * height), :]
        return remote(here, here, e_send.at[1], e_recv.at[column_from], (dp, partner))

    def x_piece(ref, s):
        return ref.at[pl.ds(s * x_rows, x_rows), :]

    def x_own(s, k):
        device = (dp, partner) if k == 0 else (dp, other(k, core))
        return remote(x_piece(x_ref, s), x_piece(x_all.at[me], s), x_send.at[k, s], x_recv.at[me, s], device)

    def x_forward(s, k):
        source = other(k, core)
        here = x_piece(x_all.at[source], s)
        return remote(here, here, x_send.at[chips + k - 1, s], x_recv.at[source, s], (dp, partner))

    def x_got(s, source):
        here = x_piece(x_all.at[source], s)
        return remote(here, here, x_send.at[0, s], x_recv.at[source, s], (dp, partner))

    def cot_own(j):
        device = mp_peer(j)
        rows = pl.ds(pl.multiple_of(device * own, own), own)
        return remote(cot_ref.at[rows, :], cot_all.at[me], c_send.at[j - 1], c_recv.at[me], (dp, device))

    def cot_got(j):
        here = cot_all.at[mp_peer(j)]
        return remote(here, here, c_send.at[j - 1], c_recv.at[mp_peer(j)], (dp, partner))

    def gains_own(j):
        return remote(gains_ref, gains_land.at[me], w_send.at[j - 1], w_recv.at[me], (dp, mp_peer(j)))

    if across:
        for j in range(1, columns):
            early(j).start()
    for j in range(1, size):
        gains_own(j).start()
    gains_land[me] = gains_ref[...]
    for c in range(cuts):
        for side, there in ((False, has_left), (True, has_right)):

            @pl.when(there)
            def _():
                along(a, c, side, own_part(c)).start()

        for j in range(1, columns):
            over(a, c, j, own_part(c)).start()
    for s in range(x_steps):
        for k in range(chips):
            x_own(s, (k + 1) % chips).start()
    for j in range(1, size):
        cot_own(j).start()
    local = [
        pltpu.make_async_copy(slots_ref, all_ref.at[dp], local_sem.at[0]),
        pltpu.make_async_copy(x_ref, x_all.at[me], local_sem.at[1]),
        pltpu.make_async_copy(
            cot_ref.at[pl.ds(pl.multiple_of(me * own, own), own), :], cot_all.at[me], local_sem.at[2]
        ),
    ]
    for copy in local:
        copy.start()
    if across:
        for j in range(1, columns):
            early_got(column(j)).wait_recv()
        for c in range(cuts, items):
            for side, there in ((False, has_left), (True, has_right)):
                mine = b == c - cuts

                @pl.when(jnp.logical_and(there, mine))
                def _():
                    along(a, c, side, own_part(c)).start()

                @pl.when(jnp.logical_and(there, jnp.logical_not(mine)))
                def _():
                    along(a, c, side).start()

    for s in range(x_steps):
        for k in range(1, chips):
            x_got(s, other(k, core)).wait_recv()
            x_forward(s, k).start()

    rope_rows = min(256, tokens)

    def rope_table(i, carry):
        here = pl.ds(pl.multiple_of(i * rope_rows, rope_rows), rope_rows)
        lane = lax.broadcasted_iota(jnp.int32, (rope_rows, LANES), 1)
        position = (lax.broadcasted_iota(jnp.int32, (rope_rows, LANES), 0) + i * rope_rows).astype(f32)
        j = lane % (HD // 2)
        angle = position * jnp.exp(j.astype(f32) * (-2.0 * math.log(10000.0) / HD))
        cos_ref[here, :] = jnp.cos(angle)
        sin_ref[here, :] = jnp.where(lane % HD < HD // 2, -1.0, 1.0) * jnp.sin(angle)
        return carry

    lax.fori_loop(0, tokens // rope_rows, rope_table, 0)

    for hop in range(1, lines):
        for c in range(items):
            for to_right in (True, False):
                line = a - hop if to_right else a + hop
                there = line >= 0 if to_right else line < lines
                onward = has_right if to_right else has_left

                @pl.when(there)
                def _():
                    along(line, c, to_right).wait_recv()

                    @pl.when(onward)
                    def _():
                        along(line, c, to_right).start()

                    if c < cuts:
                        for j in range(1, columns):
                            over(line, c, j).start()

    for s in range(x_steps):
        x_got(s, partner).wait_recv()
        for k in range(1, chips):
            x_got(s, other(k, 1 - core)).wait_recv()
    local[1].wait()
    mine = pltpu.make_async_copy(
        x_all.at[:, pl.ds(pl.multiple_of(me * own, own), own), :], x_own_ref, local_sem.at[1]
    )
    mine.start()
    mine.wait()
    start_rows = min(128, own)

    def start_part(i, carry):
        here = pl.ds(pl.multiple_of(i * start_rows, start_rows), start_rows)
        x = jnp.concatenate([x_own_ref[d, here, :] for d in range(size)], axis=1).astype(f32)
        unit_rows, inverse = normalize(x)
        start_ref[here, :] = unit_rows
        inv_ref[here, :] = jnp.broadcast_to(inverse, (start_rows, LANES))
        return carry

    lax.fori_loop(0, own // start_rows, start_part, 0)

    for line in range(lines):
        for c in range(cuts):
            for j in range(1, columns):
                over_got(line, column(j), c).wait_recv()
    for j in range(1, size):
        cot_got(j).wait_recv()
        here = gains_land.at[mp_peer(j)]
        remote(here, here, w_send.at[j - 1], w_recv.at[mp_peer(j)], (dp, partner)).wait_recv()
        gains_own(j).wait_send()
    for d in range(size):
        gains_all[:, d * narrow : (d + 1) * narrow] = gains_land[d]
    local[0].wait()
    local[2].wait()
    if across:
        for j in range(1, columns):
            early(j).wait_send()
    for s in range(x_steps):
        for k in range(chips):
            x_own(s, k).wait_send()
        for k in range(1, chips):
            x_forward(s, k).wait_send()
    for j in range(1, size):
        cot_own(j).wait_send()
    for line in range(lines):
        for c in range(items):
            @pl.when(jnp.logical_and(has_right, line <= a))
            def _():
                along(line, c, True).wait_send()

            @pl.when(jnp.logical_and(has_left, line >= a))
            def _():
                along(line, c, False).wait_send()

            if c < cuts:
                for j in range(1, columns):
                    over(line, c, j).wait_send()


def spread(slots_low, hidden_in, cotangent, gains, devices, size, collective_id):
    slots, height, _ = slots_low.shape
    tokens, narrow = hidden_in.shape
    lines, columns, across, cuts = spread_plan(devices, slots)
    items = cuts + (columns if across else 0)
    chips = size // 2
    x_steps = 4
    dma = pltpu.SemaphoreType.DMA
    return pl.pallas_call(
        functools.partial(spread_kernel, devices, size, slots, height),
        out_shape=[
            jax.ShapeDtypeStruct((devices, slots * height, D), bf16),
            jax.ShapeDtypeStruct((size, tokens, narrow), bf16),
            jax.ShapeDtypeStruct((size, tokens // size, narrow), bf16),
            jax.ShapeDtypeStruct((gains.shape[0], D), f32),
            jax.ShapeDtypeStruct((tokens, LANES), f32),
            jax.ShapeDtypeStruct((tokens, LANES), f32),
            jax.ShapeDtypeStruct((tokens // size, D), f32),
            jax.ShapeDtypeStruct((tokens // size, LANES), f32),
        ],
        in_specs=[VMEM_WHOLE] * 4,
        out_specs=[ANYWHERE] * 3 + [VMEM_WHOLE] * 5,
        scratch_shapes=[
            pltpu.VMEM((size, *gains.shape), f32),
            pltpu.VMEM((size, tokens // size, narrow), bf16),
            dma((lines, 2, items)),
            dma((lines, items)),
            dma((lines, columns, cuts)),
            dma((lines, columns, cuts)),
            dma((columns,)),
            dma((columns,)),
            dma((2 * chips - 1, x_steps)),
            dma((size, x_steps)),
            dma((size - 1,)),
            dma((size,)),
            dma((size - 1,)),
            dma((size,)),
            dma((3,)),
        ],
        compiler_params=remote_params(collective_id),
        cost_estimate=pl.CostEstimate(flops=0, bytes_accessed=devices * slots * height * D * 4, transcendentals=0),
        name="spread",
    )(slots_low.reshape(slots * height, D), hidden_in, cotangent, gains)


def shards(
    n_dp,
    hidden_in,
    cotangent,
    owners,
    masters,
    firsts,
    seconds,
    width_gains,
    width_first,
    width_second,
    hidden_gains,
    hidden_first,
    hidden_second,
):
    tokens = hidden_in.shape[0]
    narrow = hidden_in.shape[1]
    slot_count = masters.shape[1]
    block_rows = masters.shape[2]
    blocks = owners.shape[0]
    hidden_local = hidden_gains.shape[1]
    dp_index = lax.axis_index("dp")
    mp_index = lax.axis_index("mp")
    own_tokens = tokens // (D // narrow)

    block_order = jnp.arange(blocks)
    same_owner = owners[:, None] == owners[None, :]
    slot_rank = jnp.sum(
        jnp.logical_and(same_owner, block_order[None, :] < block_order[:, None]).astype(jnp.int32),
        axis=1,
    )
    owned_mask = owners == dp_index
    in_use = jnp.arange(slot_count) < jnp.sum(owned_mask.astype(jnp.int32))
    slot_block = jnp.sum(
        jnp.where(
            jnp.logical_and(owned_mask[None, :], slot_rank[None, :] == jnp.arange(slot_count)[:, None]),
            block_order[None, :],
            0,
        ),
        axis=1,
    )

    size = D // narrow
    all_slots, x_all, cot_all, gains, cosine, sine, start_unit, start_inv = spread(
        masters[0].astype(bf16), hidden_in, cotangent, width_gains, n_dp, size, 6
    )
    weights = collect(
        owners * slot_count + slot_rank, all_slots.reshape(n_dp * slot_count, block_rows, D)
    ).reshape(blocks * block_rows, D)
    operand, queries, keys, values, q_turned, k_turned = project(x_all, weights, width_gains, cosine, sine)
    attended, mixed = attend(queries, keys, values)

    attn_branch, middle, middle_low = attention_sum(
        attended, weights, start_unit, gains, 3 * narrow, size, STEPS, 1
    )
    out_rows, middle_rows, up_raw, gate_raw, d_mlp, d_middle, g_rate_mlp = mlp(
        middle_low, weights, hidden_gains, middle, cot_all, gains, size, STEPS, 2
    )
    d_attn, d_start, g_rate_attn, g_scales, g_wide, g_down = mlp_back(
        d_mlp, weights, hidden_gains, up_raw, gate_raw, middle_rows, d_middle, start_unit, attn_branch, gains,
        size, MLP_STEPS, 3,
    )
    d_attn, g_wide = lax.optimization_barrier((d_attn, g_wide))
    wide_grads = lax.psum(g_wide.reshape(-1, block_rows, D), "dp")
    d_attended, attn_grad_rows = gather_project(d_attn, weights, narrow, 3 * narrow, size, STEPS, 4, "attention_gather")
    d_queries, d_keys, d_values = attend_back(queries, keys, values, mixed, d_attended)
    grads_qkv, g_qk = project_back(
        d_queries, d_keys, d_values, q_turned, k_turned, width_gains, cosine, sine
    )
    grad_pieces, g_attn = start_sum(
        grads_qkv, weights, d_start, start_unit, start_inv, operand, attended, attn_grad_rows, size, STEPS, 5
    )
    small = jnp.zeros((8, hidden_local), f32)
    small = small.at[0:1, :narrow].set(g_qk).at[1:3, :].set(g_scales)
    attn_grads, down_grads, small, hidden_out, grad_in = tail_sum(g_attn, g_down, jnp.concatenate([g_rate_attn, g_rate_mlp], axis=0), small, out_rows, grad_pieces, n_dp, size, 7)
    hidden_out = hidden_out.reshape(tokens, narrow)
    grad_in = grad_in.reshape(tokens, narrow).astype(f32)
    width_total = jnp.concatenate([small[0:1, :narrow], small[3:5, :narrow]], axis=0)
    hidden_total = small[1:3, :]
    index = jnp.stack([slot_block, in_use.astype(jnp.int32)], axis=1)
    masters_new, firsts_new, seconds_new, weight_grads = [
        part[None]
        for part in optimizer(index, attn_grads, wide_grads, down_grads, masters[0], firsts[0], seconds[0])
    ]
    width_new, width_first_new, width_second_new = adam_update(
        width_gains, width_total, width_first, width_second, 0.0, GAIN_RATE
    )
    hidden_new, hidden_first_new, hidden_second_new = adam_update(
        hidden_gains, hidden_total, hidden_first, hidden_second, 0.0, GAIN_RATE
    )
    return (
        hidden_out,
        grad_in,
        masters_new,
        firsts_new,
        seconds_new,
        weight_grads,
        width_new,
        width_total,
        width_first_new,
        width_second_new,
        hidden_new,
        hidden_total,
        hidden_first_new,
        hidden_second_new,
    )


def solution(mesh):
    in_specs = (
        P("dp", "mp"),
        P("dp", "mp"),
        P(),
        P("mp", "dp", None, None),
        P("mp", "dp", None, None),
        P("mp", "dp", None, None),
        P(None, "mp"),
        P(None, "mp"),
        P(None, "mp"),
        P(None, "mp"),
        P(None, "mp"),
        P(None, "mp"),
    )
    out_specs = (
        P("dp", "mp"),
        P("dp", "mp"),
        P("mp", "dp", None, None),
        P("mp", "dp", None, None),
        P("mp", "dp", None, None),
        P("mp", "dp", None, None),
        P(None, "mp"),
        P(None, "mp"),
        P(None, "mp"),
        P(None, "mp"),
        P(None, "mp"),
        P(None, "mp"),
        P(None, "mp"),
        P(None, "mp"),
    )
    return jax.shard_map(functools.partial(shards, mesh.shape["dp"]), mesh=mesh, in_specs=in_specs, out_specs=out_specs, check_vma=False)
```

```python
import functools
import math

import jax
import jax.numpy as jnp
from jax import lax
from jax.experimental import pallas as pl
from jax.experimental.pallas import tpu as pltpu
from jax.sharding import PartitionSpec as P

D = 1024
HD = 64
STEP = 7
LANES = 128
STEPS = 4
MLP_STEPS = 2
LATE_PARTS = 2

EPSILON = 1e-06
ADAM_EPSILON = 1e-08
BETA_FIRST = 0.9
BETA_SECOND = 0.95
LEARN_RATE = 0.05
GAIN_RATE = 0.6
WEIGHT_DECAY = 0.1
SCORE_SCALE = float(HD) ** 0.5

f32 = jnp.float32
bf16 = jnp.bfloat16


def nn(left, right):
    return jnp.dot(left, right, preferred_element_type=f32)


def nt(left, right):
    return lax.dot_general(left, right, (((1,), (1,)), ((), ())), preferred_element_type=f32)


def tn(left, right):
    return lax.dot_general(left, right, (((0,), (0,)), ((), ())), preferred_element_type=f32)


def normalize(vector):
    inverse = lax.rsqrt(jnp.sum(vector * vector, axis=-1, keepdims=True) / D + EPSILON)
    return (vector * inverse, inverse)


def normalize_back(unit_rows, inverse, upstream):
    return inverse * (upstream - unit_rows * (jnp.sum(unit_rows * upstream, axis=-1, keepdims=True) / D))


def blend_branch(base_rows, branch, branch_rate):
    branch_unit, branch_inv = normalize(branch)
    mixed_unit, mixed_inv = normalize(base_rows + branch_rate * (branch_unit - base_rows))
    return (branch_unit, branch_inv, mixed_unit, mixed_inv)


def blend_back(base_rows, branch_unit, branch_inv, mixed_unit, mixed_inv, branch_rate, upstream):
    d_mixed = normalize_back(mixed_unit, mixed_inv, upstream)
    d_branch = normalize_back(branch_unit, branch_inv, branch_rate * d_mixed)
    return (
        (1.0 - branch_rate) * d_mixed,
        d_branch,
        jnp.sum(d_mixed * (branch_unit - base_rows), axis=0),
    )


def adam_update(params, gradient, first_moment, second_moment, decay_rate, step_rate):
    first_new = BETA_FIRST * first_moment + (1.0 - BETA_FIRST) * gradient
    second_new = BETA_SECOND * second_moment + (1.0 - BETA_SECOND) * gradient * gradient
    corrected = (
        first_new
        / (1.0 - BETA_FIRST**STEP)
        / (jnp.sqrt(second_new / (1.0 - BETA_SECOND**STEP)) + ADAM_EPSILON)
    )
    return (params - step_rate * (corrected + decay_rate * params), first_new, second_new)


def swap_halves(pair, lane):
    return jnp.where(
        lane % HD < HD // 2, pltpu.roll(pair, LANES - HD // 2, 1), pltpu.roll(pair, HD // 2, 1)
    )


def head_sums(values):
    width = values.shape[1]
    row = lax.broadcasted_iota(jnp.int32, (width, width), 0) // HD
    column = lax.broadcasted_iota(jnp.int32, (width, width), 1) // HD
    same = jnp.where(row == column, 1.0, 0.0).astype(bf16)
    high = values.astype(bf16)
    rest = values - high.astype(f32)
    middle = rest.astype(bf16)
    low = (rest - middle.astype(f32)).astype(bf16)
    return nn(high, same) + nn(middle, same) + nn(low, same)


def project_kernel(
    narrow, x_ref, w_ref, gain_ref, cos_ref, sin_ref, op_ref, q_ref, k_ref, v_ref, qr_ref, kr_ref
):
    rows = x_ref.shape[1]
    x = jnp.concatenate([x_ref[d] for d in range(x_ref.shape[0])], axis=1).astype(f32)
    operand = (x * lax.rsqrt(jnp.sum(x * x, axis=1, keepdims=True) / D + EPSILON)).astype(bf16)
    op_ref[...] = operand
    lane = lax.broadcasted_iota(jnp.int32, (rows, LANES), 1)
    cosine, sine = cos_ref[...], sin_ref[...]
    raw = nt(operand, w_ref[...])
    pairs = range(narrow // LANES)
    for which in range(2):
        out_ref, rot_ref = ((q_ref, qr_ref), (k_ref, kr_ref))[which]
        fill = (0.0, 1.0)[which]
        turned = []
        for pair in pairs:
            here = raw[:, which * narrow + pair * LANES : which * narrow + (pair + 1) * LANES]
            turned.append(here * cosine + swap_halves(here, lane) * sine)
        turned = jnp.concatenate(turned, axis=1)
        rot_ref[...] = turned
        gained = gain_ref[0:1, :] * (turned * lax.rsqrt(head_sums(turned * turned) + EPSILON))
        gained = gained.astype(bf16).astype(f32)
        if which == 0:
            gained = gained * SCORE_SCALE
        for pair in pairs:
            here = gained[:, pair * LANES : (pair + 1) * LANES]
            out_ref[2 * pair] = jnp.where(lane < HD, here, fill).astype(bf16)
            out_ref[2 * pair + 1] = jnp.where(lane < HD, pltpu.roll(here, HD, 1), fill).astype(bf16)
    for pair in range(narrow // LANES):
        here = raw[:, 2 * narrow + pair * LANES : 2 * narrow + (pair + 1) * LANES]
        v_ref[2 * pair] = jnp.where(lane < HD, here, 1.0).astype(bf16)
        v_ref[2 * pair + 1] = jnp.where(lane < HD, pltpu.roll(here, HD, 1), 1.0).astype(bf16)


def project(x_all, weights, gain, cosine, sine):
    size, tokens, narrow = x_all.shape
    heads = narrow // HD
    rows = min(512, tokens)
    head_spec = pl.BlockSpec((heads, rows, LANES), lambda i: (0, i, 0))
    row_spec = lambda width: pl.BlockSpec((rows, width), lambda i: (i, 0))
    whole = lambda a: pl.BlockSpec(a.shape, lambda i: (0, 0))
    return pl.pallas_call(
        functools.partial(project_kernel, narrow),
        grid=(tokens // rows,),
        in_specs=[pl.BlockSpec((size, rows, narrow), lambda i: (0, i, 0)), pl.BlockSpec((3 * narrow, D), lambda i: (0, 0)), whole(gain), row_spec(LANES), row_spec(LANES)],
        out_specs=[row_spec(D), head_spec, head_spec, head_spec, row_spec(narrow), row_spec(narrow)],
        out_shape=[jax.ShapeDtypeStruct((tokens, D), bf16)]
        + [jax.ShapeDtypeStruct((heads, tokens, LANES), bf16)] * 3
        + [jax.ShapeDtypeStruct((tokens, narrow), f32)] * 2,
        cost_estimate=pl.CostEstimate(
            flops=2 * tokens * D * 3 * narrow, bytes_accessed=tokens * D * 8, transcendentals=0
        ),
        name="project",
    )(x_all, weights, gain, cosine, sine)


def attend_kernel(block, q_ref, k_ref, v_ref, att_ref, o_ref):
    i = pl.program_id(1)
    lane = lax.broadcasted_iota(jnp.int32, (block, LANES), 1)
    queries = [q_ref[h] for h in range(2)]

    def step(j, sums, diagonal):
        rows = pl.ds(pl.multiple_of(j * block, block), block)
        new = []
        for h in range(2):
            weight = jnp.exp(nt(queries[h], k_ref[h, rows, :]))
            if diagonal:
                row = lax.broadcasted_iota(jnp.int32, weight.shape, 0)
                column = lax.broadcasted_iota(jnp.int32, weight.shape, 1)
                weight = jnp.where(row >= column, weight, 0.0)
            new.append(sums[h] + nn(weight.astype(bf16), v_ref[h, rows, :]))
        return tuple(new)

    zero = jnp.zeros((block, LANES), f32)
    sums = lax.fori_loop(0, i, lambda j, s: step(j, s, False), (zero, zero))
    sums = step(i, sums, True)
    mixed = []
    for h in range(2):
        total = pltpu.roll(sums[h], HD, 1)
        o_ref[h] = jnp.where(lane < HD, sums[h] / total, jnp.log(sums[h]))
        mixed.append(o_ref[h])
    att_ref[...] = jnp.where(lane < HD, mixed[0], pltpu.roll(mixed[1], HD, 1)).astype(bf16)


def attend(queries, keys, values):
    heads, tokens, _ = queries.shape
    block = min(512, tokens)
    part = pl.BlockSpec((2, block, LANES), lambda p, i: (p, i, 0))
    whole = pl.BlockSpec((2, tokens, LANES), lambda p, i: (p, 0, 0))
    return pl.pallas_call(
        functools.partial(attend_kernel, block),
        grid=(heads // 2, tokens // block),
        in_specs=[part, whole, whole],
        out_specs=[pl.BlockSpec((block, LANES), lambda p, i: (i, p)), part],
        out_shape=[
            jax.ShapeDtypeStruct((tokens, heads * HD), bf16),
            jax.ShapeDtypeStruct((heads, tokens, LANES), f32),
        ],
        cost_estimate=pl.CostEstimate(
            flops=heads * tokens * tokens * LANES * 4,
            bytes_accessed=heads * tokens * LANES * 10,
            transcendentals=heads * tokens * tokens // 2,
        ),
        name="attend",
    )(queries, keys, values)


def with_parts(lane, base, value):
    high = value.astype(bf16).astype(f32)
    rest = value - high
    middle = rest.astype(bf16).astype(f32)
    low = rest - middle
    tail = jnp.where(lane == HD, high, jnp.where(lane == HD + 1, middle, jnp.where(lane == HD + 2, low, 0.0)))
    return jnp.where(lane < HD, base, tail).astype(bf16)


def attend_back_kernel(
    block, q_ref, k_ref, v_ref, o_ref, do_ref, dq_ref, dk_ref, dv_ref, dk_sum, dv_sum
):
    i = pl.program_id(1)
    count = pl.num_programs(1)
    lane = lax.broadcasted_iota(jnp.int32, (block, LANES), 1)

    @pl.when(i == 0)
    def _():
        dk_sum[...] = jnp.zeros_like(dk_sum)
        dv_sum[...] = jnp.zeros_like(dv_sum)

    d_pair = do_ref[...].astype(f32)
    d_heads = [d_pair, pltpu.roll(d_pair, HD, 1)]
    queries, upstream = [], []
    for h in range(2):
        mixed = o_ref[h]
        delta = jnp.sum(jnp.where(lane < HD, mixed * d_heads[h], 0.0), axis=1, keepdims=True)
        queries.append(with_parts(lane, q_ref[h].astype(f32), -mixed))
        upstream.append(with_parts(lane, d_heads[h], -jnp.broadcast_to(delta, (block, LANES))))

    def step(j, sums, diagonal):
        rows = pl.ds(pl.multiple_of(j * block, block), block)
        new = []
        for h in range(2):
            keys = k_ref[h, rows, :]
            probs = jnp.exp(nt(keys, queries[h]))
            if diagonal:
                row = lax.broadcasted_iota(jnp.int32, probs.shape, 0)
                column = lax.broadcasted_iota(jnp.int32, probs.shape, 1)
                probs = jnp.where(column >= row, probs, 0.0)
            d_scores = (probs * nt(v_ref[h, rows, :], upstream[h])).astype(bf16)
            dv_sum[h, rows, :] += nn(probs.astype(bf16), upstream[h])
            dk_sum[h, rows, :] += nn(d_scores, queries[h])
            new.append(sums[h] + tn(d_scores, keys))
        return tuple(new)

    zero = jnp.zeros((block, LANES), f32)
    sums = lax.fori_loop(0, i, lambda j, s: step(j, s, False), (zero, zero))
    sums = step(i, sums, True)
    dq_ref[...] = jnp.where(lane < HD, sums[0], pltpu.roll(sums[1], HD, 1)) * SCORE_SCALE

    @pl.when(i == count - 1)
    def _():
        def put(j, carry):
            rows = pl.ds(pl.multiple_of(j * block, block), block)
            dk_ref[rows, :] = jnp.where(lane < HD, dk_sum[0, rows, :], pltpu.roll(dk_sum[1, rows, :], HD, 1))
            dv_ref[rows, :] = jnp.where(lane < HD, dv_sum[0, rows, :], pltpu.roll(dv_sum[1, rows, :], HD, 1))
            return carry

        lax.fori_loop(0, count, put, 0)


def attend_back(queries, keys, values, mixed, d_attended):
    heads, tokens, _ = queries.shape
    block = min(512, tokens)
    part = pl.BlockSpec((2, block, LANES), lambda p, i: (p, i, 0))
    whole = pl.BlockSpec((2, tokens, LANES), lambda p, i: (p, 0, 0))
    pair_part = pl.BlockSpec((block, LANES), lambda p, i: (i, p))
    pair_whole = pl.BlockSpec((tokens, LANES), lambda p, i: (0, p))
    return pl.pallas_call(
        functools.partial(attend_back_kernel, block),
        grid=(heads // 2, tokens // block),
        in_specs=[part, whole, whole, part, pair_part],
        out_specs=[pair_part, pair_whole, pair_whole],
        out_shape=[jax.ShapeDtypeStruct((tokens, heads * HD), f32)] * 3,
        scratch_shapes=[pltpu.VMEM((2, tokens, LANES), f32)] * 2,
        cost_estimate=pl.CostEstimate(
            flops=heads * tokens * tokens * LANES * 10,
            bytes_accessed=heads * tokens * LANES * 20,
            transcendentals=heads * tokens * tokens // 2,
        ),
        name="attend_back",
    )(queries, keys, values, mixed, d_attended)


def project_back_kernel(
    narrow, dq_ref, dk_ref, dv_ref, qr_ref, kr_ref, gain_ref, cos_ref, sin_ref, out_ref, gg_ref
):
    rows = dq_ref.shape[0]
    lane = lax.broadcasted_iota(jnp.int32, (rows, LANES), 1)
    cosine, sine = cos_ref[...], sin_ref[...]

    @pl.when(pl.program_id(0) == 0)
    def _():
        gg_ref[...] = jnp.zeros_like(gg_ref)

    for which in range(2):
        d_ref, rot_ref = ((dq_ref, qr_ref), (dk_ref, kr_ref))[which]
        turned = rot_ref[...]
        inverse = lax.rsqrt(head_sums(turned * turned) + EPSILON)
        unit_rows = turned * inverse
        upstream = d_ref[...]
        gg_ref[...] += jnp.sum(upstream * unit_rows, axis=0, keepdims=True)
        upstream = upstream * gain_ref[0:1, :]
        back = inverse * (upstream - unit_rows * head_sums(unit_rows * upstream))
        for pair in range(narrow // LANES):
            here = back[:, pair * LANES : (pair + 1) * LANES]
            here = here * cosine - swap_halves(here, lane) * sine
            out_ref[:, which * narrow + pair * LANES : which * narrow + (pair + 1) * LANES] = here.astype(bf16)
    out_ref[:, 2 * narrow : 3 * narrow] = dv_ref[...].astype(bf16)


def project_back(d_queries, d_keys, d_values, q_turned, k_turned, gain, cosine, sine):
    tokens, narrow = d_queries.shape
    rows = min(512, tokens)
    row_spec = lambda width: pl.BlockSpec((rows, width), lambda i: (i, 0))
    one = pl.BlockSpec((1, narrow), lambda i: (0, 0))
    whole = pl.BlockSpec(gain.shape, lambda i: (0, 0))
    return pl.pallas_call(
        functools.partial(project_back_kernel, narrow),
        grid=(tokens // rows,),
        in_specs=[row_spec(narrow)] * 5 + [whole, row_spec(LANES), row_spec(LANES)],
        out_specs=[row_spec(3 * narrow), one],
        out_shape=[
            jax.ShapeDtypeStruct((tokens, 3 * narrow), bf16),
            jax.ShapeDtypeStruct((1, narrow), f32),
        ],
        cost_estimate=pl.CostEstimate(
            flops=tokens * narrow * 60, bytes_accessed=tokens * narrow * 26, transcendentals=0
        ),
        name="project_back",
    )(d_queries, d_keys, d_values, q_turned, k_turned, gain, cosine, sine)


MESH = pl.DeviceIdType.MESH


class Group:
    def __init__(self, size, steps, tokens):
        self.size, self.steps = size, steps
        self.chips = size // 2
        self.own = tokens // size
        self.rows = self.own // steps
        self.dp, self.me = lax.axis_index("dp"), lax.axis_index("mp")
        self.chip, self.core = self.me // 2, lax.rem(self.me, 2)
        self.partner = self.me + 1 - 2 * self.core

    def other(self, k, core):
        return 2 * lax.rem(self.chip + k, self.chips) + core

    def slot(self, device):
        k = lax.rem(device // 2 - self.chip + self.chips, self.chips)
        return jnp.where(k == 0, 0, 2 * k - 1 + (lax.rem(device, 2) != self.core).astype(jnp.int32))

    def piece(self, ref, index, step):
        return ref.at[index, pl.ds(pl.multiple_of(step * self.rows, self.rows), self.rows), :]

    def copy(self, source, target, send, receive, device):
        return pltpu.make_async_remote_copy(
            src_ref=source,
            dst_ref=target,
            send_sem=send,
            recv_sem=receive,
            device_id=(self.dp, device),
            device_id_type=MESH,
        )

    def meet(self, everyone=False):
        barrier = pltpu.get_barrier_semaphore()
        devices = [self.partner] + [self.other(k, self.core) for k in range(1, self.chips)]
        if everyone:
            devices = [lax.rem(self.me + j, self.size) for j in range(1, self.size)]
        for device in devices:
            pl.semaphore_signal(barrier, inc=1, device_id=(self.dp, device), device_id_type=MESH)
        pl.semaphore_wait(barrier, len(devices))

    def place(self, i, remote_first=False):
        size, steps = self.size, self.steps
        others = steps * (size - 1)
        if remote_first:
            is_own = i >= others
            j = jnp.where(is_own, 0, i)
            s = jnp.where(is_own, i - others, j // (size - 1))
            r = lax.rem(lax.rem(j, size - 1) + 1, size - 1)
        else:
            is_own = i < steps
            j = jnp.where(is_own, 0, i - steps)
            s = jnp.where(is_own, i, j // (size - 1))
            r = lax.rem(j, size - 1)
        other = jnp.logical_not(is_own)
        is_partner = jnp.logical_and(other, r == 0)
        remote = jnp.logical_and(other, r > 0)
        is_first = jnp.logical_and(remote, lax.rem(r, 2) == 1)
        is_second = jnp.logical_and(remote, lax.rem(r, 2) == 0)
        k = jnp.where(remote, (r + 1) // 2, 0)
        core = jnp.where(jnp.logical_or(is_own, is_first), self.core, 1 - self.core)
        return self.other(k, core), s, k, is_own, is_partner, is_first, is_second

    def run(self, compute, gather=None, settle=None, remote_first=False, after=None, ready=(), between=None):
        steps, chips, size = self.steps, self.chips, self.size

        if gather:
            own_ref, all_ref, g_send, g_recv = gather

            def own_piece(s):
                return own_ref.at[pl.ds(pl.multiple_of(s * self.rows, self.rows), self.rows), :]

            def start_own(s, carry):
                for k in range(1, chips):
                    self.copy(own_piece(s), self.piece(all_ref, self.me, s), g_send.at[k, s], g_recv.at[self.me, s], self.other(k, self.core)).start()
                self.copy(own_piece(s), self.piece(all_ref, self.me, s), g_send.at[0, s], g_recv.at[self.me, s], self.partner).start()
                return carry

            lax.fori_loop(0, steps, start_own, 0)
            all_ref[self.me] = own_ref[...]

            def got(device, s):
                here = self.piece(all_ref, device, s)
                self.copy(here, here, g_send.at[0, s], g_recv.at[device, s], self.partner).wait_recv()

            def forward(k, s):
                device = self.other(k, self.core)
                here = self.piece(all_ref, device, s)
                return self.copy(here, here, g_send.at[chips + k - 1, s], g_recv.at[device, s], self.partner)

        if settle:
            out_ref, kept, to_partner, from_partner, to_chip, from_chip, p_send, p_recv, x_send, x_recv = settle

            def to_partner_copy(k, s):
                return self.copy(self.piece(to_partner, k, s), self.piece(from_partner, k, s), p_send.at[k, s], p_recv.at[k, s], self.partner)

            def to_chip_copy(k, s):
                return self.copy(self.piece(to_chip, k - 1, s), self.piece(from_chip, k - 1, s), x_send.at[k - 1, s], x_recv.at[k - 1, s], self.other(k, self.core))

        for copy in ready:
            copy.wait()

        def item(i, carry):
            device, s, k, is_own, is_partner, is_first, is_second = self.place(i, remote_first)
            if gather:

                @pl.when(jnp.logical_not(is_own))
                def _():
                    got(device, s)

                @pl.when(is_first)
                def _():
                    forward(k, s).start()

            term = compute(device, s, i)
            if between:
                between(device, jnp.logical_or(i == steps - 1, jnp.logical_and(is_partner, s == steps - 1)))
            if settle:
                here = pl.ds(pl.multiple_of(s * self.rows, self.rows), self.rows)

                @pl.when(is_own)
                def _():
                    out_ref[here, :] = term

                @pl.when(is_first)
                def _():
                    kept[...] = term

                @pl.when(jnp.logical_or(is_partner, is_second))
                def _():
                    to_partner[k, here, :] = term.astype(bf16)
                    to_partner_copy(k, s).start()

                @pl.when(is_second)
                def _():
                    to_partner_copy(k, s).wait_recv()
                    to_chip[k - 1, here, :] = (kept[...] + from_partner[k, here, :].astype(f32)).astype(bf16)
                    to_chip_copy(k, s).start()

            return carry

        lax.fori_loop(0, size * steps, item, 0)

        def end(s, carry):
            if settle:
                here = pl.ds(pl.multiple_of(s * self.rows, self.rows), self.rows)
                to_partner_copy(0, s).wait_recv()
                total = out_ref[here, :] + from_partner[0, here, :].astype(f32)
                for k in range(1, chips):
                    to_chip_copy(k, s).wait_recv()
                    total = total + from_chip[k - 1, here, :].astype(f32)
                out_ref[here, :] = total
                if after:
                    after(s)
                for k in range(chips):
                    to_partner_copy(k, s).wait_send()
                for k in range(1, chips):
                    to_chip_copy(k, s).wait_send()
            if gather:
                for k in range(2 * chips - 1):
                    self.copy(own_piece(s), own_piece(s), g_send.at[k, s], g_recv.at[0, s], self.partner).wait_send()
            return carry

        self.end = lambda first=0, last=steps: lax.fori_loop(first, last, end, 0)


def settle_scratch(size, steps, tokens):
    own, chips = tokens // size, size // 2
    return [
        pltpu.VMEM((own // steps, D), f32),
        pltpu.VMEM((chips, own, D), bf16),
        pltpu.VMEM((chips, own, D), bf16),
        pltpu.VMEM((chips - 1, own, D), bf16),
        pltpu.VMEM((chips - 1, own, D), bf16),
        pltpu.SemaphoreType.DMA((chips, steps)),
        pltpu.SemaphoreType.DMA((chips, steps)),
        pltpu.SemaphoreType.DMA((chips - 1, steps)),
        pltpu.SemaphoreType.DMA((chips - 1, steps)),
    ]


def gather_sems(size, steps):
    return [pltpu.SemaphoreType.DMA((size - 1, steps)), pltpu.SemaphoreType.DMA((size, steps))]


VMEM_WHOLE = pl.BlockSpec(memory_space=pltpu.VMEM)
ANYWHERE = pl.BlockSpec(memory_space=pl.ANY)
GRANT = 67043328


def weight_scratch(rows, count=1):
    return [pltpu.VMEM((rows, D), bf16)] * count + [pltpu.SemaphoreType.DMA((count,))]


def weight_copies(weights, buffers, sem, first):
    copies = []
    for i, buffer in enumerate(buffers):
        copies.append(pltpu.make_async_copy(weights.at[pl.ds(first, buffer.shape[0]), :], buffer, sem.at[i]))
        first += buffer.shape[0]
    return copies


def remote_params(collective_id):
    return pltpu.CompilerParams(
        collective_id=collective_id, has_side_effects=True, vmem_limit_bytes=GRANT
    )


def attention_sum_kernel(
    size, steps, first_row, rows_ref, w_hbm, start_ref, rates_ref,
    out_ref, middle_ref, low_ref, w_ref, w_sem, *scratch
):
    tokens = rows_ref.shape[0]
    group = Group(size, steps, tokens)
    (copy,) = weight_copies(w_hbm, [w_ref], w_sem, first_row)
    copy.start()
    group.meet()
    copy.wait()

    def compute(device, s, i):
        first = pl.multiple_of(device * group.own + s * group.rows, group.rows)
        return nn(rows_ref[pl.ds(first, group.rows), :], w_ref[...])

    def after(s):
        here = pl.ds(pl.multiple_of(s * group.rows, group.rows), group.rows)
        middle = blend_branch(start_ref[here, :], out_ref[here, :], rates_ref[1:2, :])[2]
        middle_ref[here, :] = middle
        low_ref[here, :] = middle.astype(bf16)

    group.run(compute, settle=(out_ref, *scratch), remote_first=True, after=after)
    group.end()


def attention_sum(rows, weights, start_unit, rates, first_row, size, steps, collective_id):
    tokens, depth = rows.shape
    own = jax.ShapeDtypeStruct((tokens // size, D), f32)
    return pl.pallas_call(
        functools.partial(attention_sum_kernel, size, steps, first_row),
        out_shape=[own, own, jax.ShapeDtypeStruct(own.shape, bf16)],
        in_specs=[VMEM_WHOLE, ANYWHERE, VMEM_WHOLE, VMEM_WHOLE],
        out_specs=[VMEM_WHOLE] * 3,
        scratch_shapes=weight_scratch(depth) + settle_scratch(size, steps, tokens),
        compiler_params=remote_params(collective_id),
        cost_estimate=pl.CostEstimate(flops=2 * tokens * depth * D, bytes_accessed=tokens * D * 8, transcendentals=0),
        name="attention_sum",
    )(rows, weights, start_unit, rates)


def mlp_kernel(
    size, steps, own_ref, w_hbm, scale_ref, middle_ref, cot_ref, rates_ref,
    out_ref, rows_ref, ur_hbm, gr_hbm, d_mlp_ref, d_middle_ref, g_rate_ref, branch_ref,
    up_ref, gate_ref, down_ref, w_sem, u_buf, g_buf, b_sem, *scratch
):
    tokens = own_ref.shape[0] * size
    group = Group(size, steps, tokens)
    copies = weight_copies(w_hbm, [up_ref, gate_ref, down_ref], w_sem, scale_ref.shape[1])
    for c in copies:
        c.start()
    group.meet()

    def save(i, device, s):
        slot = lax.rem(i, 2)
        rows = pl.ds(pl.multiple_of(device * group.own + s * group.rows, group.rows), group.rows)
        return (
            pltpu.make_async_copy(u_buf.at[slot], ur_hbm.at[rows, :], b_sem.at[0, slot]),
            pltpu.make_async_copy(g_buf.at[slot], gr_hbm.at[rows, :], b_sem.at[1, slot]),
        )

    def compute(device, s, i):
        slot = lax.rem(i, 2)

        @pl.when(i >= 2)
        def _():
            for c in save(i, device, s):
                c.wait()

        rows = group.piece(rows_ref, device, s)[...]
        up_raw = nt(rows, up_ref[...])
        gate_raw = nt(rows, gate_ref[...])
        u_buf[slot] = up_raw
        g_buf[slot] = gate_raw
        for c in save(i, device, s):
            c.start()
        gate_val = scale_ref[1:2, :] * gate_raw
        product = (scale_ref[0:1, :] * up_raw * (gate_val * jax.nn.sigmoid(gate_val))).astype(bf16)
        return nn(product, down_ref[...])

    g_rate_ref[...] = jnp.zeros_like(g_rate_ref)

    def after(s):
        here = pl.ds(pl.multiple_of(s * group.rows, group.rows), group.rows)
        middle, rate = middle_ref[here, :], rates_ref[2:3, :]
        branch_unit, branch_inv, mixed, mixed_inv = blend_branch(middle, branch_ref[here, :], rate)
        for d in range(size):
            out_ref[d, here, :] = mixed[:, d * (D // size) : (d + 1) * (D // size)]
        upstream = jnp.concatenate([cot_ref[d, here, :] for d in range(size)], axis=1).astype(f32)
        d_middle, d_branch, g_rate = blend_back(
            middle, branch_unit, branch_inv, mixed, mixed_inv, rate, upstream
        )
        d_middle_ref[here, :] = d_middle
        d_mlp_ref[here, :] = d_branch.astype(bf16)
        g_rate_ref[...] += g_rate[None]

    group.run(
        compute, gather=(own_ref, rows_ref, scratch[0], scratch[1]), settle=(branch_ref, *scratch[2:]), ready=copies, after=after
    )
    for i in range(2):
        for c in save(i, 0, 0):
            c.wait()
    group.end()


def mlp(own, weights, scales, middle, cot_all, rates, size, steps, collective_id):
    hidden = scales.shape[1]
    tokens = own.shape[0] * size
    rows = own.shape[0] // steps
    return pl.pallas_call(
        functools.partial(mlp_kernel, size, steps),
        out_shape=[
            jax.ShapeDtypeStruct((size, own.shape[0], D // size), f32),
            jax.ShapeDtypeStruct((size, own.shape[0], D), bf16),
            jax.ShapeDtypeStruct((tokens, hidden), f32),
            jax.ShapeDtypeStruct((tokens, hidden), f32),
            jax.ShapeDtypeStruct((own.shape[0], D), bf16),
            jax.ShapeDtypeStruct((own.shape[0], D), f32),
            jax.ShapeDtypeStruct((1, D), f32),
        ],
        in_specs=[VMEM_WHOLE, ANYWHERE] + [VMEM_WHOLE] * 4,
        out_specs=[VMEM_WHOLE, VMEM_WHOLE, ANYWHERE, ANYWHERE] + [VMEM_WHOLE] * 3,
        scratch_shapes=[pltpu.VMEM((own.shape[0], D), f32)]
        + weight_scratch(hidden, 3)
        + [
            pltpu.VMEM((2, rows, hidden), f32),
            pltpu.VMEM((2, rows, hidden), f32),
            pltpu.SemaphoreType.DMA((2, 2)),
        ]
        + gather_sems(size, steps)
        + settle_scratch(size, steps, tokens),
        compiler_params=remote_params(collective_id),
        cost_estimate=pl.CostEstimate(flops=6 * tokens * hidden * D, bytes_accessed=tokens * D * 12, transcendentals=tokens * hidden),
        name="mlp",
    )(own, weights, scales, middle, cot_all, rates)


def mlp_back_kernel(
    size, steps, own_ref, w_hbm, scale_ref, ur_hbm, gr_hbm, middle_rows_ref, d_middle_hbm, start_hbm, branch_hbm, rates_ref,
    d_attn_ref, d_start_ref, g_rate_ref, gs_ref, grads_hbm,
    stage, stage_sem, late, late_sem,
    sum_ref, rows_ref, product_ref, d_ref, grads_sum,
    up_ref, gate_ref, down_ref, w_sem, u_buf, g_buf, b_sem, *scratch
):
    tokens = own_ref.shape[0] * size
    group = Group(size, steps, tokens)

    def load(i):
        device, s = group.place(i)[:2]
        slot = lax.rem(i, 2)
        rows = pl.ds(pl.multiple_of(device * group.own + s * group.rows, group.rows), group.rows)
        return (
            pltpu.make_async_copy(ur_hbm.at[rows, :], u_buf.at[slot], b_sem.at[0, slot]),
            pltpu.make_async_copy(gr_hbm.at[rows, :], g_buf.at[slot], b_sem.at[1, slot]),
        )

    copies = weight_copies(w_hbm, [up_ref, gate_ref, down_ref], w_sem, scale_ref.shape[1])
    for c in (*load(0), *copies):
        c.start()
    gs_ref[...] = jnp.zeros_like(gs_ref)
    g_rate_ref[...] = jnp.zeros_like(g_rate_ref)
    group.meet()
    hidden = scale_ref.shape[1]
    part = min(256, hidden)

    def weight_grads(device):
        rows = pl.ds(pl.multiple_of(group.slot(device) * group.own, group.own), group.own)

        def one(source, offset, other):
            def column(c, carry):
                first = pl.multiple_of(c * part, part)
                to = pl.ds(pl.multiple_of(offset + first, part), part)
                term = tn(source[rows, pl.ds(first, part)], other[device])
                grads_sum[to, :] += term
                return carry

            lax.fori_loop(0, source.shape[1] // part, column, 0)

        one(d_ref, 0, middle_rows_ref)
        one(product_ref, 2 * hidden, rows_ref)

    def clear(c, carry):
        grads_sum[pl.ds(pl.multiple_of(c * part, part), part), :] = jnp.zeros((part, D), f32)
        return carry

    lax.fori_loop(0, 3 * hidden // part, clear, 0)

    def between(device, done):
        @pl.when(done)
        def _():
            weight_grads(device)

    late_rows = late.shape[2]

    def late_copies(s):
        here = pl.ds(pl.multiple_of(s * late_rows, late_rows), late_rows)
        return [
            pltpu.make_async_copy(ref.at[here, :], late.at[lax.rem(s, 2), i], late_sem.at[lax.rem(s, 2), i])
            for i, ref in enumerate((start_hbm, branch_hbm, d_middle_hbm))
        ]

    for c in late_copies(0):
        c.start()

    def after_part(s, carry):
        here = pl.ds(pl.multiple_of(s * late_rows, late_rows), late_rows)
        for c in late_copies(s):
            c.wait()

        @pl.when(s + 1 < steps * LATE_PARTS)
        def _():
            for c in late_copies(s + 1):
                c.start()

        start, branch, d_middle = [late[lax.rem(s, 2), i] for i in range(3)]
        rate = rates_ref[1:2, :]
        branch_unit, branch_inv, middle, middle_inv = blend_branch(start, branch, rate)
        d_start, d_branch, g_rate = blend_back(
            start, branch_unit, branch_inv, middle, middle_inv, rate, d_middle + sum_ref[here, :]
        )
        d_start_ref[here, :] = d_start
        d_attn_ref[here, :] = d_branch.astype(bf16)
        g_rate_ref[...] += g_rate[None]
        return carry

    def after(s):
        lax.fori_loop(s * LATE_PARTS, (s + 1) * LATE_PARTS, after_part, 0)

    def compute(device, s, i):
        slot = lax.rem(i, 2)

        @pl.when(i + 1 < size * steps)
        def _():
            for c in load(i + 1):
                c.start()

        rows = group.piece(rows_ref, device, s)[...]
        d_product = nt(rows, down_ref[...])
        for c in load(i):
            c.wait()
        first = pl.multiple_of(group.slot(device) * group.own + s * group.rows, group.rows)
        here = pl.ds(first, group.rows)
        up_raw, gate_raw = u_buf[slot], g_buf[slot]
        up_val = scale_ref[0:1, :] * up_raw
        gate_val = scale_ref[1:2, :] * gate_raw
        sigmoid = jax.nn.sigmoid(gate_val)
        activated = gate_val * sigmoid
        product_ref[here, :] = (up_val * activated).astype(bf16)
        d_up = d_product * activated
        d_gate = d_product * up_val * (sigmoid * (1.0 + gate_val * (1.0 - sigmoid)))
        gs_ref[0:1, :] += jnp.sum(d_up * up_raw, axis=0, keepdims=True)
        gs_ref[1:2, :] += jnp.sum(d_gate * gate_raw, axis=0, keepdims=True)
        d_up_raw = (d_up * scale_ref[0:1, :]).astype(bf16)
        d_gate_raw = (d_gate * scale_ref[1:2, :]).astype(bf16)
        d_ref[here, :hidden] = d_up_raw
        d_ref[here, hidden:] = d_gate_raw
        return nn(d_up_raw, up_ref[...]) + nn(d_gate_raw, gate_ref[...])

    group.run(
        compute, gather=(own_ref, rows_ref, scratch[0], scratch[1]), settle=(sum_ref, *scratch[2:]), ready=copies,
        after=after, between=between,
    )

    def rest(j, carry):
        weight_grads(group.other(1 + j // 2, lax.rem(j, 2)))
        return carry

    lax.fori_loop(0, size - 2, rest, 0)

    def stage_copy(c):
        here = pl.ds(pl.multiple_of(c * part, part), part)
        return pltpu.make_async_copy(stage.at[lax.rem(c, 2)], grads_hbm.at[here, :], stage_sem.at[lax.rem(c, 2)])

    def put(c, carry):
        @pl.when(c >= 2)
        def _():
            stage_copy(c - 2).wait()

        stage[lax.rem(c, 2)] = grads_sum[pl.ds(pl.multiple_of(c * part, part), part), :].astype(bf16)
        stage_copy(c).start()
        return carry

    parts = 3 * hidden // part
    lax.fori_loop(0, parts, put, 0)
    group.end()
    for c in range(2):
        stage_copy(c).wait()


def mlp_back(own, weights, scales, up_raw, gate_raw, middle_rows, d_middle, start_unit, branch, rates, size, steps, collective_id):
    tokens, hidden = up_raw.shape
    rows = own.shape[0] // steps
    return pl.pallas_call(
        functools.partial(mlp_back_kernel, size, steps),
        out_shape=[
            jax.ShapeDtypeStruct((own.shape[0], D), bf16),
            jax.ShapeDtypeStruct((own.shape[0], D), f32),
            jax.ShapeDtypeStruct((1, D), f32),
            jax.ShapeDtypeStruct((2, hidden), f32),
            jax.ShapeDtypeStruct((3 * hidden, D), bf16),
        ],
        in_specs=[VMEM_WHOLE, ANYWHERE, VMEM_WHOLE, ANYWHERE, ANYWHERE, VMEM_WHOLE] + [ANYWHERE] * 3 + [VMEM_WHOLE],
        out_specs=[VMEM_WHOLE] * 4 + [ANYWHERE],
        scratch_shapes=[
            pltpu.VMEM((2, min(256, hidden), D), bf16),
            pltpu.SemaphoreType.DMA((2,)),
            pltpu.VMEM((2, 3, rows // LATE_PARTS, D), f32),
            pltpu.SemaphoreType.DMA((2, 3)),
            pltpu.VMEM((own.shape[0], D), f32),
            pltpu.VMEM((size, own.shape[0], D), bf16),
            pltpu.VMEM((tokens - own.shape[0], hidden), bf16),
            pltpu.VMEM((tokens - own.shape[0], 2 * hidden), bf16),
            pltpu.VMEM((3 * hidden, D), f32),
        ]
        + weight_scratch(hidden, 3)
        + [
            pltpu.VMEM((2, rows, hidden), f32),
            pltpu.VMEM((2, rows, hidden), f32),
            pltpu.SemaphoreType.DMA((2, 2)),
        ]
        + gather_sems(size, steps)
        + settle_scratch(size, steps, tokens),
        compiler_params=remote_params(collective_id),
        cost_estimate=pl.CostEstimate(flops=6 * tokens * hidden * D, bytes_accessed=tokens * D * 24, transcendentals=tokens * hidden),
        name="mlp_back",
    )(own, weights, scales, up_raw, gate_raw, middle_rows, d_middle, start_unit, branch, rates)


def gather_project_kernel(size, steps, first_row, own_ref, w_hbm, out_ref, rows_ref, w_ref, w_sem, *scratch):
    tokens = own_ref.shape[0] * size
    group = Group(size, steps, tokens)
    copies = weight_copies(w_hbm, [w_ref], w_sem, first_row)
    copies[0].start()
    group.meet()

    def compute(device, s, i):
        first = pl.multiple_of(device * group.own + s * group.rows, group.rows)
        out_ref[pl.ds(first, group.rows), :] = nt(group.piece(rows_ref, device, s)[...], w_ref[...]).astype(bf16)

    group.run(compute, gather=(own_ref, rows_ref, scratch[0], scratch[1]), ready=copies)
    group.end()


def gather_project(own, weights, width, first_row, size, steps, collective_id, name):
    tokens = own.shape[0] * size
    return pl.pallas_call(
        functools.partial(gather_project_kernel, size, steps, first_row),
        out_shape=[
            jax.ShapeDtypeStruct((tokens, width), bf16),
            jax.ShapeDtypeStruct((size, own.shape[0], D), bf16),
        ],
        in_specs=[VMEM_WHOLE, ANYWHERE],
        out_specs=[VMEM_WHOLE, VMEM_WHOLE],
        scratch_shapes=weight_scratch(width) + gather_sems(size, steps),
        compiler_params=remote_params(collective_id),
        cost_estimate=pl.CostEstimate(flops=2 * tokens * width * D, bytes_accessed=tokens * D * 4, transcendentals=0),
        name=name,
    )(own, weights)


def start_sum_kernel(
    size, steps, rows_ref, w_hbm, base_ref, unit_ref, inv_ref, operand_hbm, attended_hbm, d_attn_hbm,
    pieces, grads_ref, operand_ref, attended_ref, d_attn_ref, late_sem, w_ref, w_sem, total_ref, *scratch
):
    tokens = rows_ref.shape[0]
    narrow = pieces.shape[2]
    group = Group(size, steps, tokens)
    copies = weight_copies(w_hbm, [w_ref], w_sem, 0)
    copies[0].start()
    late = [
        pltpu.make_async_copy(source, target, late_sem.at[i])
        for i, (source, target) in enumerate(
            ((operand_hbm, operand_ref), (attended_hbm, attended_ref), (d_attn_hbm, d_attn_ref))
        )
    ]
    for copy in late:
        copy.start()
    group.meet()
    copies[0].wait()

    def compute(device, s, i):
        first = pl.multiple_of(device * group.own + s * group.rows, group.rows)
        return nn(rows_ref[pl.ds(first, group.rows), :], w_ref[...])

    def after(s):
        here = pl.ds(pl.multiple_of(s * group.rows, group.rows), group.rows)
        back = normalize_back(unit_ref[here, :], inv_ref[here, 0:1], base_ref[here, :] + total_ref[here, :])
        for device in range(size):
            pieces[device, here, :] = back[:, device * narrow : (device + 1) * narrow].astype(bf16)

    group.run(compute, settle=(total_ref, *scratch), remote_first=True, after=after)

    for copy in late:
        copy.wait()
    for c in range(3):
        here = slice(c * narrow, (c + 1) * narrow)
        grads_ref[here, :] = tn(rows_ref[:, here], operand_ref[...]).astype(bf16)
        group.end(c * steps // 4, (c + 1) * steps // 4)
    out_sum = jnp.zeros((narrow, D), f32)
    for d in range(size):
        out_sum += tn(attended_ref[d * group.own : (d + 1) * group.own, :], d_attn_ref[d])
    grads_ref[3 * narrow :, :] = out_sum.astype(bf16)
    group.end(3 * steps // 4, steps)


def start_sum(rows, weights, base, unit_rows, inverse, operand, attended, d_attn_rows, size, steps, collective_id):
    tokens, depth = rows.shape
    own, narrow = tokens // size, D // size
    return pl.pallas_call(
        functools.partial(start_sum_kernel, size, steps),
        out_shape=[jax.ShapeDtypeStruct((size, own, narrow), bf16), jax.ShapeDtypeStruct((4 * narrow, D), bf16)],
        in_specs=[VMEM_WHOLE, ANYWHERE] + [VMEM_WHOLE] * 3 + [ANYWHERE] * 3,
        out_specs=[VMEM_WHOLE] * 2,
        scratch_shapes=[
            pltpu.VMEM(operand.shape, bf16),
            pltpu.VMEM(attended.shape, bf16),
            pltpu.VMEM(d_attn_rows.shape, bf16),
            pltpu.SemaphoreType.DMA((3,)),
        ]
        + weight_scratch(depth)
        + [
            pltpu.VMEM((own, D), f32),
        ]
        + settle_scratch(size, steps, tokens),
        compiler_params=remote_params(collective_id),
        cost_estimate=pl.CostEstimate(flops=2 * tokens * depth * D, bytes_accessed=tokens * D * 8, transcendentals=0),
        name="start_sum",
    )(rows, weights, base, unit_rows, inverse, operand, attended, d_attn_rows)


def tail_plan(devices, rows):
    lines = min(4, devices)
    columns = devices // lines
    cuts = 2 if rows % (devices * 32) == 0 else 1
    return lines, columns, cuts, rows // (devices * cuts)


def tail_sum_kernel(
    devices, size, late_ref, home_ref, rates_ref, small_ref, hidden_ref, back_ref,
    late_out, home_out, small_out, hidden_out, back_out,
    y_land, y_sum, z_land, rate_parts, rate_land, pack, small_land,
    a_send, a_recv, b_send, b_recv, c_send, c_recv, d_send, d_recv, m_send, m_recv, s_send, s_recv, h_send, h_recv, g_send, g_recv, e_send, e_recv, f_send, f_recv, local_sem
):
    dp, me = lax.axis_index("dp"), lax.axis_index("mp")
    lines, columns, cuts, rows = tail_plan(devices, late_ref.shape[0])
    a, b = dp // columns, lax.rem(dp, columns)
    span = lines * rows
    narrow = rate_parts.shape[2]
    chunks = [(late_ref, late_out, q) for q in range(cuts)]
    pieces = e_send.shape[0]
    height = home_ref.shape[0] // pieces

    def remote(source, target, send, receive, device):
        return pltpu.make_async_remote_copy(
            src_ref=source, dst_ref=target, send_sem=send, recv_sem=receive, device_id=device, device_id_type=MESH
        )

    def peer(j):
        return lax.rem(dp + j, devices)

    def column(j):
        return lax.rem(b + j, columns)

    def line(j):
        return lax.rem(a + j, lines)

    barrier = pltpu.get_barrier_semaphore()

    def greet(j, carry):
        pl.semaphore_signal(barrier, inc=1, device_id=(peer(j), me), device_id_type=MESH)
        return carry

    lax.fori_loop(1, devices, greet, 0)
    for j in range(1, size):
        pl.semaphore_signal(barrier, inc=1, device_id=(dp, lax.rem(me + j, size)), device_id_type=MESH)
    pl.semaphore_wait(barrier, devices - 1 + size - 1)

    def part(ref, q, col):
        return ref.at[pl.ds(pl.multiple_of((q * columns + col) * span, span), span), :]

    def to_column(c, j):
        ref, _, q = chunks[c]
        return remote(part(ref, q, column(j)), y_land.at[c, b], a_send.at[c, j], a_recv.at[c, b], (a * columns + column(j), me))

    def from_column(c, j):
        here = y_land.at[c, column(j)]
        return remote(here, here, a_send.at[c, j], a_recv.at[c, column(j)], (a * columns + column(j), me))

    def to_line(c, j):
        there = pl.ds(pl.multiple_of(line(j) * rows, rows), rows)
        return remote(y_sum.at[c, there, :], z_land.at[c, a], b_send.at[c, j], b_recv.at[c, a], (line(j) * columns + b, me))

    def from_line(c, j):
        here = z_land.at[c, line(j)]
        return remote(here, here, b_send.at[c, j], b_recv.at[c, line(j)], (line(j) * columns + b, me))

    def sum_of(c, col, row):
        _, out, q = chunks[c]
        return out.at[(q * columns + col) * lines + row]

    def back_line(c, j):
        here = sum_of(c, b, a)
        return remote(here, here, c_send.at[c, j], c_recv.at[c, a], (line(j) * columns + b, me))

    def back_line_got(c, j):
        here = sum_of(c, b, line(j))
        return remote(here, here, c_send.at[c, j], c_recv.at[c, line(j)], (line(j) * columns + b, me))

    def back_column(c, i, j):
        here = sum_of(c, b, line(i))
        return remote(here, here, d_send.at[c, i, j], d_recv.at[c, line(i), b], (a * columns + column(j), me))

    def back_column_got(c, i, j):
        here = sum_of(c, column(j), line(i))
        return remote(here, here, d_send.at[c, i, j], d_recv.at[c, line(i), column(j)], (a * columns + column(j), me))

    def home(col, row, p):
        return home_out.at[row * columns + col, pl.ds(p * height, height), :]

    def home_line(p, j):
        return remote(
            home_ref.at[pl.ds(p * height, height), :], home(b, a, p), e_send.at[p, j], e_recv.at[p, a], (line(j) * columns + b, me)
        )

    def home_line_got(p, j):
        here = home(b, line(j), p)
        return remote(here, here, e_send.at[p, j], e_recv.at[p, line(j)], (line(j) * columns + b, me))

    def home_column(p, i, j):
        here = home(b, line(i), p)
        source = here if i else home_ref.at[pl.ds(p * height, height), :]
        return remote(source, here, f_send.at[p, i, j], f_recv.at[p, line(i), b], (a * columns + column(j), me))

    def home_column_got(p, i, j):
        here = home(column(j), line(i), p)
        return remote(here, here, f_send.at[p, i, j], f_recv.at[p, line(i), column(j)], (a * columns + column(j), me))

    def home_pass(p):
        for i in range(1, lines):
            home_line_got(p, i).wait_recv()
            for j in range(1, columns):
                home_column(p, i, j).start()

    def rate_copy(j):
        device = lax.rem(me + j, size)
        return remote(rate_parts.at[device], rate_land.at[me], m_send.at[j - 1], m_recv.at[me], (dp, device))

    for c in range(len(chunks)):
        for j in range(1, columns):
            to_column(c, j).start()
    for p in range(pieces):
        for j in range(1, lines):
            home_line(p, j).start()
        for j in range(1, columns):
            home_column(p, 0, j).start()
    stay = [
        pltpu.make_async_copy(source, target, local_sem.at[i])
        for i, (source, target) in enumerate(
            ((home_ref, home_out.at[dp]), (hidden_ref.at[me], hidden_out.at[me]), (back_ref.at[me], back_out.at[me]))
        )
    ]
    for copy in stay:
        copy.start()
    for d in range(size):
        rate_parts[d, 0:2, :] = rates_ref[:, d * narrow : (d + 1) * narrow]
    for j in range(1, size):
        rate_copy(j).start()

    def deal(j):
        device = lax.rem(me + j, size)
        return [
            remote(source.at[device], target.at[me], send.at[j - 1], receive.at[me], (dp, device))
            for source, target, send, receive in ((hidden_ref, hidden_out, h_send, h_recv), (back_ref, back_out, g_send, g_recv))
        ]

    def dealt(j):
        device = lax.rem(me + j, size)
        return [
            remote(target.at[device], target.at[device], send.at[j - 1], receive.at[device], (dp, device))
            for target, send, receive in ((hidden_out, h_send, h_recv), (back_out, g_send, g_recv))
        ]

    for j in range(1, size):
        for copy in deal(j):
            copy.start()

    rates = rate_parts[me]
    for j in range(1, size):
        source = lax.rem(me + j, size)
        remote(rate_land.at[source], rate_land.at[source], m_send.at[j - 1], m_recv.at[source], (dp, source)).wait_recv()
        rates = rates + rate_land[source]
    pack[...] = small_ref[...]
    pack[3:5, :narrow] = rates[0:2, :]

    def small_copy(j):
        return remote(pack, small_land.at[dp], s_send.at[j - 1], s_recv.at[dp], (peer(j), me))

    def small_give(j, carry):
        small_copy(j).start()
        return carry

    lax.fori_loop(1, devices, small_give, 0)

    def settle_column(c):
        ref, _, q = chunks[c]
        for j in range(1, columns):
            from_column(c, j).wait_recv()

        def add(i, carry):
            here = pl.ds(pl.multiple_of(i * rows, rows), rows)
            own = pl.ds(pl.multiple_of((q * columns + b) * span + i * rows, rows), rows)
            total = ref[own, :].astype(f32)
            for j in range(1, columns):
                total = total + y_land[c, column(j), here, :].astype(f32)
            y_sum[c, here, :] = total.astype(bf16)
            return carry

        lax.fori_loop(0, lines, add, 0)
        for j in range(1, lines):
            to_line(c, j).start()

    def settle_line(c):
        for j in range(1, lines):
            from_line(c, j).wait_recv()
        total = y_sum[c, pl.ds(pl.multiple_of(a * rows, rows), rows), :].astype(f32)
        for j in range(1, lines):
            total = total + z_land[c, line(j)].astype(f32)
        sum_of(c, b, a)[...] = total.astype(bf16)
        for j in range(1, lines):
            back_line(c, j).start()
        for j in range(1, columns):
            back_column(c, 0, j).start()

    def pass_on(c):
        for i in range(1, lines):
            back_line_got(c, i).wait_recv()
            for j in range(1, columns):
                back_column(c, i, j).start()

    count = len(chunks)
    for c in range(count):
        settle_column(c)
    for p in range(pieces - 1):
        home_pass(p)
    for step in range(count + 2):
        if 1 <= step <= count:
            settle_line(step - 1)
        if step == 1:
            home_pass(pieces - 1)
        if step >= 2:
            pass_on(step - 2)

    def small_take(j, total):
        source = peer(j)
        remote(small_land.at[source], small_land.at[source], s_send.at[j - 1], s_recv.at[source], (source, me)).wait_recv()
        return total + small_land[source]

    small_out[...] = lax.fori_loop(1, devices, small_take, pack[...])
    for c in range(count):
        for i in range(lines):
            for j in range(1, columns):
                back_column_got(c, i, j).wait_recv()
                back_column(c, i, j).wait_send()
        for j in range(1, lines):
            back_line(c, j).wait_send()
            to_line(c, j).wait_send()
        for j in range(1, columns):
            to_column(c, j).wait_send()
    for p in range(pieces):
        for i in range(lines):
            for j in range(1, columns):
                home_column_got(p, i, j).wait_recv()
                home_column(p, i, j).wait_send()
        for j in range(1, lines):
            home_line(p, j).wait_send()

    def finish(j, carry):
        small_copy(j).wait_send()
        return carry

    lax.fori_loop(1, devices, finish, 0)
    for j in range(1, size):
        rate_copy(j).wait_send()
        for copy in dealt(j):
            copy.wait_recv()
        for copy in deal(j):
            copy.wait_send()
    for copy in stay:
        copy.wait()


def tail_sum(late, home, rates, small, hidden, back, devices, size, collective_id):
    lines, columns, cuts, rows = tail_plan(devices, late.shape[0])
    narrow = D // size
    chunks = cuts
    pieces = next(p for p in (4, 3, 1) if home.shape[0] % (16 * p) == 0)
    dma = pltpu.SemaphoreType.DMA
    total = jax.ShapeDtypeStruct((late.shape[0] // rows, rows, D), bf16)
    homes = jax.ShapeDtypeStruct((devices, *home.shape), bf16)
    return pl.pallas_call(
        functools.partial(tail_sum_kernel, devices, size),
        out_shape=[total, homes] + [jax.ShapeDtypeStruct(x.shape, x.dtype) for x in (small, hidden, back)],
        in_specs=[VMEM_WHOLE] * 6,
        out_specs=[VMEM_WHOLE, ANYWHERE, VMEM_WHOLE, ANYWHERE, ANYWHERE],
        scratch_shapes=[
            pltpu.VMEM((chunks, columns, lines * rows, D), bf16),
            pltpu.VMEM((chunks, lines * rows, D), bf16),
            pltpu.VMEM((chunks, lines, rows, D), bf16),
            pltpu.VMEM((size, 8, narrow), f32),
            pltpu.VMEM((size, 8, narrow), f32),
            pltpu.VMEM(small.shape, f32),
            pltpu.VMEM((devices, *small.shape), f32),
            dma((chunks, columns)), dma((chunks, columns)),
            dma((chunks, lines)), dma((chunks, lines)),
            dma((chunks, lines)), dma((chunks, lines)),
            dma((chunks, lines, columns)), dma((chunks, lines, columns)),
            dma((size - 1,)), dma((size,)),
            dma((devices - 1,)), dma((devices,)),
            dma((size - 1,)), dma((size,)),
            dma((size - 1,)), dma((size,)),
            dma((pieces, lines)), dma((pieces, lines)),
            dma((pieces, lines, columns)), dma((pieces, lines, columns)),
            dma((3,)),
        ],
        compiler_params=remote_params(collective_id),
        cost_estimate=pl.CostEstimate(flops=0, bytes_accessed=late.shape[0] * D * 16, transcendentals=0),
        name="tail_sum",
    )(late, home, rates, small, hidden, back)


def optimizer_kernel(
    counts, index_ref, attn_ref, mlp_ref, m_ref, f_ref, s_ref, mo_ref, fo_ref, so_ref, go_ref
):
    group = m_ref.shape[0]
    for j in range(group):
        slot = pl.program_id(0) * group + j
        block, live = index_ref[slot, 0], index_ref[slot, 1]

        @pl.when(live == 0)
        def _():
            for ref in (mo_ref, fo_ref, so_ref, go_ref):
                ref[j] = jnp.zeros_like(m_ref[j])

        for ref, first, last in (
            (attn_ref, 0, counts[0]),
            (mlp_ref, counts[0], sum(counts)),
        ):

            @pl.when(jnp.logical_and(live == 1, jnp.logical_and(block >= first, block < last)))
            def _():
                gradient = ref[block - first].astype(f32)
                stepped, first_new, second_new = adam_update(
                    m_ref[j], gradient, f_ref[j], s_ref[j], WEIGHT_DECAY, LEARN_RATE
                )
                go_ref[j] = gradient
                fo_ref[j] = first_new
                so_ref[j] = second_new
                mo_ref[j] = stepped * lax.rsqrt(jnp.sum(stepped * stepped, axis=-1, keepdims=True) + EPSILON)


def optimizer(index, attn_grads, mlp_grads, masters, firsts, seconds):
    slots, height, _ = masters.shape
    group = math.gcd(slots, 4)
    grads = [g.reshape(-1, height, D) for g in (attn_grads, mlp_grads)]
    block = pl.BlockSpec((group, height, D), lambda i, ref: (i, 0, 0))
    return pl.pallas_call(
        functools.partial(optimizer_kernel, tuple(g.shape[0] for g in grads)),
        grid_spec=pltpu.PrefetchScalarGridSpec(
            num_scalar_prefetch=1,
            grid=(slots // group,),
            in_specs=[pl.BlockSpec(memory_space=pltpu.VMEM)] * 2 + [block] * 3,
            out_specs=[block] * 4,
        ),
        out_shape=[jax.ShapeDtypeStruct(masters.shape, f32)] * 4,
        compiler_params=pltpu.CompilerParams(vmem_limit_bytes=GRANT),
        cost_estimate=pl.CostEstimate(flops=20 * masters.size, bytes_accessed=30 * masters.size, transcendentals=0),
        name="optimizer",
    )(index, *grads, masters, firsts, seconds)


def collect_kernel(count, places_ref, slots_hbm, out_ref, sems):
    def copy(b):
        return pltpu.make_async_copy(slots_hbm.at[places_ref[b]], out_ref.at[b], sems.at[b])

    def start(b, carry):
        copy(b).start()
        return carry

    def wait(b, carry):
        copy(b).wait()
        return carry

    lax.fori_loop(0, count, start, 0)
    lax.fori_loop(0, count, wait, 0)


def collect(places, slots):
    count, shape = places.shape[0], slots.shape[1:]
    return pl.pallas_call(
        functools.partial(collect_kernel, count),
        grid_spec=pltpu.PrefetchScalarGridSpec(
            num_scalar_prefetch=1,
            grid=(1,),
            in_specs=[pl.BlockSpec(memory_space=pl.ANY)],
            out_specs=pl.BlockSpec(memory_space=pltpu.VMEM),
            scratch_shapes=[pltpu.SemaphoreType.DMA((count,))],
        ),
        out_shape=jax.ShapeDtypeStruct((count, *shape), bf16),
        compiler_params=pltpu.CompilerParams(vmem_limit_bytes=GRANT),
        cost_estimate=pl.CostEstimate(flops=0, bytes_accessed=4 * count * math.prod(shape), transcendentals=0),
        name="collect",
    )(places, slots)


def spread_plan(devices, slots):
    lines = min(4, devices)
    columns = devices // lines
    across = slots * 5 // 32 if columns == 2 else 0
    cuts = next(q for q in (9, 3, 2, 1) if (slots - across) % q == 0)
    return lines, columns, across, cuts


def spread_kernel(
    devices, size, slots, height, slots_ref, x_ref, cot_ref, gains_ref,
    all_ref, x_all, cot_all, gains_all, cos_ref, sin_ref, start_ref, inv_ref, gains_land, x_own_ref,
    z_send, z_recv, y_send, y_recv, e_send, e_recv, x_send, x_recv, c_send, c_recv, w_send, w_recv, local_sem
):
    lines, columns, across, cuts = spread_plan(devices, slots)
    dp, me = lax.axis_index("dp"), lax.axis_index("mp")
    a, b = dp // columns, lax.rem(dp, columns)
    chips = size // 2
    chip, core = me // 2, lax.rem(me, 2)
    partner = me + 1 - 2 * core
    tokens, narrow = x_ref.shape
    own = tokens // size
    x_steps = x_recv.shape[1]
    x_rows = tokens // x_steps
    cut_rows = (slots - across) * height // cuts
    has_left, has_right = a > 0, a < lines - 1

    def remote(source, target, send, receive, device):
        return pltpu.make_async_remote_copy(
            src_ref=source, dst_ref=target, send_sem=send, recv_sem=receive, device_id=device, device_id_type=MESH
        )

    def column(j):
        return lax.rem(b + j, columns)

    def other(k, which):
        return 2 * lax.rem(chip + k, chips) + which

    def mp_peer(j):
        return lax.rem(me + j, size)

    barrier = pltpu.get_barrier_semaphore()

    def greet(device):
        pl.semaphore_signal(barrier, inc=1, device_id=device, device_id_type=MESH)

    for j in range(1, columns):
        greet((a * columns + column(j), me))
    for j in range(1, size):
        greet((dp, mp_peer(j)))

    @pl.when(has_left)
    def _():
        greet((dp - columns, me))

    @pl.when(has_right)
    def _():
        greet((dp + columns, me))

    pl.semaphore_wait(
        barrier, columns - 1 + size - 1 + has_left.astype(jnp.int32) + has_right.astype(jnp.int32)
    )

    items = cuts + (columns if across else 0)

    def region(ref, line, c, row=None):
        if c < cuts:
            source, first, count = line * columns + b, across * height + c * cut_rows, cut_rows
        else:
            source, first, count = line * columns + (c - cuts), 0, across * height
        return ref.at[source, pl.ds(first, count), :]

    def own_part(c):
        first, count = (across * height + c * cut_rows, cut_rows) if c < cuts else (0, across * height)
        return slots_ref.at[pl.ds(first, count), :]

    def along(line, c, to_right, source=None):
        here = region(all_ref, line, c)
        side = 1 if to_right else 0
        device = (dp + columns if to_right else dp - columns, me)
        return remote(here if source is None else source, here, z_send.at[line, side, c], z_recv.at[line, c], device)

    def over(line, c, j, source=None):
        here = region(all_ref, line, c)
        return remote(
            here if source is None else source, here, y_send.at[line, j, c], y_recv.at[line, b, c],
            (a * columns + column(j), me),
        )

    def over_got(line, column_from, c):
        first = across * height + c * cut_rows
        here = all_ref.at[line * columns + column_from, pl.ds(first, cut_rows), :]
        return remote(here, here, y_send.at[line, 1, c], y_recv.at[line, column_from, c], (dp, partner))

    def early(j):
        here = all_ref.at[dp, pl.ds(0, across * height), :]
        return remote(own_part(cuts), here, e_send.at[j], e_recv.at[b], (a * columns + column(j), me))

    def early_got(column_from):
        here = all_ref.at[a * columns + column_from, pl.ds(0, across * height), :]
        return remote(here, here, e_send.at[1], e_recv.at[column_from], (dp, partner))

    def x_piece(ref, s):
        return ref.at[pl.ds(s * x_rows, x_rows), :]

    def x_own(s, k):
        device = (dp, partner) if k == 0 else (dp, other(k, core))
        return remote(x_piece(x_ref, s), x_piece(x_all.at[me], s), x_send.at[k, s], x_recv.at[me, s], device)

    def x_forward(s, k):
        source = other(k, core)
        here = x_piece(x_all.at[source], s)
        return remote(here, here, x_send.at[chips + k - 1, s], x_recv.at[source, s], (dp, partner))

    def x_got(s, source):
        here = x_piece(x_all.at[source], s)
        return remote(here, here, x_send.at[0, s], x_recv.at[source, s], (dp, partner))

    def cot_own(j):
        device = mp_peer(j)
        rows = pl.ds(pl.multiple_of(device * own, own), own)
        return remote(cot_ref.at[rows, :], cot_all.at[me], c_send.at[j - 1], c_recv.at[me], (dp, device))

    def cot_got(j):
        here = cot_all.at[mp_peer(j)]
        return remote(here, here, c_send.at[j - 1], c_recv.at[mp_peer(j)], (dp, partner))

    def gains_own(j):
        return remote(gains_ref, gains_land.at[me], w_send.at[j - 1], w_recv.at[me], (dp, mp_peer(j)))

    if across:
        for j in range(1, columns):
            early(j).start()
    for j in range(1, size):
        gains_own(j).start()
    gains_land[me] = gains_ref[...]
    for c in range(cuts):
        for side, there in ((False, has_left), (True, has_right)):

            @pl.when(there)
            def _():
                along(a, c, side, own_part(c)).start()

        for j in range(1, columns):
            over(a, c, j, own_part(c)).start()
    for s in range(x_steps):
        for k in range(chips):
            x_own(s, (k + 1) % chips).start()
    for j in range(1, size):
        cot_own(j).start()
    local = [
        pltpu.make_async_copy(slots_ref, all_ref.at[dp], local_sem.at[0]),
        pltpu.make_async_copy(x_ref, x_all.at[me], local_sem.at[1]),
        pltpu.make_async_copy(
            cot_ref.at[pl.ds(pl.multiple_of(me * own, own), own), :], cot_all.at[me], local_sem.at[2]
        ),
    ]
    for copy in local:
        copy.start()
    if across:
        for j in range(1, columns):
            early_got(column(j)).wait_recv()
        for c in range(cuts, items):
            for side, there in ((False, has_left), (True, has_right)):
                mine = b == c - cuts

                @pl.when(jnp.logical_and(there, mine))
                def _():
                    along(a, c, side, own_part(c)).start()

                @pl.when(jnp.logical_and(there, jnp.logical_not(mine)))
                def _():
                    along(a, c, side).start()

    for s in range(x_steps):
        for k in range(1, chips):
            x_got(s, other(k, core)).wait_recv()
            x_forward(s, k).start()

    rope_rows = min(256, tokens)

    def rope_table(i, carry):
        here = pl.ds(pl.multiple_of(i * rope_rows, rope_rows), rope_rows)
        lane = lax.broadcasted_iota(jnp.int32, (rope_rows, LANES), 1)
        position = (lax.broadcasted_iota(jnp.int32, (rope_rows, LANES), 0) + i * rope_rows).astype(f32)
        j = lane % (HD // 2)
        angle = position * jnp.exp(j.astype(f32) * (-2.0 * math.log(10000.0) / HD))
        cos_ref[here, :] = jnp.cos(angle)
        sin_ref[here, :] = jnp.where(lane % HD < HD // 2, -1.0, 1.0) * jnp.sin(angle)
        return carry

    lax.fori_loop(0, tokens // rope_rows, rope_table, 0)

    for hop in range(1, lines):
        for c in range(items):
            for to_right in (True, False):
                line = a - hop if to_right else a + hop
                there = line >= 0 if to_right else line < lines
                onward = has_right if to_right else has_left

                @pl.when(there)
                def _():
                    along(line, c, to_right).wait_recv()

                    @pl.when(onward)
                    def _():
                        along(line, c, to_right).start()

                    if c < cuts:
                        for j in range(1, columns):
                            over(line, c, j).start()

    for s in range(x_steps):
        x_got(s, partner).wait_recv()
        for k in range(1, chips):
            x_got(s, other(k, 1 - core)).wait_recv()
    local[1].wait()
    mine = pltpu.make_async_copy(
        x_all.at[:, pl.ds(pl.multiple_of(me * own, own), own), :], x_own_ref, local_sem.at[1]
    )
    mine.start()
    mine.wait()
    start_rows = min(128, own)

    def start_part(i, carry):
        here = pl.ds(pl.multiple_of(i * start_rows, start_rows), start_rows)
        x = jnp.concatenate([x_own_ref[d, here, :] for d in range(size)], axis=1).astype(f32)
        unit_rows, inverse = normalize(x)
        start_ref[here, :] = unit_rows
        inv_ref[here, :] = jnp.broadcast_to(inverse, (start_rows, LANES))
        return carry

    lax.fori_loop(0, own // start_rows, start_part, 0)

    for line in range(lines):
        for c in range(cuts):
            for j in range(1, columns):
                over_got(line, column(j), c).wait_recv()
    for j in range(1, size):
        cot_got(j).wait_recv()
        here = gains_land.at[mp_peer(j)]
        remote(here, here, w_send.at[j - 1], w_recv.at[mp_peer(j)], (dp, partner)).wait_recv()
        gains_own(j).wait_send()
    for d in range(size):
        gains_all[:, d * narrow : (d + 1) * narrow] = gains_land[d]
    local[0].wait()
    local[2].wait()
    if across:
        for j in range(1, columns):
            early(j).wait_send()
    for s in range(x_steps):
        for k in range(chips):
            x_own(s, k).wait_send()
        for k in range(1, chips):
            x_forward(s, k).wait_send()
    for j in range(1, size):
        cot_own(j).wait_send()
    for line in range(lines):
        for c in range(items):
            @pl.when(jnp.logical_and(has_right, line <= a))
            def _():
                along(line, c, True).wait_send()

            @pl.when(jnp.logical_and(has_left, line >= a))
            def _():
                along(line, c, False).wait_send()

            if c < cuts:
                for j in range(1, columns):
                    over(line, c, j).wait_send()


def spread(slots_low, hidden_in, cotangent, gains, devices, size, collective_id):
    slots, height, _ = slots_low.shape
    tokens, narrow = hidden_in.shape
    lines, columns, across, cuts = spread_plan(devices, slots)
    items = cuts + (columns if across else 0)
    chips = size // 2
    x_steps = 4
    dma = pltpu.SemaphoreType.DMA
    return pl.pallas_call(
        functools.partial(spread_kernel, devices, size, slots, height),
        out_shape=[
            jax.ShapeDtypeStruct((devices, slots * height, D), bf16),
            jax.ShapeDtypeStruct((size, tokens, narrow), bf16),
            jax.ShapeDtypeStruct((size, tokens // size, narrow), bf16),
            jax.ShapeDtypeStruct((gains.shape[0], D), f32),
            jax.ShapeDtypeStruct((tokens, LANES), f32),
            jax.ShapeDtypeStruct((tokens, LANES), f32),
            jax.ShapeDtypeStruct((tokens // size, D), f32),
            jax.ShapeDtypeStruct((tokens // size, LANES), f32),
        ],
        in_specs=[VMEM_WHOLE] * 4,
        out_specs=[ANYWHERE] * 3 + [VMEM_WHOLE] * 5,
        scratch_shapes=[
            pltpu.VMEM((size, *gains.shape), f32),
            pltpu.VMEM((size, tokens // size, narrow), bf16),
            dma((lines, 2, items)),
            dma((lines, items)),
            dma((lines, columns, cuts)),
            dma((lines, columns, cuts)),
            dma((columns,)),
            dma((columns,)),
            dma((2 * chips - 1, x_steps)),
            dma((size, x_steps)),
            dma((size - 1,)),
            dma((size,)),
            dma((size - 1,)),
            dma((size,)),
            dma((3,)),
        ],
        compiler_params=remote_params(collective_id),
        cost_estimate=pl.CostEstimate(flops=0, bytes_accessed=devices * slots * height * D * 4, transcendentals=0),
        name="spread",
    )(slots_low.reshape(slots * height, D), hidden_in, cotangent, gains)


def shards(
    n_dp,
    hidden_in,
    cotangent,
    owners,
    masters,
    firsts,
    seconds,
    width_gains,
    width_first,
    width_second,
    hidden_gains,
    hidden_first,
    hidden_second,
):
    tokens = hidden_in.shape[0]
    narrow = hidden_in.shape[1]
    slot_count = masters.shape[1]
    block_rows = masters.shape[2]
    blocks = owners.shape[0]
    hidden_local = hidden_gains.shape[1]
    dp_index = lax.axis_index("dp")
    mp_index = lax.axis_index("mp")
    own_tokens = tokens // (D // narrow)

    block_order = jnp.arange(blocks)
    same_owner = owners[:, None] == owners[None, :]
    slot_rank = jnp.sum(
        jnp.logical_and(same_owner, block_order[None, :] < block_order[:, None]).astype(jnp.int32),
        axis=1,
    )
    owned_mask = owners == dp_index
    in_use = jnp.arange(slot_count) < jnp.sum(owned_mask.astype(jnp.int32))
    slot_block = jnp.sum(
        jnp.where(
            jnp.logical_and(owned_mask[None, :], slot_rank[None, :] == jnp.arange(slot_count)[:, None]),
            block_order[None, :],
            0,
        ),
        axis=1,
    )

    size = D // narrow
    all_slots, x_all, cot_all, gains, cosine, sine, start_unit, start_inv = spread(
        masters[0].astype(bf16), hidden_in, cotangent, width_gains, n_dp, size, 6
    )
    weights = collect(
        owners * slot_count + slot_rank, all_slots.reshape(n_dp * slot_count, block_rows, D)
    ).reshape(blocks * block_rows, D)
    operand, queries, keys, values, q_turned, k_turned = project(x_all, weights, width_gains, cosine, sine)
    attended, mixed = attend(queries, keys, values)

    attn_branch, middle, middle_low = attention_sum(
        attended, weights, start_unit, gains, 3 * narrow, size, STEPS, 1
    )
    out_rows, middle_rows, up_raw, gate_raw, d_mlp, d_middle, g_rate_mlp = mlp(
        middle_low, weights, hidden_gains, middle, cot_all, gains, size, STEPS, 2
    )
    d_attn, d_start, g_rate_attn, g_scales, g_mlp = mlp_back(
        d_mlp, weights, hidden_gains, up_raw, gate_raw, middle_rows, d_middle, start_unit, attn_branch, gains,
        size, MLP_STEPS, 3,
    )
    d_attn, g_mlp = lax.optimization_barrier((d_attn, g_mlp))
    mlp_home = lax.psum_scatter(g_mlp, "dp", scatter_dimension=0, tiled=True)
    d_attended, attn_grad_rows = gather_project(d_attn, weights, narrow, 3 * narrow, size, STEPS, 4, "attention_gather")
    d_queries, d_keys, d_values = attend_back(queries, keys, values, mixed, d_attended)
    grads_qkv, g_qk = project_back(
        d_queries, d_keys, d_values, q_turned, k_turned, width_gains, cosine, sine
    )
    grad_pieces, g_attn = start_sum(
        grads_qkv, weights, d_start, start_unit, start_inv, operand, attended, attn_grad_rows, size, STEPS, 5
    )
    small = jnp.zeros((8, hidden_local), f32)
    small = small.at[0:1, :narrow].set(g_qk).at[1:3, :].set(g_scales)
    attn_grads, mlp_grads, small, hidden_out, grad_in = tail_sum(g_attn, mlp_home, jnp.concatenate([g_rate_attn, g_rate_mlp], axis=0), small, out_rows, grad_pieces, n_dp, size, 7)
    hidden_out = hidden_out.reshape(tokens, narrow)
    grad_in = grad_in.reshape(tokens, narrow).astype(f32)
    width_total = jnp.concatenate([small[0:1, :narrow], small[3:5, :narrow]], axis=0)
    hidden_total = small[1:3, :]
    index = jnp.stack([slot_block, in_use.astype(jnp.int32)], axis=1)
    masters_new, firsts_new, seconds_new, weight_grads = [
        part[None]
        for part in optimizer(index, attn_grads, mlp_grads, masters[0], firsts[0], seconds[0])
    ]
    width_new, width_first_new, width_second_new = adam_update(
        width_gains, width_total, width_first, width_second, 0.0, GAIN_RATE
    )
    hidden_new, hidden_first_new, hidden_second_new = adam_update(
        hidden_gains, hidden_total, hidden_first, hidden_second, 0.0, GAIN_RATE
    )
    return (
        hidden_out,
        grad_in,
        masters_new,
        firsts_new,
        seconds_new,
        weight_grads,
        width_new,
        width_total,
        width_first_new,
        width_second_new,
        hidden_new,
        hidden_total,
        hidden_first_new,
        hidden_second_new,
    )


def solution(mesh):
    in_specs = (
        P("dp", "mp"),
        P("dp", "mp"),
        P(),
        P("mp", "dp", None, None),
        P("mp", "dp", None, None),
        P("mp", "dp", None, None),
        P(None, "mp"),
        P(None, "mp"),
        P(None, "mp"),
        P(None, "mp"),
        P(None, "mp"),
        P(None, "mp"),
    )
    out_specs = (
        P("dp", "mp"),
        P("dp", "mp"),
        P("mp", "dp", None, None),
        P("mp", "dp", None, None),
        P("mp", "dp", None, None),
        P("mp", "dp", None, None),
        P(None, "mp"),
        P(None, "mp"),
        P(None, "mp"),
        P(None, "mp"),
        P(None, "mp"),
        P(None, "mp"),
        P(None, "mp"),
        P(None, "mp"),
    )
    return jax.shard_map(functools.partial(shards, mesh.shape["dp"]), mesh=mesh, in_specs=in_specs, out_specs=out_specs, check_vma=False)
```

```python
import functools
import math

import jax
import jax.numpy as jnp
from jax import lax
from jax.experimental import pallas as pl
from jax.experimental.pallas import tpu as pltpu
from jax.sharding import PartitionSpec as P

D = 1024
HD = 64
STEP = 7
LANES = 128
STEPS = 4
MLP_STEPS = 2
LATE_PARTS = 2

EPSILON = 1e-06
ADAM_EPSILON = 1e-08
BETA_FIRST = 0.9
BETA_SECOND = 0.95
LEARN_RATE = 0.05
GAIN_RATE = 0.6
WEIGHT_DECAY = 0.1
SCORE_SCALE = float(HD) ** 0.5

f32 = jnp.float32
bf16 = jnp.bfloat16


def nn(left, right):
    return jnp.dot(left, right, preferred_element_type=f32)


def nt(left, right):
    return lax.dot_general(left, right, (((1,), (1,)), ((), ())), preferred_element_type=f32)


def tn(left, right):
    return lax.dot_general(left, right, (((0,), (0,)), ((), ())), preferred_element_type=f32)


def normalize(vector):
    inverse = lax.rsqrt(jnp.sum(vector * vector, axis=-1, keepdims=True) / D + EPSILON)
    return (vector * inverse, inverse)


def normalize_back(unit_rows, inverse, upstream):
    return inverse * (upstream - unit_rows * (jnp.sum(unit_rows * upstream, axis=-1, keepdims=True) / D))


def blend_branch(base_rows, branch, branch_rate):
    branch_unit, branch_inv = normalize(branch)
    mixed_unit, mixed_inv = normalize(base_rows + branch_rate * (branch_unit - base_rows))
    return (branch_unit, branch_inv, mixed_unit, mixed_inv)


def blend_back(base_rows, branch_unit, branch_inv, mixed_unit, mixed_inv, branch_rate, upstream):
    d_mixed = normalize_back(mixed_unit, mixed_inv, upstream)
    d_branch = normalize_back(branch_unit, branch_inv, branch_rate * d_mixed)
    return (
        (1.0 - branch_rate) * d_mixed,
        d_branch,
        jnp.sum(d_mixed * (branch_unit - base_rows), axis=0),
    )


def adam_update(params, gradient, first_moment, second_moment, decay_rate, step_rate):
    first_new = BETA_FIRST * first_moment + (1.0 - BETA_FIRST) * gradient
    second_new = BETA_SECOND * second_moment + (1.0 - BETA_SECOND) * gradient * gradient
    corrected = (
        first_new
        / (1.0 - BETA_FIRST**STEP)
        / (jnp.sqrt(second_new / (1.0 - BETA_SECOND**STEP)) + ADAM_EPSILON)
    )
    return (params - step_rate * (corrected + decay_rate * params), first_new, second_new)


def swap_halves(pair, lane):
    return jnp.where(
        lane % HD < HD // 2, pltpu.roll(pair, LANES - HD // 2, 1), pltpu.roll(pair, HD // 2, 1)
    )


def head_sums(values):
    width = values.shape[1]
    row = lax.broadcasted_iota(jnp.int32, (width, width), 0) // HD
    column = lax.broadcasted_iota(jnp.int32, (width, width), 1) // HD
    same = jnp.where(row == column, 1.0, 0.0).astype(bf16)
    high = values.astype(bf16)
    rest = values - high.astype(f32)
    middle = rest.astype(bf16)
    low = (rest - middle.astype(f32)).astype(bf16)
    return nn(high, same) + nn(middle, same) + nn(low, same)


def project_kernel(
    narrow, x_ref, w_ref, gain_ref, cos_ref, sin_ref, op_ref, q_ref, k_ref, v_ref, qr_ref, kr_ref
):
    rows = x_ref.shape[1]
    x = jnp.concatenate([x_ref[d] for d in range(x_ref.shape[0])], axis=1).astype(f32)
    operand = (x * lax.rsqrt(jnp.sum(x * x, axis=1, keepdims=True) / D + EPSILON)).astype(bf16)
    op_ref[...] = operand
    lane = lax.broadcasted_iota(jnp.int32, (rows, LANES), 1)
    cosine, sine = cos_ref[...], sin_ref[...]
    raw = nt(operand, w_ref[...])
    pairs = range(narrow // LANES)
    for which in range(2):
        out_ref, rot_ref = ((q_ref, qr_ref), (k_ref, kr_ref))[which]
        fill = (0.0, 1.0)[which]
        turned = []
        for pair in pairs:
            here = raw[:, which * narrow + pair * LANES : which * narrow + (pair + 1) * LANES]
            turned.append(here * cosine + swap_halves(here, lane) * sine)
        turned = jnp.concatenate(turned, axis=1)
        rot_ref[...] = turned
        gained = gain_ref[0:1, :] * (turned * lax.rsqrt(head_sums(turned * turned) + EPSILON))
        gained = gained.astype(bf16).astype(f32)
        if which == 0:
            gained = gained * SCORE_SCALE
        for pair in pairs:
            here = gained[:, pair * LANES : (pair + 1) * LANES]
            out_ref[2 * pair] = jnp.where(lane < HD, here, fill).astype(bf16)
            out_ref[2 * pair + 1] = jnp.where(lane < HD, pltpu.roll(here, HD, 1), fill).astype(bf16)
    for pair in range(narrow // LANES):
        here = raw[:, 2 * narrow + pair * LANES : 2 * narrow + (pair + 1) * LANES]
        v_ref[2 * pair] = jnp.where(lane < HD, here, 1.0).astype(bf16)
        v_ref[2 * pair + 1] = jnp.where(lane < HD, pltpu.roll(here, HD, 1), 1.0).astype(bf16)


def project(x_all, weights, gain, cosine, sine):
    size, tokens, narrow = x_all.shape
    heads = narrow // HD
    rows = min(512, tokens)
    head_spec = pl.BlockSpec((heads, rows, LANES), lambda i: (0, i, 0))
    row_spec = lambda width: pl.BlockSpec((rows, width), lambda i: (i, 0))
    whole = lambda a: pl.BlockSpec(a.shape, lambda i: (0, 0))
    return pl.pallas_call(
        functools.partial(project_kernel, narrow),
        grid=(tokens // rows,),
        in_specs=[pl.BlockSpec((size, rows, narrow), lambda i: (0, i, 0)), pl.BlockSpec((3 * narrow, D), lambda i: (0, 0)), whole(gain), row_spec(LANES), row_spec(LANES)],
        out_specs=[row_spec(D), head_spec, head_spec, head_spec, row_spec(narrow), row_spec(narrow)],
        out_shape=[jax.ShapeDtypeStruct((tokens, D), bf16)]
        + [jax.ShapeDtypeStruct((heads, tokens, LANES), bf16)] * 3
        + [jax.ShapeDtypeStruct((tokens, narrow), f32)] * 2,
        cost_estimate=pl.CostEstimate(
            flops=2 * tokens * D * 3 * narrow, bytes_accessed=tokens * D * 8, transcendentals=0
        ),
        name="project",
    )(x_all, weights, gain, cosine, sine)


def attend_kernel(block, q_ref, k_ref, v_ref, att_ref, o_ref):
    i = pl.program_id(1)
    lane = lax.broadcasted_iota(jnp.int32, (block, LANES), 1)
    width = min(256, block)

    def head(h, carry):
        queries = q_ref[h]

        def step(j, total):
            rows = pl.ds(pl.multiple_of(j * block, block), block)
            return total + nn(jnp.exp(nt(queries, k_ref[h, rows, :])).astype(bf16), v_ref[h, rows, :])

        total = jnp.zeros((block, LANES), f32)
        if block < k_ref.shape[1]:
            total = lax.fori_loop(0, i, step, total)
        parts = [total[first : first + width] for first in range(0, block, width)]
        for c in range(len(parts)):
            rows = pl.ds(pl.multiple_of(i * block + c * width, width), width)
            weight = jnp.exp(nt(queries[c * width :], k_ref[h, rows, :]))
            row = lax.broadcasted_iota(jnp.int32, weight.shape, 0)
            column = lax.broadcasted_iota(jnp.int32, weight.shape, 1)
            term = nn(jnp.where(row >= column, weight, 0.0).astype(bf16), v_ref[h, rows, :])
            for r in range(c, len(parts)):
                parts[r] = parts[r] + term[(r - c) * width : (r - c + 1) * width]
        total = jnp.concatenate(parts, axis=0)
        o_ref[h] = jnp.where(lane < HD, total / pltpu.roll(total, HD, 1), jnp.log(total))
        return carry

    lax.fori_loop(0, 2, head, 0)
    att_ref[...] = jnp.where(lane < HD, o_ref[0], pltpu.roll(o_ref[1], HD, 1)).astype(bf16)


def attend(queries, keys, values):
    heads, tokens, _ = queries.shape
    block = min(2048, tokens)
    part = pl.BlockSpec((2, block, LANES), lambda p, i: (p, i, 0))
    whole = pl.BlockSpec((2, tokens, LANES), lambda p, i: (p, 0, 0))
    return pl.pallas_call(
        functools.partial(attend_kernel, block),
        grid=(heads // 2, tokens // block),
        in_specs=[part, whole, whole],
        out_specs=[pl.BlockSpec((block, LANES), lambda p, i: (i, p)), part],
        out_shape=[
            jax.ShapeDtypeStruct((tokens, heads * HD), bf16),
            jax.ShapeDtypeStruct((heads, tokens, LANES), f32),
        ],
        compiler_params=pltpu.CompilerParams(vmem_limit_bytes=56 << 20),
        cost_estimate=pl.CostEstimate(
            flops=heads * tokens * tokens * LANES * 4,
            bytes_accessed=heads * tokens * LANES * 10,
            transcendentals=heads * tokens * tokens // 2,
        ),
        name="attend",
    )(queries, keys, values)


def with_parts(lane, base, value):
    high = value.astype(bf16).astype(f32)
    rest = value - high
    middle = rest.astype(bf16).astype(f32)
    low = rest - middle
    tail = jnp.where(lane == HD, high, jnp.where(lane == HD + 1, middle, jnp.where(lane == HD + 2, low, 0.0)))
    return jnp.where(lane < HD, base, tail).astype(bf16)


def attend_back_kernel(
    block, q_ref, k_ref, v_ref, o_ref, do_ref, dq_ref, dk_ref, dv_ref, dk_sum, dv_sum
):
    i = pl.program_id(1)
    count = pl.num_programs(1)
    lane = lax.broadcasted_iota(jnp.int32, (block, LANES), 1)

    @pl.when(i == 0)
    def _():
        dk_sum[...] = jnp.zeros_like(dk_sum)
        dv_sum[...] = jnp.zeros_like(dv_sum)

    d_pair = do_ref[...].astype(f32)
    d_heads = [d_pair, pltpu.roll(d_pair, HD, 1)]
    queries, upstream = [], []
    for h in range(2):
        mixed = o_ref[h]
        delta = jnp.sum(jnp.where(lane < HD, mixed * d_heads[h], 0.0), axis=1, keepdims=True)
        queries.append(with_parts(lane, q_ref[h].astype(f32), -mixed))
        upstream.append(with_parts(lane, d_heads[h], -jnp.broadcast_to(delta, (block, LANES))))

    def step(j, sums, diagonal):
        rows = pl.ds(pl.multiple_of(j * block, block), block)
        new = []
        for h in range(2):
            keys = k_ref[h, rows, :]
            probs = jnp.exp(nt(keys, queries[h]))
            if diagonal:
                row = lax.broadcasted_iota(jnp.int32, probs.shape, 0)
                column = lax.broadcasted_iota(jnp.int32, probs.shape, 1)
                probs = jnp.where(column >= row, probs, 0.0)
            d_scores = (probs * nt(v_ref[h, rows, :], upstream[h])).astype(bf16)
            dv_sum[h, rows, :] += nn(probs.astype(bf16), upstream[h])
            dk_sum[h, rows, :] += nn(d_scores, queries[h])
            new.append(sums[h] + tn(d_scores, keys))
        return tuple(new)

    zero = jnp.zeros((block, LANES), f32)
    sums = lax.fori_loop(0, i, lambda j, s: step(j, s, False), (zero, zero))
    sums = step(i, sums, True)
    dq_ref[...] = jnp.where(lane < HD, sums[0], pltpu.roll(sums[1], HD, 1)) * SCORE_SCALE

    @pl.when(i == count - 1)
    def _():
        def put(j, carry):
            rows = pl.ds(pl.multiple_of(j * block, block), block)
            dk_ref[rows, :] = jnp.where(lane < HD, dk_sum[0, rows, :], pltpu.roll(dk_sum[1, rows, :], HD, 1))
            dv_ref[rows, :] = jnp.where(lane < HD, dv_sum[0, rows, :], pltpu.roll(dv_sum[1, rows, :], HD, 1))
            return carry

        lax.fori_loop(0, count, put, 0)


def attend_back(queries, keys, values, mixed, d_attended):
    heads, tokens, _ = queries.shape
    block = min(512, tokens)
    part = pl.BlockSpec((2, block, LANES), lambda p, i: (p, i, 0))
    whole = pl.BlockSpec((2, tokens, LANES), lambda p, i: (p, 0, 0))
    pair_part = pl.BlockSpec((block, LANES), lambda p, i: (i, p))
    pair_whole = pl.BlockSpec((tokens, LANES), lambda p, i: (0, p))
    return pl.pallas_call(
        functools.partial(attend_back_kernel, block),
        grid=(heads // 2, tokens // block),
        in_specs=[part, whole, whole, part, pair_part],
        out_specs=[pair_part, pair_whole, pair_whole],
        out_shape=[jax.ShapeDtypeStruct((tokens, heads * HD), f32)] * 3,
        scratch_shapes=[pltpu.VMEM((2, tokens, LANES), f32)] * 2,
        cost_estimate=pl.CostEstimate(
            flops=heads * tokens * tokens * LANES * 10,
            bytes_accessed=heads * tokens * LANES * 20,
            transcendentals=heads * tokens * tokens // 2,
        ),
        name="attend_back",
    )(queries, keys, values, mixed, d_attended)


def project_back_kernel(
    narrow, dq_ref, dk_ref, dv_ref, qr_ref, kr_ref, gain_ref, cos_ref, sin_ref, out_ref, gg_ref
):
    rows = dq_ref.shape[0]
    lane = lax.broadcasted_iota(jnp.int32, (rows, LANES), 1)
    cosine, sine = cos_ref[...], sin_ref[...]

    @pl.when(pl.program_id(0) == 0)
    def _():
        gg_ref[...] = jnp.zeros_like(gg_ref)

    for which in range(2):
        d_ref, rot_ref = ((dq_ref, qr_ref), (dk_ref, kr_ref))[which]
        turned = rot_ref[...]
        inverse = lax.rsqrt(head_sums(turned * turned) + EPSILON)
        unit_rows = turned * inverse
        upstream = d_ref[...]
        gg_ref[...] += jnp.sum(upstream * unit_rows, axis=0, keepdims=True)
        upstream = upstream * gain_ref[0:1, :]
        back = inverse * (upstream - unit_rows * head_sums(unit_rows * upstream))
        for pair in range(narrow // LANES):
            here = back[:, pair * LANES : (pair + 1) * LANES]
            here = here * cosine - swap_halves(here, lane) * sine
            out_ref[:, which * narrow + pair * LANES : which * narrow + (pair + 1) * LANES] = here.astype(bf16)
    out_ref[:, 2 * narrow : 3 * narrow] = dv_ref[...].astype(bf16)


def project_back(d_queries, d_keys, d_values, q_turned, k_turned, gain, cosine, sine):
    tokens, narrow = d_queries.shape
    rows = min(512, tokens)
    row_spec = lambda width: pl.BlockSpec((rows, width), lambda i: (i, 0))
    one = pl.BlockSpec((1, narrow), lambda i: (0, 0))
    whole = pl.BlockSpec(gain.shape, lambda i: (0, 0))
    return pl.pallas_call(
        functools.partial(project_back_kernel, narrow),
        grid=(tokens // rows,),
        in_specs=[row_spec(narrow)] * 5 + [whole, row_spec(LANES), row_spec(LANES)],
        out_specs=[row_spec(3 * narrow), one],
        out_shape=[
            jax.ShapeDtypeStruct((tokens, 3 * narrow), bf16),
            jax.ShapeDtypeStruct((1, narrow), f32),
        ],
        cost_estimate=pl.CostEstimate(
            flops=tokens * narrow * 60, bytes_accessed=tokens * narrow * 26, transcendentals=0
        ),
        name="project_back",
    )(d_queries, d_keys, d_values, q_turned, k_turned, gain, cosine, sine)


MESH = pl.DeviceIdType.MESH


class Group:
    def __init__(self, size, steps, tokens):
        self.size, self.steps = size, steps
        self.chips = size // 2
        self.own = tokens // size
        self.rows = self.own // steps
        self.dp, self.me = lax.axis_index("dp"), lax.axis_index("mp")
        self.chip, self.core = self.me // 2, lax.rem(self.me, 2)
        self.partner = self.me + 1 - 2 * self.core

    def other(self, k, core):
        return 2 * lax.rem(self.chip + k, self.chips) + core

    def slot(self, device):
        k = lax.rem(device // 2 - self.chip + self.chips, self.chips)
        return jnp.where(k == 0, 0, 2 * k - 1 + (lax.rem(device, 2) != self.core).astype(jnp.int32))

    def piece(self, ref, index, step):
        return ref.at[index, pl.ds(pl.multiple_of(step * self.rows, self.rows), self.rows), :]

    def copy(self, source, target, send, receive, device):
        return pltpu.make_async_remote_copy(
            src_ref=source,
            dst_ref=target,
            send_sem=send,
            recv_sem=receive,
            device_id=(self.dp, device),
            device_id_type=MESH,
        )

    def meet(self, everyone=False):
        barrier = pltpu.get_barrier_semaphore()
        devices = [self.partner] + [self.other(k, self.core) for k in range(1, self.chips)]
        if everyone:
            devices = [lax.rem(self.me + j, self.size) for j in range(1, self.size)]
        for device in devices:
            pl.semaphore_signal(barrier, inc=1, device_id=(self.dp, device), device_id_type=MESH)
        pl.semaphore_wait(barrier, len(devices))

    def place(self, i, remote_first=False):
        size, steps = self.size, self.steps
        others = steps * (size - 1)
        if remote_first:
            is_own = i >= others
            j = jnp.where(is_own, 0, i)
            s = jnp.where(is_own, i - others, j // (size - 1))
            r = lax.rem(lax.rem(j, size - 1) + 1, size - 1)
        else:
            is_own = i < steps
            j = jnp.where(is_own, 0, i - steps)
            s = jnp.where(is_own, i, j // (size - 1))
            r = lax.rem(j, size - 1)
        other = jnp.logical_not(is_own)
        is_partner = jnp.logical_and(other, r == 0)
        remote = jnp.logical_and(other, r > 0)
        is_first = jnp.logical_and(remote, lax.rem(r, 2) == 1)
        is_second = jnp.logical_and(remote, lax.rem(r, 2) == 0)
        k = jnp.where(remote, (r + 1) // 2, 0)
        core = jnp.where(jnp.logical_or(is_own, is_first), self.core, 1 - self.core)
        return self.other(k, core), s, k, is_own, is_partner, is_first, is_second

    def run(self, compute, gather=None, settle=None, remote_first=False, after=None, ready=(), between=None):
        steps, chips, size = self.steps, self.chips, self.size

        if gather:
            own_ref, all_ref, g_send, g_recv = gather

            def own_piece(s):
                return own_ref.at[pl.ds(pl.multiple_of(s * self.rows, self.rows), self.rows), :]

            def start_own(s, carry):
                for k in range(1, chips):
                    self.copy(own_piece(s), self.piece(all_ref, self.me, s), g_send.at[k, s], g_recv.at[self.me, s], self.other(k, self.core)).start()
                self.copy(own_piece(s), self.piece(all_ref, self.me, s), g_send.at[0, s], g_recv.at[self.me, s], self.partner).start()
                return carry

            lax.fori_loop(0, steps, start_own, 0)
            all_ref[self.me] = own_ref[...]

            def got(device, s):
                here = self.piece(all_ref, device, s)
                self.copy(here, here, g_send.at[0, s], g_recv.at[device, s], self.partner).wait_recv()

            def forward(k, s):
                device = self.other(k, self.core)
                here = self.piece(all_ref, device, s)
                return self.copy(here, here, g_send.at[chips + k - 1, s], g_recv.at[device, s], self.partner)

        if settle:
            out_ref, kept, to_partner, from_partner, to_chip, from_chip, p_send, p_recv, x_send, x_recv = settle

            def to_partner_copy(k, s):
                return self.copy(self.piece(to_partner, k, s), self.piece(from_partner, k, s), p_send.at[k, s], p_recv.at[k, s], self.partner)

            def to_chip_copy(k, s):
                return self.copy(self.piece(to_chip, k - 1, s), self.piece(from_chip, k - 1, s), x_send.at[k - 1, s], x_recv.at[k - 1, s], self.other(k, self.core))

        for copy in ready:
            copy.wait()

        def item(i, carry):
            device, s, k, is_own, is_partner, is_first, is_second = self.place(i, remote_first)
            if gather:

                @pl.when(jnp.logical_not(is_own))
                def _():
                    got(device, s)

                @pl.when(is_first)
                def _():
                    forward(k, s).start()

            term = compute(device, s, i)
            if between:
                between(device, jnp.logical_or(i == steps - 1, jnp.logical_and(is_partner, s == steps - 1)))
            if settle:
                here = pl.ds(pl.multiple_of(s * self.rows, self.rows), self.rows)

                @pl.when(is_own)
                def _():
                    out_ref[here, :] = term

                @pl.when(is_first)
                def _():
                    kept[...] = term

                @pl.when(jnp.logical_or(is_partner, is_second))
                def _():
                    to_partner[k, here, :] = term.astype(bf16)
                    to_partner_copy(k, s).start()

                @pl.when(is_second)
                def _():
                    to_partner_copy(k, s).wait_recv()
                    to_chip[k - 1, here, :] = (kept[...] + from_partner[k, here, :].astype(f32)).astype(bf16)
                    to_chip_copy(k, s).start()

            return carry

        lax.fori_loop(0, size * steps, item, 0)

        def end(s, carry):
            if settle:
                here = pl.ds(pl.multiple_of(s * self.rows, self.rows), self.rows)
                to_partner_copy(0, s).wait_recv()
                total = out_ref[here, :] + from_partner[0, here, :].astype(f32)
                for k in range(1, chips):
                    to_chip_copy(k, s).wait_recv()
                    total = total + from_chip[k - 1, here, :].astype(f32)
                out_ref[here, :] = total
                if after:
                    after(s)
                for k in range(chips):
                    to_partner_copy(k, s).wait_send()
                for k in range(1, chips):
                    to_chip_copy(k, s).wait_send()
            if gather:
                for k in range(2 * chips - 1):
                    self.copy(own_piece(s), own_piece(s), g_send.at[k, s], g_recv.at[0, s], self.partner).wait_send()
            return carry

        self.end = lambda first=0, last=steps: lax.fori_loop(first, last, end, 0)


def settle_scratch(size, steps, tokens):
    own, chips = tokens // size, size // 2
    return [
        pltpu.VMEM((own // steps, D), f32),
        pltpu.VMEM((chips, own, D), bf16),
        pltpu.VMEM((chips, own, D), bf16),
        pltpu.VMEM((chips - 1, own, D), bf16),
        pltpu.VMEM((chips - 1, own, D), bf16),
        pltpu.SemaphoreType.DMA((chips, steps)),
        pltpu.SemaphoreType.DMA((chips, steps)),
        pltpu.SemaphoreType.DMA((chips - 1, steps)),
        pltpu.SemaphoreType.DMA((chips - 1, steps)),
    ]


def gather_sems(size, steps):
    return [pltpu.SemaphoreType.DMA((size - 1, steps)), pltpu.SemaphoreType.DMA((size, steps))]


VMEM_WHOLE = pl.BlockSpec(memory_space=pltpu.VMEM)
ANYWHERE = pl.BlockSpec(memory_space=pl.ANY)
GRANT = 67043328


def weight_scratch(rows, count=1):
    return [pltpu.VMEM((rows, D), bf16)] * count + [pltpu.SemaphoreType.DMA((count,))]


def weight_copies(weights, buffers, sem, first):
    copies = []
    for i, buffer in enumerate(buffers):
        copies.append(pltpu.make_async_copy(weights.at[pl.ds(first, buffer.shape[0]), :], buffer, sem.at[i]))
        first += buffer.shape[0]
    return copies


def remote_params(collective_id):
    return pltpu.CompilerParams(
        collective_id=collective_id, has_side_effects=True, vmem_limit_bytes=GRANT
    )


def attention_sum_kernel(
    size, steps, first_row, rows_ref, w_hbm, start_ref, rates_ref,
    out_ref, middle_ref, low_ref, w_ref, w_sem, *scratch
):
    tokens = rows_ref.shape[0]
    group = Group(size, steps, tokens)
    (copy,) = weight_copies(w_hbm, [w_ref], w_sem, first_row)
    copy.start()
    group.meet()
    copy.wait()

    def compute(device, s, i):
        first = pl.multiple_of(device * group.own + s * group.rows, group.rows)
        return nn(rows_ref[pl.ds(first, group.rows), :], w_ref[...])

    def after(s):
        here = pl.ds(pl.multiple_of(s * group.rows, group.rows), group.rows)
        middle = blend_branch(start_ref[here, :], out_ref[here, :], rates_ref[1:2, :])[2]
        middle_ref[here, :] = middle
        low_ref[here, :] = middle.astype(bf16)

    group.run(compute, settle=(out_ref, *scratch), remote_first=True, after=after)
    group.end()


def attention_sum(rows, weights, start_unit, rates, first_row, size, steps, collective_id):
    tokens, depth = rows.shape
    own = jax.ShapeDtypeStruct((tokens // size, D), f32)
    return pl.pallas_call(
        functools.partial(attention_sum_kernel, size, steps, first_row),
        out_shape=[own, own, jax.ShapeDtypeStruct(own.shape, bf16)],
        in_specs=[VMEM_WHOLE, ANYWHERE, VMEM_WHOLE, VMEM_WHOLE],
        out_specs=[VMEM_WHOLE] * 3,
        scratch_shapes=weight_scratch(depth) + settle_scratch(size, steps, tokens),
        compiler_params=remote_params(collective_id),
        cost_estimate=pl.CostEstimate(flops=2 * tokens * depth * D, bytes_accessed=tokens * D * 8, transcendentals=0),
        name="attention_sum",
    )(rows, weights, start_unit, rates)


def mlp_kernel(
    size, steps, own_ref, w_hbm, scale_ref, middle_ref, cot_ref, rates_ref,
    out_ref, rows_hbm, ur_hbm, gr_hbm, d_mlp_ref, d_middle_ref, g_rate_ref, branch_ref, rows_ref, r_sem,
    up_ref, gate_ref, down_ref, w_sem, u_buf, g_buf, b_sem, *scratch
):
    tokens = own_ref.shape[0] * size
    group = Group(size, steps, tokens)
    copies = weight_copies(w_hbm, [up_ref, gate_ref, down_ref], w_sem, scale_ref.shape[1])
    for c in copies:
        c.start()
    group.meet()

    def save(i, device, s):
        slot = lax.rem(i, 2)
        rows = pl.ds(pl.multiple_of(device * group.own + s * group.rows, group.rows), group.rows)
        return (
            pltpu.make_async_copy(u_buf.at[slot], ur_hbm.at[rows, :], b_sem.at[0, slot]),
            pltpu.make_async_copy(g_buf.at[slot], gr_hbm.at[rows, :], b_sem.at[1, slot]),
        )

    def compute(device, s, i):
        slot = lax.rem(i, 2)

        @pl.when(i >= 2)
        def _():
            for c in save(i, device, s):
                c.wait()

        rows = group.piece(rows_ref, device, s)[...]
        up_raw = nt(rows, up_ref[...])
        gate_raw = nt(rows, gate_ref[...])
        u_buf[slot] = up_raw
        g_buf[slot] = gate_raw
        for c in save(i, device, s):
            c.start()
        gate_val = scale_ref[1:2, :] * gate_raw
        product = (scale_ref[0:1, :] * up_raw * (gate_val * jax.nn.sigmoid(gate_val))).astype(bf16)
        return nn(product, down_ref[...])

    g_rate_ref[...] = jnp.zeros_like(g_rate_ref)

    def after(s):
        here = pl.ds(pl.multiple_of(s * group.rows, group.rows), group.rows)
        middle, rate = middle_ref[here, :], rates_ref[2:3, :]
        branch_unit, branch_inv, mixed, mixed_inv = blend_branch(middle, branch_ref[here, :], rate)
        for d in range(size):
            out_ref[d, here, :] = mixed[:, d * (D // size) : (d + 1) * (D // size)]
        upstream = jnp.concatenate([cot_ref[d, here, :] for d in range(size)], axis=1).astype(f32)
        d_middle, d_branch, g_rate = blend_back(
            middle, branch_unit, branch_inv, mixed, mixed_inv, rate, upstream
        )
        d_middle_ref[here, :] = d_middle
        d_mlp_ref[here, :] = d_branch.astype(bf16)
        g_rate_ref[...] += g_rate[None]

    group.run(
        compute, gather=(own_ref, rows_ref, scratch[0], scratch[1]), settle=(branch_ref, *scratch[2:]), ready=copies, after=after
    )
    keep = pltpu.make_async_copy(rows_ref, rows_hbm, r_sem.at[0])
    keep.start()
    for i in range(2):
        for c in save(i, 0, 0):
            c.wait()
    group.end()
    keep.wait()


def mlp(own, weights, scales, middle, cot_all, rates, size, steps, collective_id):
    hidden = scales.shape[1]
    tokens = own.shape[0] * size
    rows = own.shape[0] // steps
    return pl.pallas_call(
        functools.partial(mlp_kernel, size, steps),
        out_shape=[
            jax.ShapeDtypeStruct((size, own.shape[0], D // size), f32),
            jax.ShapeDtypeStruct((size, own.shape[0], D), bf16),
            jax.ShapeDtypeStruct((tokens, hidden), f32),
            jax.ShapeDtypeStruct((tokens, hidden), f32),
            jax.ShapeDtypeStruct((own.shape[0], D), bf16),
            jax.ShapeDtypeStruct((own.shape[0], D), f32),
            jax.ShapeDtypeStruct((1, D), f32),
        ],
        in_specs=[VMEM_WHOLE, ANYWHERE] + [VMEM_WHOLE] * 4,
        out_specs=[VMEM_WHOLE, ANYWHERE, ANYWHERE, ANYWHERE] + [VMEM_WHOLE] * 3,
        scratch_shapes=[
            pltpu.VMEM((own.shape[0], D), f32),
            pltpu.VMEM((size, own.shape[0], D), bf16),
            pltpu.SemaphoreType.DMA((1,)),
        ]
        + weight_scratch(hidden, 3)
        + [
            pltpu.VMEM((2, rows, hidden), f32),
            pltpu.VMEM((2, rows, hidden), f32),
            pltpu.SemaphoreType.DMA((2, 2)),
        ]
        + gather_sems(size, steps)
        + settle_scratch(size, steps, tokens),
        compiler_params=remote_params(collective_id),
        cost_estimate=pl.CostEstimate(flops=6 * tokens * hidden * D, bytes_accessed=tokens * D * 12, transcendentals=tokens * hidden),
        name="mlp",
    )(own, weights, scales, middle, cot_all, rates)


def mlp_back_kernel(
    size, steps, own_ref, w_hbm, scale_ref, ur_hbm, gr_hbm, middle_rows_ref, d_middle_hbm, start_hbm, branch_hbm, rates_ref,
    d_attn_ref, d_start_ref, g_rate_ref, gs_ref, grads_hbm,
    stage, stage_sem, late, late_sem,
    sum_ref, rows_ref, product_ref, d_ref, grads_sum,
    up_ref, gate_ref, down_ref, w_sem, u_buf, g_buf, b_sem, *scratch
):
    tokens = own_ref.shape[0] * size
    group = Group(size, steps, tokens)

    def load(i):
        device, s = group.place(i)[:2]
        slot = lax.rem(i, 2)
        rows = pl.ds(pl.multiple_of(device * group.own + s * group.rows, group.rows), group.rows)
        return (
            pltpu.make_async_copy(ur_hbm.at[rows, :], u_buf.at[slot], b_sem.at[0, slot]),
            pltpu.make_async_copy(gr_hbm.at[rows, :], g_buf.at[slot], b_sem.at[1, slot]),
        )

    copies = weight_copies(w_hbm, [up_ref, gate_ref, down_ref], w_sem, scale_ref.shape[1])
    for c in (*load(0), *copies):
        c.start()
    gs_ref[...] = jnp.zeros_like(gs_ref)
    g_rate_ref[...] = jnp.zeros_like(g_rate_ref)
    group.meet()
    hidden = scale_ref.shape[1]
    part = min(256, hidden)

    def weight_grads(device):
        rows = pl.ds(pl.multiple_of(group.slot(device) * group.own, group.own), group.own)

        def one(source, offset, other):
            def column(c, carry):
                first = pl.multiple_of(c * part, part)
                to = pl.ds(pl.multiple_of(offset + first, part), part)
                term = tn(source[rows, pl.ds(first, part)], other[device])
                grads_sum[to, :] += term
                return carry

            lax.fori_loop(0, source.shape[1] // part, column, 0)

        one(d_ref, 0, middle_rows_ref)
        one(product_ref, 2 * hidden, rows_ref)

    def clear(c, carry):
        grads_sum[pl.ds(pl.multiple_of(c * part, part), part), :] = jnp.zeros((part, D), f32)
        return carry

    lax.fori_loop(0, 3 * hidden // part, clear, 0)

    def between(device, done):
        @pl.when(done)
        def _():
            weight_grads(device)

    late_rows = late.shape[2]

    def late_copies(s):
        here = pl.ds(pl.multiple_of(s * late_rows, late_rows), late_rows)
        return [
            pltpu.make_async_copy(ref.at[here, :], late.at[lax.rem(s, 2), i], late_sem.at[lax.rem(s, 2), i])
            for i, ref in enumerate((start_hbm, branch_hbm, d_middle_hbm))
        ]

    for c in late_copies(0):
        c.start()

    def after_part(s, carry):
        here = pl.ds(pl.multiple_of(s * late_rows, late_rows), late_rows)
        for c in late_copies(s):
            c.wait()

        @pl.when(s + 1 < steps * LATE_PARTS)
        def _():
            for c in late_copies(s + 1):
                c.start()

        start, branch, d_middle = [late[lax.rem(s, 2), i] for i in range(3)]
        rate = rates_ref[1:2, :]
        branch_unit, branch_inv, middle, middle_inv = blend_branch(start, branch, rate)
        d_start, d_branch, g_rate = blend_back(
            start, branch_unit, branch_inv, middle, middle_inv, rate, d_middle + sum_ref[here, :]
        )
        d_start_ref[here, :] = d_start
        d_attn_ref[here, :] = d_branch.astype(bf16)
        g_rate_ref[...] += g_rate[None]
        return carry

    def after(s):
        lax.fori_loop(s * LATE_PARTS, (s + 1) * LATE_PARTS, after_part, 0)

    def compute(device, s, i):
        slot = lax.rem(i, 2)

        @pl.when(i + 1 < size * steps)
        def _():
            for c in load(i + 1):
                c.start()

        rows = group.piece(rows_ref, device, s)[...]
        d_product = nt(rows, down_ref[...])
        for c in load(i):
            c.wait()
        first = pl.multiple_of(group.slot(device) * group.own + s * group.rows, group.rows)
        here = pl.ds(first, group.rows)
        up_raw, gate_raw = u_buf[slot], g_buf[slot]
        up_val = scale_ref[0:1, :] * up_raw
        gate_val = scale_ref[1:2, :] * gate_raw
        sigmoid = jax.nn.sigmoid(gate_val)
        activated = gate_val * sigmoid
        product_ref[here, :] = (up_val * activated).astype(bf16)
        d_up = d_product * activated
        d_gate = d_product * up_val * (sigmoid * (1.0 + gate_val * (1.0 - sigmoid)))
        gs_ref[0:1, :] += jnp.sum(d_up * up_raw, axis=0, keepdims=True)
        gs_ref[1:2, :] += jnp.sum(d_gate * gate_raw, axis=0, keepdims=True)
        d_up_raw = (d_up * scale_ref[0:1, :]).astype(bf16)
        d_gate_raw = (d_gate * scale_ref[1:2, :]).astype(bf16)
        d_ref[here, :hidden] = d_up_raw
        d_ref[here, hidden:] = d_gate_raw
        return nn(d_up_raw, up_ref[...]) + nn(d_gate_raw, gate_ref[...])

    group.run(
        compute, gather=(own_ref, rows_ref, scratch[0], scratch[1]), settle=(sum_ref, *scratch[2:]), ready=copies,
        after=after, between=between,
    )

    def rest(j, carry):
        weight_grads(group.other(1 + j // 2, lax.rem(j, 2)))
        return carry

    lax.fori_loop(0, size - 2, rest, 0)

    def stage_copy(c):
        here = pl.ds(pl.multiple_of(c * part, part), part)
        return pltpu.make_async_copy(stage.at[lax.rem(c, 2)], grads_hbm.at[here, :], stage_sem.at[lax.rem(c, 2)])

    def put(c, carry):
        @pl.when(c >= 2)
        def _():
            stage_copy(c - 2).wait()

        stage[lax.rem(c, 2)] = grads_sum[pl.ds(pl.multiple_of(c * part, part), part), :].astype(bf16)
        stage_copy(c).start()
        return carry

    parts = 3 * hidden // part
    lax.fori_loop(0, parts, put, 0)
    group.end()
    for c in range(2):
        stage_copy(c).wait()


def mlp_back(own, weights, scales, up_raw, gate_raw, middle_rows, d_middle, start_unit, branch, rates, size, steps, collective_id):
    tokens, hidden = up_raw.shape
    rows = own.shape[0] // steps
    return pl.pallas_call(
        functools.partial(mlp_back_kernel, size, steps),
        out_shape=[
            jax.ShapeDtypeStruct((own.shape[0], D), bf16),
            jax.ShapeDtypeStruct((own.shape[0], D), f32),
            jax.ShapeDtypeStruct((1, D), f32),
            jax.ShapeDtypeStruct((2, hidden), f32),
            jax.ShapeDtypeStruct((3 * hidden, D), bf16),
        ],
        in_specs=[VMEM_WHOLE, ANYWHERE, VMEM_WHOLE, ANYWHERE, ANYWHERE, VMEM_WHOLE] + [ANYWHERE] * 3 + [VMEM_WHOLE],
        out_specs=[VMEM_WHOLE] * 4 + [ANYWHERE],
        scratch_shapes=[
            pltpu.VMEM((2, min(256, hidden), D), bf16),
            pltpu.SemaphoreType.DMA((2,)),
            pltpu.VMEM((2, 3, rows // LATE_PARTS, D), f32),
            pltpu.SemaphoreType.DMA((2, 3)),
            pltpu.VMEM((own.shape[0], D), f32),
            pltpu.VMEM((size, own.shape[0], D), bf16),
            pltpu.VMEM((tokens - own.shape[0], hidden), bf16),
            pltpu.VMEM((tokens - own.shape[0], 2 * hidden), bf16),
            pltpu.VMEM((3 * hidden, D), f32),
        ]
        + weight_scratch(hidden, 3)
        + [
            pltpu.VMEM((2, rows, hidden), f32),
            pltpu.VMEM((2, rows, hidden), f32),
            pltpu.SemaphoreType.DMA((2, 2)),
        ]
        + gather_sems(size, steps)
        + settle_scratch(size, steps, tokens),
        compiler_params=remote_params(collective_id),
        cost_estimate=pl.CostEstimate(flops=6 * tokens * hidden * D, bytes_accessed=tokens * D * 24, transcendentals=tokens * hidden),
        name="mlp_back",
    )(own, weights, scales, up_raw, gate_raw, middle_rows, d_middle, start_unit, branch, rates)


def gather_project_kernel(size, steps, first_row, own_ref, w_hbm, out_ref, rows_ref, w_ref, w_sem, *scratch):
    tokens = own_ref.shape[0] * size
    group = Group(size, steps, tokens)
    copies = weight_copies(w_hbm, [w_ref], w_sem, first_row)
    copies[0].start()
    group.meet()

    def compute(device, s, i):
        first = pl.multiple_of(device * group.own + s * group.rows, group.rows)
        out_ref[pl.ds(first, group.rows), :] = nt(group.piece(rows_ref, device, s)[...], w_ref[...]).astype(bf16)

    group.run(compute, gather=(own_ref, rows_ref, scratch[0], scratch[1]), ready=copies)
    group.end()


def gather_project(own, weights, width, first_row, size, steps, collective_id, name):
    tokens = own.shape[0] * size
    return pl.pallas_call(
        functools.partial(gather_project_kernel, size, steps, first_row),
        out_shape=[
            jax.ShapeDtypeStruct((tokens, width), bf16),
            jax.ShapeDtypeStruct((size, own.shape[0], D), bf16),
        ],
        in_specs=[VMEM_WHOLE, ANYWHERE],
        out_specs=[VMEM_WHOLE, VMEM_WHOLE],
        scratch_shapes=weight_scratch(width) + gather_sems(size, steps),
        compiler_params=remote_params(collective_id),
        cost_estimate=pl.CostEstimate(flops=2 * tokens * width * D, bytes_accessed=tokens * D * 4, transcendentals=0),
        name=name,
    )(own, weights)


def start_sum_kernel(
    size, steps, rows_ref, w_hbm, base_ref, unit_ref, inv_ref, operand_hbm, attended_hbm, d_attn_hbm,
    pieces, grads_ref, operand_ref, attended_ref, d_attn_ref, late_sem, w_ref, w_sem, total_ref, *scratch
):
    tokens = rows_ref.shape[0]
    narrow = pieces.shape[2]
    group = Group(size, steps, tokens)
    copies = weight_copies(w_hbm, [w_ref], w_sem, 0)
    copies[0].start()
    late = [
        pltpu.make_async_copy(source, target, late_sem.at[i])
        for i, (source, target) in enumerate(
            ((operand_hbm, operand_ref), (attended_hbm, attended_ref), (d_attn_hbm, d_attn_ref))
        )
    ]
    for copy in late:
        copy.start()
    group.meet()
    copies[0].wait()

    def compute(device, s, i):
        first = pl.multiple_of(device * group.own + s * group.rows, group.rows)
        return nn(rows_ref[pl.ds(first, group.rows), :], w_ref[...])

    def after(s):
        here = pl.ds(pl.multiple_of(s * group.rows, group.rows), group.rows)
        back = normalize_back(unit_ref[here, :], inv_ref[here, 0:1], base_ref[here, :] + total_ref[here, :])
        for device in range(size):
            pieces[device, here, :] = back[:, device * narrow : (device + 1) * narrow].astype(bf16)

    group.run(compute, settle=(total_ref, *scratch), remote_first=True, after=after)

    for copy in late:
        copy.wait()
    for c in range(3):
        here = slice(c * narrow, (c + 1) * narrow)
        grads_ref[here, :] = tn(rows_ref[:, here], operand_ref[...]).astype(bf16)
        group.end(c * steps // 4, (c + 1) * steps // 4)
    out_sum = jnp.zeros((narrow, D), f32)
    for d in range(size):
        out_sum += tn(attended_ref[d * group.own : (d + 1) * group.own, :], d_attn_ref[d])
    grads_ref[3 * narrow :, :] = out_sum.astype(bf16)
    group.end(3 * steps // 4, steps)


def start_sum(rows, weights, base, unit_rows, inverse, operand, attended, d_attn_rows, size, steps, collective_id):
    tokens, depth = rows.shape
    own, narrow = tokens // size, D // size
    return pl.pallas_call(
        functools.partial(start_sum_kernel, size, steps),
        out_shape=[jax.ShapeDtypeStruct((size, own, narrow), bf16), jax.ShapeDtypeStruct((4 * narrow, D), bf16)],
        in_specs=[VMEM_WHOLE, ANYWHERE] + [VMEM_WHOLE] * 3 + [ANYWHERE] * 3,
        out_specs=[VMEM_WHOLE] * 2,
        scratch_shapes=[
            pltpu.VMEM(operand.shape, bf16),
            pltpu.VMEM(attended.shape, bf16),
            pltpu.VMEM(d_attn_rows.shape, bf16),
            pltpu.SemaphoreType.DMA((3,)),
        ]
        + weight_scratch(depth)
        + [
            pltpu.VMEM((own, D), f32),
        ]
        + settle_scratch(size, steps, tokens),
        compiler_params=remote_params(collective_id),
        cost_estimate=pl.CostEstimate(flops=2 * tokens * depth * D, bytes_accessed=tokens * D * 8, transcendentals=0),
        name="start_sum",
    )(rows, weights, base, unit_rows, inverse, operand, attended, d_attn_rows)


def tail_plan(devices, rows):
    lines = min(4, devices)
    columns = devices // lines
    cuts = 2 if rows % (devices * 32) == 0 else 1
    return lines, columns, cuts, rows // (devices * cuts)


def tail_sum_kernel(
    devices, size, late_ref, home_ref, rate_attn_ref, rate_mlp_ref, gain_ref, scale_ref, hidden_ref, back_ref,
    late_out, home_out, small_out, hidden_out, back_out,
    y_land, y_sum, z_land, rate_parts, rate_land, pack, small_land,
    a_send, a_recv, b_send, b_recv, c_send, c_recv, d_send, d_recv, m_send, m_recv, s_send, s_recv, h_send, h_recv, g_send, g_recv, e_send, e_recv, f_send, f_recv, local_sem
):
    dp, me = lax.axis_index("dp"), lax.axis_index("mp")
    lines, columns, cuts, rows = tail_plan(devices, late_ref.shape[0])
    a, b = dp // columns, lax.rem(dp, columns)
    span = lines * rows
    narrow = rate_parts.shape[2]
    chunks = [(late_ref, late_out, q) for q in range(cuts)]
    pieces = e_send.shape[0]
    height = home_ref.shape[0] // pieces

    def remote(source, target, send, receive, device):
        return pltpu.make_async_remote_copy(
            src_ref=source, dst_ref=target, send_sem=send, recv_sem=receive, device_id=device, device_id_type=MESH
        )

    def peer(j):
        return lax.rem(dp + j, devices)

    def column(j):
        return lax.rem(b + j, columns)

    def line(j):
        return lax.rem(a + j, lines)

    barrier = pltpu.get_barrier_semaphore()

    def greet(j, carry):
        pl.semaphore_signal(barrier, inc=1, device_id=(peer(j), me), device_id_type=MESH)
        return carry

    lax.fori_loop(1, devices, greet, 0)
    for j in range(1, size):
        pl.semaphore_signal(barrier, inc=1, device_id=(dp, lax.rem(me + j, size)), device_id_type=MESH)
    pl.semaphore_wait(barrier, devices - 1 + size - 1)

    def part(ref, q, col):
        return ref.at[pl.ds(pl.multiple_of((q * columns + col) * span, span), span), :]

    def to_column(c, j):
        ref, _, q = chunks[c]
        return remote(part(ref, q, column(j)), y_land.at[c, b], a_send.at[c, j], a_recv.at[c, b], (a * columns + column(j), me))

    def from_column(c, j):
        here = y_land.at[c, column(j)]
        return remote(here, here, a_send.at[c, j], a_recv.at[c, column(j)], (a * columns + column(j), me))

    def to_line(c, j):
        there = pl.ds(pl.multiple_of(line(j) * rows, rows), rows)
        return remote(y_sum.at[c, there, :], z_land.at[c, a], b_send.at[c, j], b_recv.at[c, a], (line(j) * columns + b, me))

    def from_line(c, j):
        here = z_land.at[c, line(j)]
        return remote(here, here, b_send.at[c, j], b_recv.at[c, line(j)], (line(j) * columns + b, me))

    def sum_of(c, col, row):
        _, out, q = chunks[c]
        return out.at[(q * columns + col) * lines + row]

    def back_line(c, j):
        here = sum_of(c, b, a)
        return remote(here, here, c_send.at[c, j], c_recv.at[c, a], (line(j) * columns + b, me))

    def back_line_got(c, j):
        here = sum_of(c, b, line(j))
        return remote(here, here, c_send.at[c, j], c_recv.at[c, line(j)], (line(j) * columns + b, me))

    def back_column(c, i, j):
        here = sum_of(c, b, line(i))
        return remote(here, here, d_send.at[c, i, j], d_recv.at[c, line(i), b], (a * columns + column(j), me))

    def back_column_got(c, i, j):
        here = sum_of(c, column(j), line(i))
        return remote(here, here, d_send.at[c, i, j], d_recv.at[c, line(i), column(j)], (a * columns + column(j), me))

    def home(col, row, p):
        return home_out.at[row * columns + col, pl.ds(p * height, height), :]

    def home_line(p, j):
        return remote(
            home_ref.at[pl.ds(p * height, height), :], home(b, a, p), e_send.at[p, j], e_recv.at[p, a], (line(j) * columns + b, me)
        )

    def home_line_got(p, j):
        here = home(b, line(j), p)
        return remote(here, here, e_send.at[p, j], e_recv.at[p, line(j)], (line(j) * columns + b, me))

    def home_column(p, i, j):
        here = home(b, line(i), p)
        source = here if i else home_ref.at[pl.ds(p * height, height), :]
        return remote(source, here, f_send.at[p, i, j], f_recv.at[p, line(i), b], (a * columns + column(j), me))

    def home_column_got(p, i, j):
        here = home(column(j), line(i), p)
        return remote(here, here, f_send.at[p, i, j], f_recv.at[p, line(i), column(j)], (a * columns + column(j), me))

    def home_pass(p):
        for i in range(1, lines):
            home_line_got(p, i).wait_recv()
            for j in range(1, columns):
                home_column(p, i, j).start()

    def rate_copy(j):
        device = lax.rem(me + j, size)
        return remote(rate_parts.at[device], rate_land.at[me], m_send.at[j - 1], m_recv.at[me], (dp, device))

    for c in range(len(chunks)):
        for j in range(1, columns):
            to_column(c, j).start()
    for p in range(pieces):
        for j in range(1, lines):
            home_line(p, j).start()
        for j in range(1, columns):
            home_column(p, 0, j).start()
    stay = [
        pltpu.make_async_copy(source, target, local_sem.at[i])
        for i, (source, target) in enumerate(
            ((home_ref, home_out.at[dp]), (hidden_ref.at[me], hidden_out.at[me]), (back_ref.at[me], back_out.at[me]))
        )
    ]
    for copy in stay:
        copy.start()
    for d in range(size):
        rate_parts[d, 0:1, :] = rate_attn_ref[:, d * narrow : (d + 1) * narrow]
        rate_parts[d, 1:2, :] = rate_mlp_ref[:, d * narrow : (d + 1) * narrow]
    for j in range(1, size):
        rate_copy(j).start()

    def deal(j):
        device = lax.rem(me + j, size)
        return [
            remote(source.at[device], target.at[me], send.at[j - 1], receive.at[me], (dp, device))
            for source, target, send, receive in ((hidden_ref, hidden_out, h_send, h_recv), (back_ref, back_out, g_send, g_recv))
        ]

    def dealt(j):
        device = lax.rem(me + j, size)
        return [
            remote(target.at[device], target.at[device], send.at[j - 1], receive.at[device], (dp, device))
            for target, send, receive in ((hidden_out, h_send, h_recv), (back_out, g_send, g_recv))
        ]

    for j in range(1, size):
        for copy in deal(j):
            copy.start()

    rates = rate_parts[me]
    for j in range(1, size):
        source = lax.rem(me + j, size)
        remote(rate_land.at[source], rate_land.at[source], m_send.at[j - 1], m_recv.at[source], (dp, source)).wait_recv()
        rates = rates + rate_land[source]
    pack[...] = jnp.zeros_like(pack)
    pack[0:1, :narrow] = gain_ref[...]
    pack[1:3, :] = scale_ref[...]
    pack[3:5, :narrow] = rates[0:2, :]

    def small_copy(j):
        return remote(pack, small_land.at[dp], s_send.at[j - 1], s_recv.at[dp], (peer(j), me))

    def small_give(j, carry):
        small_copy(j).start()
        return carry

    lax.fori_loop(1, devices, small_give, 0)

    def settle_column(c):
        ref, _, q = chunks[c]
        for j in range(1, columns):
            from_column(c, j).wait_recv()

        def add(i, carry):
            here = pl.ds(pl.multiple_of(i * rows, rows), rows)
            own = pl.ds(pl.multiple_of((q * columns + b) * span + i * rows, rows), rows)
            total = ref[own, :].astype(f32)
            for j in range(1, columns):
                total = total + y_land[c, column(j), here, :].astype(f32)
            y_sum[c, here, :] = total.astype(bf16)
            return carry

        lax.fori_loop(0, lines, add, 0)
        for j in range(1, lines):
            to_line(c, j).start()

    def settle_line(c):
        for j in range(1, lines):
            from_line(c, j).wait_recv()
        total = y_sum[c, pl.ds(pl.multiple_of(a * rows, rows), rows), :].astype(f32)
        for j in range(1, lines):
            total = total + z_land[c, line(j)].astype(f32)
        sum_of(c, b, a)[...] = total.astype(bf16)
        for j in range(1, lines):
            back_line(c, j).start()
        for j in range(1, columns):
            back_column(c, 0, j).start()

    def pass_on(c):
        for i in range(1, lines):
            back_line_got(c, i).wait_recv()
            for j in range(1, columns):
                back_column(c, i, j).start()

    count = len(chunks)
    for c in range(count):
        settle_column(c)
    for p in range(pieces - 1):
        home_pass(p)
    for step in range(count + 2):
        if 1 <= step <= count:
            settle_line(step - 1)
        if step == 1:
            home_pass(pieces - 1)
        if step >= 2:
            pass_on(step - 2)

    def small_take(j, total):
        source = peer(j)
        remote(small_land.at[source], small_land.at[source], s_send.at[j - 1], s_recv.at[source], (source, me)).wait_recv()
        return total + small_land[source]

    small_out[...] = lax.fori_loop(1, devices, small_take, pack[...])
    for c in range(count):
        for i in range(lines):
            for j in range(1, columns):
                back_column_got(c, i, j).wait_recv()
                back_column(c, i, j).wait_send()
        for j in range(1, lines):
            back_line(c, j).wait_send()
            to_line(c, j).wait_send()
        for j in range(1, columns):
            to_column(c, j).wait_send()
    for p in range(pieces):
        for i in range(lines):
            for j in range(1, columns):
                home_column_got(p, i, j).wait_recv()
                home_column(p, i, j).wait_send()
        for j in range(1, lines):
            home_line(p, j).wait_send()

    def finish(j, carry):
        small_copy(j).wait_send()
        return carry

    lax.fori_loop(1, devices, finish, 0)
    for j in range(1, size):
        rate_copy(j).wait_send()
        for copy in dealt(j):
            copy.wait_recv()
        for copy in deal(j):
            copy.wait_send()
    for copy in stay:
        copy.wait()


def tail_sum(late, home, rate_attn, rate_mlp, gain, scales, hidden, back, devices, size, collective_id):
    lines, columns, cuts, rows = tail_plan(devices, late.shape[0])
    narrow = D // size
    small = jax.ShapeDtypeStruct((8, scales.shape[1]), f32)
    chunks = cuts
    pieces = next(p for p in (4, 3, 1) if home.shape[0] % (16 * p) == 0)
    dma = pltpu.SemaphoreType.DMA
    total = jax.ShapeDtypeStruct((late.shape[0] // rows, rows, D), bf16)
    homes = jax.ShapeDtypeStruct((devices, *home.shape), bf16)
    return pl.pallas_call(
        functools.partial(tail_sum_kernel, devices, size),
        out_shape=[total, homes] + [jax.ShapeDtypeStruct(x.shape, x.dtype) for x in (small, hidden, back)],
        in_specs=[VMEM_WHOLE] * 8,
        out_specs=[VMEM_WHOLE, ANYWHERE, VMEM_WHOLE, ANYWHERE, ANYWHERE],
        scratch_shapes=[
            pltpu.VMEM((chunks, columns, lines * rows, D), bf16),
            pltpu.VMEM((chunks, lines * rows, D), bf16),
            pltpu.VMEM((chunks, lines, rows, D), bf16),
            pltpu.VMEM((size, 8, narrow), f32),
            pltpu.VMEM((size, 8, narrow), f32),
            pltpu.VMEM(small.shape, f32),
            pltpu.VMEM((devices, *small.shape), f32),
            dma((chunks, columns)), dma((chunks, columns)),
            dma((chunks, lines)), dma((chunks, lines)),
            dma((chunks, lines)), dma((chunks, lines)),
            dma((chunks, lines, columns)), dma((chunks, lines, columns)),
            dma((size - 1,)), dma((size,)),
            dma((devices - 1,)), dma((devices,)),
            dma((size - 1,)), dma((size,)),
            dma((size - 1,)), dma((size,)),
            dma((pieces, lines)), dma((pieces, lines)),
            dma((pieces, lines, columns)), dma((pieces, lines, columns)),
            dma((3,)),
        ],
        compiler_params=remote_params(collective_id),
        cost_estimate=pl.CostEstimate(flops=0, bytes_accessed=late.shape[0] * D * 16, transcendentals=0),
        name="tail_sum",
    )(late, home, rate_attn, rate_mlp, gain, scales, hidden, back)


def optimizer_kernel(counts, group, index_ref, *refs):
    grads, (m_ref, f_ref, s_ref, mo_ref, fo_ref, so_ref, go_ref) = refs[: 2 * group], refs[2 * group :]
    for j in range(group):
        slot = pl.program_id(0) * group + j
        block, live = index_ref[slot, 0], index_ref[slot, 1]

        @pl.when(live == 0)
        def _():
            for ref in (mo_ref, fo_ref, so_ref, go_ref):
                ref[j] = jnp.zeros_like(m_ref[j])

        @pl.when(live == 1)
        def _():
            gradient = jnp.where(block < counts[0], grads[2 * j][0].astype(f32), grads[2 * j + 1][0].astype(f32))
            stepped, first_new, second_new = adam_update(
                m_ref[j], gradient, f_ref[j], s_ref[j], WEIGHT_DECAY, LEARN_RATE
            )
            go_ref[j] = gradient
            fo_ref[j] = first_new
            so_ref[j] = second_new
            mo_ref[j] = stepped * lax.rsqrt(jnp.sum(stepped * stepped, axis=-1, keepdims=True) + EPSILON)


def optimizer(index, attn_grads, mlp_grads, masters, firsts, seconds):
    slots, height, _ = masters.shape
    group = math.gcd(slots, 4)
    grads = [g.reshape(-1, height, D) for g in (attn_grads, mlp_grads)]
    counts = tuple(g.shape[0] for g in grads)
    block = pl.BlockSpec((group, height, D), lambda i, ref: (i, 0, 0))

    def attn_block(j):
        return pl.BlockSpec(
            (1, height, D), lambda i, ref: (jnp.minimum(ref[i * group + j, 0], counts[0] - 1), 0, 0)
        )

    def mlp_block(j):
        return pl.BlockSpec(
            (1, height, D), lambda i, ref: (jnp.maximum(ref[i * group + j, 0] - counts[0], 0), 0, 0)
        )

    return pl.pallas_call(
        functools.partial(optimizer_kernel, counts, group),
        grid_spec=pltpu.PrefetchScalarGridSpec(
            num_scalar_prefetch=1,
            grid=(slots // group,),
            in_specs=[spec(j) for j in range(group) for spec in (attn_block, mlp_block)] + [block] * 3,
            out_specs=[block] * 4,
        ),
        out_shape=[jax.ShapeDtypeStruct(masters.shape, f32)] * 4,
        compiler_params=pltpu.CompilerParams(vmem_limit_bytes=GRANT),
        cost_estimate=pl.CostEstimate(flops=20 * masters.size, bytes_accessed=30 * masters.size, transcendentals=0),
        name="optimizer",
    )(index, *(grads * group), masters, firsts, seconds)


def collect_kernel(count, places_ref, slots_hbm, out_hbm, held, sems, out_sems):
    chunks = out_sems.shape[0]
    each = count // chunks

    def copy(b):
        return pltpu.make_async_copy(slots_hbm.at[places_ref[b]], held.at[b], sems.at[b])

    def start(b, carry):
        copy(b).start()
        return carry

    def wait(b, carry):
        copy(b).wait()
        return carry

    def out(c):
        here = pl.ds(c * each, each)
        return pltpu.make_async_copy(held.at[here], out_hbm.at[here], out_sems.at[c])

    lax.fori_loop(0, count, start, 0)
    for c in range(chunks):
        lax.fori_loop(c * each, (c + 1) * each, wait, 0)
        out(c).start()
    for c in range(chunks):
        out(c).wait()


def collect(places, slots):
    count, shape = places.shape[0], slots.shape[1:]
    return pl.pallas_call(
        functools.partial(collect_kernel, count),
        grid_spec=pltpu.PrefetchScalarGridSpec(
            num_scalar_prefetch=1,
            grid=(1,),
            in_specs=[pl.BlockSpec(memory_space=pl.ANY)],
            out_specs=pl.BlockSpec(memory_space=pl.ANY),
            scratch_shapes=[
                pltpu.VMEM((count, *shape), bf16),
                pltpu.SemaphoreType.DMA((count,)),
                pltpu.SemaphoreType.DMA((math.gcd(count, 8),)),
            ],
        ),
        out_shape=jax.ShapeDtypeStruct((count, *shape), bf16),
        compiler_params=pltpu.CompilerParams(vmem_limit_bytes=GRANT),
        cost_estimate=pl.CostEstimate(flops=0, bytes_accessed=4 * count * math.prod(shape), transcendentals=0),
        name="collect",
    )(places, slots)


def spread_plan(devices, slots):
    lines = min(4, devices)
    columns = devices // lines
    across = slots * 5 // 32 if columns == 2 else 0
    cuts = next(q for q in (9, 3, 2, 1) if (slots - across) % q == 0)
    return lines, columns, across, cuts


def spread_kernel(
    devices, size, slots, height, slots_ref, x_ref, cot_ref, gains_ref,
    all_ref, x_all, cot_all, gains_all, cos_ref, sin_ref, start_ref, inv_ref, gains_land, x_own_ref,
    z_send, z_recv, y_send, y_recv, e_send, e_recv, x_send, x_recv, c_send, c_recv, w_send, w_recv, local_sem
):
    lines, columns, across, cuts = spread_plan(devices, slots)
    dp, me = lax.axis_index("dp"), lax.axis_index("mp")
    a, b = dp // columns, lax.rem(dp, columns)
    chips = size // 2
    chip, core = me // 2, lax.rem(me, 2)
    partner = me + 1 - 2 * core
    tokens, narrow = x_ref.shape
    own = tokens // size
    x_steps = x_recv.shape[1]
    x_rows = tokens // x_steps
    cut_rows = (slots - across) * height // cuts
    has_left, has_right = a > 0, a < lines - 1

    def remote(source, target, send, receive, device):
        return pltpu.make_async_remote_copy(
            src_ref=source, dst_ref=target, send_sem=send, recv_sem=receive, device_id=device, device_id_type=MESH
        )

    def column(j):
        return lax.rem(b + j, columns)

    def other(k, which):
        return 2 * lax.rem(chip + k, chips) + which

    def mp_peer(j):
        return lax.rem(me + j, size)

    barrier = pltpu.get_barrier_semaphore()

    def greet(device):
        pl.semaphore_signal(barrier, inc=1, device_id=device, device_id_type=MESH)

    for j in range(1, columns):
        greet((a * columns + column(j), me))
    for j in range(1, size):
        greet((dp, mp_peer(j)))

    @pl.when(has_left)
    def _():
        greet((dp - columns, me))

    @pl.when(has_right)
    def _():
        greet((dp + columns, me))

    pl.semaphore_wait(
        barrier, columns - 1 + size - 1 + has_left.astype(jnp.int32) + has_right.astype(jnp.int32)
    )

    items = cuts + (columns if across else 0)

    def region(ref, line, c, row=None):
        if c < cuts:
            source, first, count = line * columns + b, across * height + c * cut_rows, cut_rows
        else:
            source, first, count = line * columns + (c - cuts), 0, across * height
        return ref.at[source, pl.ds(first, count), :]

    def own_part(c):
        first, count = (across * height + c * cut_rows, cut_rows) if c < cuts else (0, across * height)
        return slots_ref.at[pl.ds(first, count), :]

    def along(line, c, to_right, source=None):
        here = region(all_ref, line, c)
        side = 1 if to_right else 0
        device = (dp + columns if to_right else dp - columns, me)
        return remote(here if source is None else source, here, z_send.at[line, side, c], z_recv.at[line, c], device)

    def over(line, c, j, source=None):
        here = region(all_ref, line, c)
        return remote(
            here if source is None else source, here, y_send.at[line, j, c], y_recv.at[line, b, c],
            (a * columns + column(j), me),
        )

    def over_got(line, column_from, c):
        first = across * height + c * cut_rows
        here = all_ref.at[line * columns + column_from, pl.ds(first, cut_rows), :]
        return remote(here, here, y_send.at[line, 1, c], y_recv.at[line, column_from, c], (dp, partner))

    def early(j):
        here = all_ref.at[dp, pl.ds(0, across * height), :]
        return remote(own_part(cuts), here, e_send.at[j], e_recv.at[b], (a * columns + column(j), me))

    def early_got(column_from):
        here = all_ref.at[a * columns + column_from, pl.ds(0, across * height), :]
        return remote(here, here, e_send.at[1], e_recv.at[column_from], (dp, partner))

    def x_piece(ref, s):
        return ref.at[pl.ds(s * x_rows, x_rows), :]

    def x_own(s, k):
        device = (dp, partner) if k == 0 else (dp, other(k, core))
        return remote(x_piece(x_ref, s), x_piece(x_all.at[me], s), x_send.at[k, s], x_recv.at[me, s], device)

    def x_forward(s, k):
        source = other(k, core)
        here = x_piece(x_all.at[source], s)
        return remote(here, here, x_send.at[chips + k - 1, s], x_recv.at[source, s], (dp, partner))

    def x_got(s, source):
        here = x_piece(x_all.at[source], s)
        return remote(here, here, x_send.at[0, s], x_recv.at[source, s], (dp, partner))

    def cot_own(j):
        device = mp_peer(j)
        rows = pl.ds(pl.multiple_of(device * own, own), own)
        return remote(cot_ref.at[rows, :], cot_all.at[me], c_send.at[j - 1], c_recv.at[me], (dp, device))

    def cot_got(j):
        here = cot_all.at[mp_peer(j)]
        return remote(here, here, c_send.at[j - 1], c_recv.at[mp_peer(j)], (dp, partner))

    def gains_own(j):
        return remote(gains_ref, gains_land.at[me], w_send.at[j - 1], w_recv.at[me], (dp, mp_peer(j)))

    if across:
        for j in range(1, columns):
            early(j).start()
    for j in range(1, size):
        gains_own(j).start()
    gains_land[me] = gains_ref[...]
    for c in range(cuts):
        for side, there in ((False, has_left), (True, has_right)):

            @pl.when(there)
            def _():
                along(a, c, side, own_part(c)).start()

        for j in range(1, columns):
            over(a, c, j, own_part(c)).start()
    for s in range(x_steps):
        for k in range(chips):
            x_own(s, (k + 1) % chips).start()
    for j in range(1, size):
        cot_own(j).start()
    local = [
        pltpu.make_async_copy(slots_ref, all_ref.at[dp], local_sem.at[0]),
        pltpu.make_async_copy(x_ref, x_all.at[me], local_sem.at[1]),
        pltpu.make_async_copy(
            cot_ref.at[pl.ds(pl.multiple_of(me * own, own), own), :], cot_all.at[me], local_sem.at[2]
        ),
    ]
    for copy in local:
        copy.start()
    if across:
        for j in range(1, columns):
            early_got(column(j)).wait_recv()
        for c in range(cuts, items):
            for side, there in ((False, has_left), (True, has_right)):
                mine = b == c - cuts

                @pl.when(jnp.logical_and(there, mine))
                def _():
                    along(a, c, side, own_part(c)).start()

                @pl.when(jnp.logical_and(there, jnp.logical_not(mine)))
                def _():
                    along(a, c, side).start()

    for s in range(x_steps):
        for k in range(1, chips):
            x_got(s, other(k, core)).wait_recv()
            x_forward(s, k).start()

    rope_rows = min(256, tokens)

    def rope_table(i, carry):
        here = pl.ds(pl.multiple_of(i * rope_rows, rope_rows), rope_rows)
        lane = lax.broadcasted_iota(jnp.int32, (rope_rows, LANES), 1)
        position = (lax.broadcasted_iota(jnp.int32, (rope_rows, LANES), 0) + i * rope_rows).astype(f32)
        j = lane % (HD // 2)
        angle = position * jnp.exp(j.astype(f32) * (-2.0 * math.log(10000.0) / HD))
        cos_ref[here, :] = jnp.cos(angle)
        sin_ref[here, :] = jnp.where(lane % HD < HD // 2, -1.0, 1.0) * jnp.sin(angle)
        return carry

    lax.fori_loop(0, tokens // rope_rows, rope_table, 0)

    for hop in range(1, lines):
        for c in range(items):
            for to_right in (True, False):
                line = a - hop if to_right else a + hop
                there = line >= 0 if to_right else line < lines
                onward = has_right if to_right else has_left

                @pl.when(there)
                def _():
                    along(line, c, to_right).wait_recv()

                    @pl.when(onward)
                    def _():
                        along(line, c, to_right).start()

                    if c < cuts:
                        for j in range(1, columns):
                            over(line, c, j).start()

    for s in range(x_steps):
        x_got(s, partner).wait_recv()
        for k in range(1, chips):
            x_got(s, other(k, 1 - core)).wait_recv()
    local[1].wait()
    mine = pltpu.make_async_copy(
        x_all.at[:, pl.ds(pl.multiple_of(me * own, own), own), :], x_own_ref, local_sem.at[1]
    )
    mine.start()
    mine.wait()
    start_rows = min(128, own)

    def start_part(i, carry):
        here = pl.ds(pl.multiple_of(i * start_rows, start_rows), start_rows)
        x = jnp.concatenate([x_own_ref[d, here, :] for d in range(size)], axis=1).astype(f32)
        unit_rows, inverse = normalize(x)
        start_ref[here, :] = unit_rows
        inv_ref[here, :] = jnp.broadcast_to(inverse, (start_rows, LANES))
        return carry

    lax.fori_loop(0, own // start_rows, start_part, 0)

    for line in range(lines):
        for c in range(cuts):
            for j in range(1, columns):
                over_got(line, column(j), c).wait_recv()
    for j in range(1, size):
        cot_got(j).wait_recv()
        here = gains_land.at[mp_peer(j)]
        remote(here, here, w_send.at[j - 1], w_recv.at[mp_peer(j)], (dp, partner)).wait_recv()
        gains_own(j).wait_send()
    for d in range(size):
        gains_all[:, d * narrow : (d + 1) * narrow] = gains_land[d]
    local[0].wait()
    local[2].wait()
    if across:
        for j in range(1, columns):
            early(j).wait_send()
    for s in range(x_steps):
        for k in range(chips):
            x_own(s, k).wait_send()
        for k in range(1, chips):
            x_forward(s, k).wait_send()
    for j in range(1, size):
        cot_own(j).wait_send()
    for line in range(lines):
        for c in range(items):
            @pl.when(jnp.logical_and(has_right, line <= a))
            def _():
                along(line, c, True).wait_send()

            @pl.when(jnp.logical_and(has_left, line >= a))
            def _():
                along(line, c, False).wait_send()

            if c < cuts:
                for j in range(1, columns):
                    over(line, c, j).wait_send()


def spread(slots_low, hidden_in, cotangent, gains, devices, size, collective_id):
    slots, height, _ = slots_low.shape
    tokens, narrow = hidden_in.shape
    lines, columns, across, cuts = spread_plan(devices, slots)
    items = cuts + (columns if across else 0)
    chips = size // 2
    x_steps = 4
    dma = pltpu.SemaphoreType.DMA
    return pl.pallas_call(
        functools.partial(spread_kernel, devices, size, slots, height),
        out_shape=[
            jax.ShapeDtypeStruct((devices, slots * height, D), bf16),
            jax.ShapeDtypeStruct((size, tokens, narrow), bf16),
            jax.ShapeDtypeStruct((size, tokens // size, narrow), bf16),
            jax.ShapeDtypeStruct((gains.shape[0], D), f32),
            jax.ShapeDtypeStruct((tokens, LANES), f32),
            jax.ShapeDtypeStruct((tokens, LANES), f32),
            jax.ShapeDtypeStruct((tokens // size, D), f32),
            jax.ShapeDtypeStruct((tokens // size, LANES), f32),
        ],
        in_specs=[VMEM_WHOLE] * 4,
        out_specs=[ANYWHERE] * 3 + [VMEM_WHOLE] * 5,
        scratch_shapes=[
            pltpu.VMEM((size, *gains.shape), f32),
            pltpu.VMEM((size, tokens // size, narrow), bf16),
            dma((lines, 2, items)),
            dma((lines, items)),
            dma((lines, columns, cuts)),
            dma((lines, columns, cuts)),
            dma((columns,)),
            dma((columns,)),
            dma((2 * chips - 1, x_steps)),
            dma((size, x_steps)),
            dma((size - 1,)),
            dma((size,)),
            dma((size - 1,)),
            dma((size,)),
            dma((3,)),
        ],
        compiler_params=remote_params(collective_id),
        cost_estimate=pl.CostEstimate(flops=0, bytes_accessed=devices * slots * height * D * 4, transcendentals=0),
        name="spread",
    )(slots_low.reshape(slots * height, D), hidden_in, cotangent, gains)


def shards(
    n_dp,
    hidden_in,
    cotangent,
    owners,
    masters,
    firsts,
    seconds,
    width_gains,
    width_first,
    width_second,
    hidden_gains,
    hidden_first,
    hidden_second,
):
    tokens = hidden_in.shape[0]
    narrow = hidden_in.shape[1]
    slot_count = masters.shape[1]
    block_rows = masters.shape[2]
    blocks = owners.shape[0]
    hidden_local = hidden_gains.shape[1]
    dp_index = lax.axis_index("dp")
    mp_index = lax.axis_index("mp")
    own_tokens = tokens // (D // narrow)

    block_order = jnp.arange(blocks)
    same_owner = owners[:, None] == owners[None, :]
    slot_rank = jnp.sum(
        jnp.logical_and(same_owner, block_order[None, :] < block_order[:, None]).astype(jnp.int32),
        axis=1,
    )
    owned_mask = owners == dp_index
    in_use = jnp.arange(slot_count) < jnp.sum(owned_mask.astype(jnp.int32))
    slot_block = jnp.sum(
        jnp.where(
            jnp.logical_and(owned_mask[None, :], slot_rank[None, :] == jnp.arange(slot_count)[:, None]),
            block_order[None, :],
            0,
        ),
        axis=1,
    )

    size = D // narrow
    all_slots, x_all, cot_all, gains, cosine, sine, start_unit, start_inv = spread(
        masters[0].astype(bf16), hidden_in, cotangent, width_gains, n_dp, size, 6
    )
    weights = collect(
        owners * slot_count + slot_rank, all_slots.reshape(n_dp * slot_count, block_rows, D)
    ).reshape(blocks * block_rows, D)
    operand, queries, keys, values, q_turned, k_turned = project(x_all, weights, width_gains, cosine, sine)
    attended, mixed = attend(queries, keys, values)

    attn_branch, middle, middle_low = attention_sum(
        attended, weights, start_unit, gains, 3 * narrow, size, STEPS, 1
    )
    out_rows, middle_rows, up_raw, gate_raw, d_mlp, d_middle, g_rate_mlp = mlp(
        middle_low, weights, hidden_gains, middle, cot_all, gains, size, STEPS, 2
    )
    d_attn, d_start, g_rate_attn, g_scales, g_mlp = mlp_back(
        d_mlp, weights, hidden_gains, up_raw, gate_raw, middle_rows, d_middle, start_unit, attn_branch, gains,
        size, MLP_STEPS, 3,
    )
    d_attn, g_mlp = lax.optimization_barrier((d_attn, g_mlp))
    mlp_home = lax.psum_scatter(g_mlp, "dp", scatter_dimension=0, tiled=True)
    d_attended, attn_grad_rows = gather_project(d_attn, weights, narrow, 3 * narrow, size, STEPS, 4, "attention_gather")
    d_queries, d_keys, d_values = attend_back(queries, keys, values, mixed, d_attended)
    grads_qkv, g_qk = project_back(
        d_queries, d_keys, d_values, q_turned, k_turned, width_gains, cosine, sine
    )
    grad_pieces, g_attn = start_sum(
        grads_qkv, weights, d_start, start_unit, start_inv, operand, attended, attn_grad_rows, size, STEPS, 5
    )
    attn_grads, mlp_grads, small, hidden_out, grad_in = tail_sum(g_attn, mlp_home, g_rate_attn, g_rate_mlp, g_qk, g_scales, out_rows, grad_pieces, n_dp, size, 7)
    hidden_out = hidden_out.reshape(tokens, narrow)
    grad_in = grad_in.reshape(tokens, narrow).astype(f32)
    width_total = jnp.concatenate([small[0:1, :narrow], small[3:5, :narrow]], axis=0)
    hidden_total = small[1:3, :]
    index = jnp.stack([slot_block, in_use.astype(jnp.int32)], axis=1)
    masters_new, firsts_new, seconds_new, weight_grads = [
        part[None]
        for part in optimizer(index, attn_grads, mlp_grads, masters[0], firsts[0], seconds[0])
    ]
    width_new, width_first_new, width_second_new = adam_update(
        width_gains, width_total, width_first, width_second, 0.0, GAIN_RATE
    )
    hidden_new, hidden_first_new, hidden_second_new = adam_update(
        hidden_gains, hidden_total, hidden_first, hidden_second, 0.0, GAIN_RATE
    )
    return (
        hidden_out,
        grad_in,
        masters_new,
        firsts_new,
        seconds_new,
        weight_grads,
        width_new,
        width_total,
        width_first_new,
        width_second_new,
        hidden_new,
        hidden_total,
        hidden_first_new,
        hidden_second_new,
    )


def solution(mesh):
    in_specs = (
        P("dp", "mp"),
        P("dp", "mp"),
        P(),
        P("mp", "dp", None, None),
        P("mp", "dp", None, None),
        P("mp", "dp", None, None),
        P(None, "mp"),
        P(None, "mp"),
        P(None, "mp"),
        P(None, "mp"),
        P(None, "mp"),
        P(None, "mp"),
    )
    out_specs = (
        P("dp", "mp"),
        P("dp", "mp"),
        P("mp", "dp", None, None),
        P("mp", "dp", None, None),
        P("mp", "dp", None, None),
        P("mp", "dp", None, None),
        P(None, "mp"),
        P(None, "mp"),
        P(None, "mp"),
        P(None, "mp"),
        P(None, "mp"),
        P(None, "mp"),
        P(None, "mp"),
        P(None, "mp"),
    )
    return jax.shard_map(functools.partial(shards, mesh.shape["dp"]), mesh=mesh, in_specs=in_specs, out_specs=out_specs, check_vma=False)
```
